32 devices in a mesh: comp: 2 (over core), tile: 16 (over z, y, x).
Axes of the slice: x: 2, y: 2, z: 4, core: 2. Of those that a mesh axis runs over, the one named last changes fastest.
Arguments:
- state: float32 [2, 8, 256, 1024], P('comp', None, 'tile'), may hold values from -80 to 80, as said below
- basis: bfloat16 [12, 2, 8, 256, 1024], P(None, 'comp', None, 'tile'), may hold values from -4 to 4
- kappa: float32 [2, 256, 1024], P('comp', 'tile'), may hold values from 0.05 to 0.22
- vmix: float32 [2, 8, 8], P('comp'), may hold values from -1 to 1
- land_mask: int32 [256, 1024], P('tile'), may hold values 0 or 1
- send_rows: int32 [2, 16, 16, 8], P('comp', 'tile'), may hold values from 0 to 127
- recv_slots: int32 [2, 16, 128, 4], P('comp', 'tile'), may hold values from 0 to 127
- recv_weights: float32 [2, 16, 128, 4], P('comp', 'tile'), may hold values from 0.1 to 0.4
Outputs:
- direction: float32 [2, 8, 256, 1024], P('comp', None, 'tile')
- coefs: float32 [12], replicated
The draws below stay inside these ranges and needn't reach their ends.
Inputs may be any that keep to these rules, and one draw needn't show every extreme that they name: `state`: the perturbation is noise plus a combination of the basis vectors.
All inputs are finite; a program needn't handle non-finite values. No bound on the sum of `land_mask` on one device may be relied on, other than what follows from the above.
Results may differ from the reference program's by a relative error of at most 0.0003.
Values sent between devices are 32-bit elements; how exact they have to be, the bound alone decides.
No kernel may reach another device: no remote copies, remote signals or barrier semaphores. Data moves between devices by JAX's collectives and lax.ppermute only.
A program may use at most 64 MiB of HBM per device.

```python
import jax
import jax.numpy as jnp
from jax import lax

LEV = 8
COLS = 1024
FLUX = 4
OVER = 4
CAP = 8
VECS = 12
TILES = 16
ROWS = 256
NB = 128


def basis_field(key):
    inner = jax.random.fold_in(key, 7)
    return jnp.clip(jax.random.normal(inner, (VECS, 2, LEV, ROWS, COLS), jnp.float32), -4.0, 4.0)


def draw_basis(key, part):
    return basis_field(key).astype(jnp.bfloat16)


def draw_state(key, part):
    qvals = basis_field(key).astype(jnp.bfloat16).astype(jnp.float32)
    amps = jax.random.uniform(jax.random.fold_in(key, 11), (VECS,), jnp.float32, -1.5, 1.5)
    noise = jnp.clip(jax.random.normal(jax.random.fold_in(key, 13), (2, LEV, ROWS, COLS), jnp.float32), -4.0, 4.0)
    mixed = 0.5 * noise
    for index in range(VECS):
        mixed = mixed + amps[index] * qvals[index]
    return mixed


def plant(array, own_key, low, largest):
    dims = array.shape
    spot = [jax.random.randint(jax.random.fold_in(own_key, axis), (), 0, dims[axis]) for axis in range(len(dims))]
    array = array.at[tuple(spot)].set(low)
    longest = dims.index(max(dims))
    spot[longest] = (spot[longest] + 1) % dims[longest]
    return array.at[tuple(spot)].set(largest)


def shard_levels(rng, shape, shards, least, top_value):
    loudness, own = 1.0, jax.random.fold_in(rng, 6)
    for dim, blocks in shards:
        draws = jnp.exp(jax.random.uniform(jax.random.fold_in(own, dim), (blocks,), jnp.float32, least / len(shards), top_value / len(shards)))
        loudness = loudness * jnp.repeat(draws, shape[dim] // blocks).reshape([-1 if axis == dim else 1 for axis in range(len(shape))])
    return loudness


def bell_draw(rng, shape, deviation, reach, cuts=(), kind=jnp.bfloat16):
    result = deviation * jax.random.normal(rng, shape, jnp.float32)
    if cuts:
        result = result * shard_levels(rng, shape, cuts, -0.22, 0.18)
    return jnp.clip(result, -reach, reach).astype(kind)


def setup_inputs(seed: int = 0) -> dict:
    key_list = jax.random.split(jax.random.key(seed), 9)
    state = draw_state(jax.random.fold_in(key_list[8], 71), 0)
    basis = draw_basis(jax.random.fold_in(key_list[8], 71), 0)
    kappa = jnp.clip(0.05 + 0.17 * jax.random.uniform(key_list[2], (2, ROWS, COLS), jnp.float32) ** shard_levels(key_list[2], (2, ROWS, COLS), ((0, 2), (1, 16)), -0.2, 0.2), 0.05, 0.22)
    vmix = bell_draw(key_list[3], (2, LEV, LEV), (4 * LEV) ** -0.5, 1.0, ((0, 2),), jnp.float32)
    land_mask = plant((jax.random.randint(key_list[4], (ROWS, COLS), 0, 4) < 3).astype(jnp.int32), jax.random.fold_in(key_list[4], 1), 0, 1)
    send_rows = plant(jax.random.randint(key_list[5], (2, TILES, TILES, CAP), 0, NB), jax.random.fold_in(key_list[5], 1), 0, NB - 1).astype(jnp.int32)
    recv_slots = plant(jax.random.randint(key_list[6], (2, TILES, NB, OVER), 0, TILES * CAP), jax.random.fold_in(key_list[6], 1), 0, (TILES * CAP) - 1).astype(jnp.int32)
    recv_weights = jnp.clip(0.1 + 0.3 * jax.random.uniform(key_list[7], (2, TILES, NB, OVER), jnp.float32) ** shard_levels(key_list[7], (2, TILES, NB, OVER), ((0, 2), (1, 16)), -0.2, 0.2), 0.1, 0.4)
    return {"state": state, "basis": basis, "kappa": kappa, "vmix": vmix, "land_mask": land_mask, "send_rows": send_rows, "recv_slots": recv_slots, "recv_weights": recv_weights}


def advance(x, kap, vert_mat, maskf, forced):
    padded = jnp.pad(x, ((0, 0), (0, 0), (1, 1), (0, 0)))
    lap = padded[:, :, 2:] + padded[:, :, :-2] + jnp.roll(x, 1, -1) + jnp.roll(x, -1, -1) - 4.0 * x
    vert = jnp.einsum('clm,cmrq->clrq', vert_mat, x, precision=lax.Precision.HIGHEST)
    return maskf[:, None] * (x + kap[:, None] * lap + vert + forced)

def reference(state, basis, kappa, vmix, land_mask, send_rows, recv_slots, recv_weights):
    surface = state[:, :FLUX].reshape(2, FLUX, TILES, NB, 128)
    band_ids = jnp.arange(TILES, dtype=jnp.int32)
    imports = []
    for recv in range(2):
        send = 1 - recv
        src = surface[send]

        def one(dest):
            rows_idx = send_rows[send][:, dest, :]
            buf = src[:, band_ids[:, None], rows_idx]
            flat = buf.reshape(FLUX, TILES * CAP, 128)
            picked = flat[:, recv_slots[recv, dest]]
            return jnp.einsum('ek,fekq->feq', recv_weights[recv, dest], picked, precision=lax.Precision.HIGHEST)
        per_band = lax.map(one, band_ids)
        imports.append(jnp.transpose(per_band, (1, 0, 2, 3)).reshape(FLUX, ROWS, COLS))
    imports = jnp.stack(imports)
    forced = jnp.concatenate([imports, jnp.zeros((2, LEV - FLUX, ROWS, COLS), jnp.float32)], 1)
    maskf = jnp.stack([land_mask.astype(jnp.float32), jnp.ones((ROWS, COLS), jnp.float32)])
    x = state
    for step in range(2):
        x = advance(x, kappa, vmix, maskf, forced)
    total = 2 * LEV * ROWS * COLS
    vflat = x.reshape(-1)
    qmat = basis.reshape(VECS, -1).astype(jnp.float32)
    coefs = jnp.dot(qmat, vflat, precision=lax.Precision.HIGHEST) / total
    remain = vflat - jnp.dot(coefs, qmat, precision=lax.Precision.HIGHEST)
    normsq = jnp.sum(remain * remain)
    direction = remain / jnp.sqrt(normsq / total + 1e-06)
    return (direction.reshape(2, LEV, ROWS, COLS), coefs)
```

```python
import functools

import jax
import jax.numpy as jnp
from jax import lax
from jax.experimental import pallas as pl
from jax.experimental.pallas import tpu as pltpu
from jax.sharding import PartitionSpec as P

FLUX = 4
LANES = 128
VMEM = pl.BlockSpec(memory_space=pltpu.VMEM)
SMEM = pl.BlockSpec(memory_space=pltpu.SMEM)
LIMIT = 24 << 20


def call(kernel, outs, in_specs, out_specs, scratch=(), cost=None):
    return pl.pallas_call(
        kernel,
        out_shape=outs,
        in_specs=in_specs,
        out_specs=out_specs,
        scratch_shapes=list(scratch),
        cost_estimate=cost,
        compiler_params=pltpu.CompilerParams(vmem_limit_bytes=LIMIT),
    )


def split(a):
    high = a.astype(jnp.bfloat16)
    return high, (a - high.astype(jnp.float32)).astype(jnp.bfloat16)


def gather_kernel(rows, rows_ref, state_ref, out_ref, x_ref, sems):
    cap, bands = rows_ref.shape
    per = x_ref.shape[0]
    top = FLUX * rows
    copies = []
    for part, (lo, hi) in enumerate(((0, top), (top, x_ref.shape[1]))):
        for c in range(per):
            copy = pltpu.make_async_copy(
                state_ref.at[lo:hi, c * LANES : (c + 1) * LANES],
                x_ref.at[c, lo:hi, :],
                sems.at[part * per + c],
            )
            copy.start()
            copies.append(copy)
    for copy in copies[:per]:
        copy.wait()

    def band(d, carry):
        for j in range(cap):
            b = rows_ref[j, d]
            r = lax.div(b, per)
            piece = x_ref[lax.rem(b, per), pl.ds(r, FLUX, stride=rows), :]
            out_ref[pl.ds(d * (cap * FLUX) + j, FLUX, stride=cap), :] = piece
        return carry

    lax.fori_loop(0, bands, band, 0)
    for copy in copies[per:]:
        copy.wait()


def early_kernel(slots_ref, weights_ref, basis_ref, matrix_ref, gram_ref):
    over, blocks = slots_ref.shape
    slots = matrix_ref.shape[2]
    row = lax.broadcasted_iota(jnp.int32, (slots, blocks), 0)
    mat = jnp.zeros((slots, blocks), jnp.float32)
    for k in range(over):
        mat = mat + jnp.where(slots_ref[k : k + 1, :] == row, weights_ref[k : k + 1, :], 0.0)
    high, low = split(mat.T)
    matrix_ref[0] = high
    matrix_ref[1] = low

    vecs, levels, rows, cols = basis_ref.shape
    n = vecs * rows
    total = jnp.zeros((n, n), jnp.float32)
    for l in range(levels):
        a = basis_ref[:, l].reshape(n, cols)
        total = total + lax.dot_general(
            a, a, (((1,), (1,)), ((), ())), preferred_element_type=jnp.float32
        )
    i0 = lax.broadcasted_iota(jnp.int32, (n, n), 0)
    i1 = lax.broadcasted_iota(jnp.int32, (n, n), 1)
    total = jnp.where(lax.rem(i0, rows) == lax.rem(i1, rows), total, 0.0)
    part = jnp.sum(total.reshape(vecs, rows, n), axis=1)
    j0 = lax.broadcasted_iota(jnp.int32, (n, LANES), 0)
    j1 = lax.broadcasted_iota(jnp.int32, (n, LANES), 1)
    fold = jnp.where(lax.div(j0, rows) == j1, 1.0, 0.0)
    gram = jnp.dot(part, fold, precision=lax.Precision.HIGHEST)
    packed = [jnp.zeros((1, LANES), jnp.float32), jnp.zeros((1, LANES), jnp.float32)]
    for i in range(vecs):
        shift = 16 * (i % 8)
        line = gram[i : i + 1, :]
        packed[i // 8] = packed[i // 8] + (pltpu.roll(line, shift, 1) if shift else line)
    gram_ref[...] = jnp.concatenate(packed, axis=0)


def shifted(parts, up):
    n = len(parts)
    lane = lax.broadcasted_iota(jnp.int32, parts[0].shape, 1)
    rolled = [pltpu.roll(p, 1 if up else LANES - 1, 1) for p in parts]
    edge = 0 if up else LANES - 1
    step = -1 if up else 1
    return [jnp.where(lane == edge, rolled[(c + step) % n], rolled[c]) for c in range(n)]


def regrid_kernel(
    rows, buf_ref, matrix_ref, x_ref, kappa_ref, mask_ref, vmix_ref, f_ref, p1_ref, p2_ref
):
    slots = matrix_ref.shape[2]
    per = x_ref.shape[0]
    levels = x_ref.shape[1] // rows
    cap = buf_ref.shape[1] // FLUX
    wide = jnp.concatenate(
        [buf_ref[:, f * cap : (f + 1) * cap, :].reshape(slots, LANES) for f in range(FLUX)], axis=1
    )
    bh, bl = split(wide)
    wh, wl = matrix_ref[0], matrix_ref[1]
    dot = functools.partial(jnp.dot, preferred_element_type=jnp.float32)
    out = dot(wh, bh) + (dot(wh, bl) + dot(wl, bh))
    for f in range(FLUX):
        for c in range(per):
            f_ref[c, f * rows : (f + 1) * rows, :] = out[
                c * rows : (c + 1) * rows, f * LANES : (f + 1) * LANES
            ]
    ocean = lax.axis_index("comp") == 0
    even = lax.rem(lax.axis_index("tile"), 2) == 0
    vmix = vmix_ref[...]
    pays = []
    for edge, inner in ((0, 1), (rows - 1, rows - 2)):
        xs = [x_ref[c, pl.ds(edge, levels, stride=rows), :] for c in range(per)]
        left, right = shifted(xs, True), shifted(xs, False)
        pay = []
        for c in range(per):
            s = slice(c * LANES, (c + 1) * LANES)
            x = xs[c]
            xi = x_ref[c, pl.ds(inner, levels, stride=rows), :]
            fe = f_ref[c, pl.ds(edge, FLUX, stride=rows), :]
            k = kappa_ref[edge : edge + 1, s]
            m = jnp.where(ocean, mask_ref[edge : edge + 1, s].astype(jnp.float32), 1.0)
            acc = x + k * (xi + left[c] + right[c] - 4.0 * x)
            for q in range(levels):
                acc = acc + vmix[:, q : q + 1] * x[q : q + 1, :]
            acc = acc + jnp.concatenate([fe, jnp.zeros((levels - FLUX, LANES), jnp.float32)], axis=0)
            pay.append((m * acc, x, m * k))
        pays.append(pay)
    for ref, flag in ((p1_ref, even), (p2_ref, jnp.logical_not(even))):
        for c in range(per):
            a, x, b = [jnp.where(flag, v, u) for u, v in zip(pays[0][c], pays[1][c])]
            ref[c * levels : (c + 1) * levels, :] = a
            ref[(per + c) * levels : (per + c + 1) * levels, :] = x
            ref[2 * per * levels + c : 2 * per * levels + c + 1, :] = b


def step_kernel(
    rows, x0_ref, f_ref, h1_ref, h2_ref, kappa_ref, mask_ref, vmix_ref, basis_ref, gram_ref,
    x_ref, sums_ref, x1_ref, halo_ref,
):
    per = x0_ref.shape[0]
    levels = x0_ref.shape[1] // rows
    vecs = basis_ref.shape[0]
    ocean = lax.axis_index("comp") == 0
    even = lax.rem(lax.axis_index("tile"), 2) == 0
    for side in range(2):
        flag = even if side == 1 else jnp.logical_not(even)

        def take(lo, n):
            return jnp.where(flag, h1_ref[lo : lo + n, :], h2_ref[lo : lo + n, :])

        for c in range(per):
            edge = x0_ref[c, pl.ds(side * (rows - 1), levels, stride=rows), :]
            a = take(c * levels, levels)
            b = take(2 * per * levels + c, 1)
            halo_ref[side, c] = take((per + c) * levels, levels)
            halo_ref[2 + side, c] = a + b * edge
    row = lax.broadcasted_iota(jnp.int32, (rows, LANES), 0)

    def advance(src, dst, base):
        for l in range(levels):
            part = slice(l * rows, (l + 1) * rows)
            xs = [src[c, part, :] for c in range(per)]
            left, right = shifted(xs, True), shifted(xs, False)
            for c in range(per):
                s = slice(c * LANES, (c + 1) * LANES)
                x = xs[c]
                prev = halo_ref[base, c, l : l + 1, :]
                nxt = halo_ref[base + 1, c, l : l + 1, :]
                up = jnp.where(row == 0, prev, pltpu.roll(x, 1, 0))
                down = jnp.where(row == rows - 1, nxt, pltpu.roll(x, rows - 1, 0))
                acc = x + kappa_ref[:, s] * (up + down + left[c] + right[c] - 4.0 * x)
                for q in range(levels):
                    acc = acc + vmix_ref[l, q] * src[c, q * rows : (q + 1) * rows, :]
                if l < FLUX:
                    acc = acc + f_ref[c, part, :]
                mask = jnp.where(ocean, mask_ref[:, s].astype(jnp.float32), 1.0)
                dst[c, part, :] = mask * acc

    advance(x0_ref, x1_ref, 0)
    advance(x1_ref, x_ref, 2)

    def level(l, accs):
        accs = list(accs)
        for c in range(per):
            s = slice(c * LANES, (c + 1) * LANES)
            x = x_ref[c, pl.ds(l * rows, rows), :]
            for i in range(vecs):
                t = x * basis_ref[i, l, :, s].astype(jnp.float32)
                accs[i] = accs[i] + t.reshape(rows // 8, 8, LANES).sum(0)
            accs[vecs] = accs[vecs] + (x * x).reshape(rows // 8, 8, LANES).sum(0)
        return tuple(accs)

    zero = jnp.zeros((8, LANES), jnp.float32)
    accs = lax.fori_loop(0, levels, level, (zero,) * (vecs + 1))
    lane = lax.broadcasted_iota(jnp.int32, (1, LANES), 1)
    line = jnp.zeros((1, LANES), jnp.float32)
    for i in range(vecs + 1):
        tot = jnp.sum(jnp.sum(accs[i], axis=0, keepdims=True), axis=1, keepdims=True)
        line = line + jnp.where(lane == 64 + i, tot, 0.0)
    block = gram_ref[...] + jnp.concatenate([jnp.zeros((1, LANES), jnp.float32), line], axis=0)
    for d in range(sums_ref.shape[0]):
        sums_ref[d] = block


def finish_kernel(rows, total, x_ref, basis_ref, sums_ref, out_ref, coef_ref):
    per = x_ref.shape[0]
    levels = x_ref.shape[1] // rows
    vecs = basis_ref.shape[0]
    sums = jnp.sum(sums_ref[...], axis=0)
    lane = lax.broadcasted_iota(jnp.int32, (1, LANES), 1)
    tail = pltpu.roll(sums[1:2, :], 64, 1)
    coef = jnp.where(lane < vecs, tail, 0.0) / total
    coef_ref[...] = coef[:, :vecs]
    square = jnp.sum(jnp.where(lane == vecs, tail, 0.0), axis=1, keepdims=True)
    splat = [jnp.sum(jnp.where(lane == i, coef, 0.0), axis=1, keepdims=True) for i in range(vecs)]
    quad = jnp.zeros((1, LANES), jnp.float32)
    for i in range(vecs):
        shift = (LANES - 16 * (i % 8)) % LANES
        line = sums[i // 8 : i // 8 + 1, :]
        line = pltpu.roll(line, shift, 1) if shift else line
        quad = quad + splat[i] * jnp.where(lane < vecs, line, 0.0)
    extra = jnp.sum(coef * (quad - 2.0 * total * coef), axis=1, keepdims=True)
    scale = 1.0 / jnp.sqrt((square + extra) / total + 1e-06)
    wide = [jnp.broadcast_to(scale * s, (8, LANES)) for s in splat]
    scale = jnp.broadcast_to(scale, (8, LANES))

    def level(l, carry):
        for c in range(per):
            s = slice(c * LANES, (c + 1) * LANES)
            x = x_ref[c, pl.ds(l * rows, rows), :].reshape(rows // 8, 8, LANES) * scale
            for i in range(vecs):
                b = basis_ref[i, l, :, s].astype(jnp.float32).reshape(rows // 8, 8, LANES)
                x = x - wide[i] * b
            out_ref[pl.ds(l * rows, rows), s] = x.reshape(rows, LANES)
        return carry

    lax.fori_loop(0, levels, level, 0)


def body(state, basis, kappa, vmix, land_mask, send_rows, recv_slots, recv_weights):
    _, levels, rows, cols = state.shape
    vecs = basis.shape[0]
    bands, cap = send_rows.shape[2:]
    blocks, over = recv_slots.shape[2:]
    per = cols // LANES
    comps = lax.axis_size("comp")
    devices = comps * bands
    total = float(levels * rows * cols * devices)
    f32 = jnp.float32
    flat = state.reshape(levels * rows, cols)
    vectors = basis[:, 0]
    kap, vm = kappa[0], vmix[0]

    field = jax.ShapeDtypeStruct((per, levels * rows, LANES), f32)
    bucket, columns = call(
        functools.partial(gather_kernel, rows),
        (jax.ShapeDtypeStruct((bands * FLUX * cap, LANES), f32), field),
        [SMEM, pl.BlockSpec(memory_space=pl.ANY)],
        (VMEM, VMEM),
        scratch=(pltpu.SemaphoreType.DMA((2 * per,)),),
    )(send_rows[0, 0].T, flat)
    moved = lax.all_to_all(bucket.reshape(bands, FLUX * cap, LANES), "tile", 0, 0)

    def by_column(a):
        return a[0, 0].reshape(rows, per, over).transpose(2, 1, 0).reshape(over, blocks)

    matrix, gram = call(
        early_kernel,
        (
            jax.ShapeDtypeStruct((2, blocks, bands * cap), jnp.bfloat16),
            jax.ShapeDtypeStruct((2, LANES), f32),
        ),
        [VMEM] * 3,
        (VMEM, VMEM),
        cost=pl.CostEstimate(flops=10**9, bytes_accessed=4 << 20, transcendentals=0),
    )(by_column(recv_slots), by_column(recv_weights), vectors)

    arrived = lax.ppermute(moved, "comp", [(i, i ^ 1) for i in range(comps)])
    pay = jax.ShapeDtypeStruct((2 * levels * per + per, LANES), f32)
    imported, pay1, pay2 = call(
        functools.partial(regrid_kernel, rows),
        (jax.ShapeDtypeStruct((per, FLUX * rows, LANES), f32), pay, pay),
        [VMEM] * 6,
        (VMEM,) * 3,
    )(arrived, matrix, columns, kap, land_mask, vm)
    pairs1 = [(i, i ^ 1) for i in range(bands)]
    pairs2 = [p for i in range(1, bands - 1, 2) for p in ((i, i + 1), (i + 1, i))]
    got1 = lax.ppermute(pay1, "tile", pairs1)
    got2 = lax.ppermute(pay2, "tile", pairs2)
    x, sums = call(
        functools.partial(step_kernel, rows),
        (field, jax.ShapeDtypeStruct((devices, 2, LANES), f32)),
        [VMEM] * 6 + [SMEM] + [VMEM] * 2,
        (VMEM, VMEM),
        scratch=(
            pltpu.VMEM((per, levels * rows, LANES), f32),
            pltpu.VMEM((4, per, levels, LANES), f32),
        ),
    )(columns, imported, got1, got2, kap, land_mask, vm, vectors, gram)
    sums = lax.all_to_all(sums, ("comp", "tile"), 0, 0)
    direction, coefs = call(
        functools.partial(finish_kernel, rows, total),
        (
            jax.ShapeDtypeStruct((levels * rows, cols), f32),
            jax.ShapeDtypeStruct((1, vecs), f32),
        ),
        [VMEM] * 3,
        (VMEM, VMEM),
    )(x, vectors, sums)
    return direction.reshape(1, levels, rows, cols), coefs.reshape(vecs)


def solution(mesh):
    return jax.shard_map(
        body,
        mesh=mesh,
        in_specs=(
            P("comp", None, "tile", None),
            P(None, "comp", None, "tile", None),
            P("comp", "tile", None),
            P("comp", None, None),
            P("tile", None),
            P("comp", "tile", None, None),
            P("comp", "tile", None, None),
            P("comp", "tile", None, None),
        ),
        out_specs=(P("comp", None, "tile", None), P()),
        check_vma=False,
    )
```

```python
import functools

import jax
import jax.numpy as jnp
from jax import lax
from jax.experimental import pallas as pl
from jax.experimental.pallas import tpu as pltpu
from jax.sharding import PartitionSpec as P


FLUX = 4
LANES = 128
HBM = pl.BlockSpec(memory_space=pltpu.HBM)
VMEM = pl.BlockSpec(memory_space=pltpu.VMEM)
SMEM = pl.BlockSpec(memory_space=pltpu.SMEM)
LIMIT = 24 << 20


def call(kernel, outs, in_specs, out_specs, scratch=(), cost=None):
    return pl.pallas_call(
        kernel,
        out_shape=outs,
        in_specs=in_specs,
        out_specs=out_specs,
        scratch_shapes=list(scratch),
        cost_estimate=cost,
        compiler_params=pltpu.CompilerParams(vmem_limit_bytes=LIMIT),
    )


def in_hbm(a):
    return pltpu.with_memory_space_constraint(a, pltpu.HBM)


def split(a):
    high = a.astype(jnp.bfloat16)
    return high, (a - high.astype(jnp.float32)).astype(jnp.bfloat16)


def gather_kernel(rows, index_ref, state_ref, out_ref, x_ref, rows_ref, sems):
    cap, bands = rows_ref.shape
    per = x_ref.shape[0]
    top = FLUX * rows
    index = pltpu.make_async_copy(index_ref, rows_ref, sems.at[2 * per])
    index.start()
    copies = []
    for part, (lo, hi) in enumerate(((0, top), (top, x_ref.shape[1]))):
        for c in range(per):
            copy = pltpu.make_async_copy(
                state_ref.at[lo:hi, c * LANES : (c + 1) * LANES],
                x_ref.at[c, lo:hi, :],
                sems.at[part * per + c],
            )
            copy.start()
            copies.append(copy)
    index.wait()
    for copy in copies[:per]:
        copy.wait()

    def band(d, carry):
        for j in range(cap):
            b = rows_ref[j, d]
            r = lax.div(b, per)
            piece = x_ref[lax.rem(b, per), pl.ds(r, FLUX, stride=rows), :]
            out_ref[pl.ds(d * (cap * FLUX) + j, FLUX, stride=cap), :] = piece
        return carry

    lax.fori_loop(0, bands, band, 0)
    for copy in copies[per:]:
        copy.wait()


def gram_kernel(basis_hbm, gram_ref, basis_ref, sems):
    vecs, levels, rows, cols = basis_ref.shape
    copies = [
        pltpu.make_async_copy(basis_hbm.at[:, l], basis_ref.at[:, l], sems.at[l])
        for l in range(levels)
    ]
    for copy in copies:
        copy.start()
    n = vecs * rows
    total = jnp.zeros((n, n), jnp.float32)
    for l in range(levels):
        copies[l].wait()
        a = basis_ref[:, l].reshape(n, cols)
        total = total + lax.dot_general(
            a, a, (((1,), (1,)), ((), ())), preferred_element_type=jnp.float32
        )
    i0 = lax.broadcasted_iota(jnp.int32, (n, n), 0)
    i1 = lax.broadcasted_iota(jnp.int32, (n, n), 1)
    total = jnp.where(lax.rem(i0, rows) == lax.rem(i1, rows), total, 0.0)
    part = jnp.sum(total.reshape(vecs, rows, n), axis=1)
    j0 = lax.broadcasted_iota(jnp.int32, (n, LANES), 0)
    j1 = lax.broadcasted_iota(jnp.int32, (n, LANES), 1)
    fold = jnp.where(lax.div(j0, rows) == j1, 1.0, 0.0)
    gram = jnp.dot(part, fold, precision=lax.Precision.HIGHEST)
    packed = [jnp.zeros((1, LANES), jnp.float32), jnp.zeros((1, LANES), jnp.float32)]
    for i in range(vecs):
        shift = 16 * (i % 8)
        line = gram[i : i + 1, :]
        packed[i // 8] = packed[i // 8] + (pltpu.roll(line, shift, 1) if shift else line)
    gram_ref[...] = jnp.concatenate(packed, axis=0)


def shifted(parts, up):
    n = len(parts)
    lane = lax.broadcasted_iota(jnp.int32, parts[0].shape, 1)
    rolled = [pltpu.roll(p, 1 if up else LANES - 1, 1) for p in parts]
    edge = 0 if up else LANES - 1
    step = -1 if up else 1
    return [jnp.where(lane == edge, rolled[(c + step) % n], rolled[c]) for c in range(n)]


def early_kernel(
    rows, slots_ref, weights_ref, x_ref, kappa_ref, mask_ref, vmix_ref, matrix_ref, p1_ref, p2_ref
):
    over, blocks = slots_ref.shape
    slots = matrix_ref.shape[1]
    per = x_ref.shape[0]
    levels = x_ref.shape[1] // rows
    row = lax.broadcasted_iota(jnp.int32, (slots, blocks), 0)
    mat = jnp.zeros((slots, blocks), jnp.float32)
    for k in range(over):
        mat = mat + jnp.where(slots_ref[k : k + 1, :] == row, weights_ref[k : k + 1, :], 0.0)
    b0 = lax.broadcasted_iota(jnp.int32, (blocks, blocks), 0)
    b1 = lax.broadcasted_iota(jnp.int32, (blocks, blocks), 1)
    order = jnp.where(lax.rem(b0, rows) * per + lax.div(b0, rows) == b1, 1.0, 0.0)
    matrix_ref[...] = jnp.dot(order, mat.T, precision=lax.Precision.HIGHEST)

    ocean = lax.axis_index("comp") == 0
    even = lax.rem(lax.axis_index("tile"), 2) == 0
    vmix = vmix_ref[...]
    pays = []
    for edge, inner in ((0, 1), (rows - 1, rows - 2)):
        xs = [x_ref[c, pl.ds(edge, levels, stride=rows), :] for c in range(per)]
        left, right = shifted(xs, True), shifted(xs, False)
        pay = []
        for c in range(per):
            s = slice(c * LANES, (c + 1) * LANES)
            x = xs[c]
            xi = x_ref[c, pl.ds(inner, levels, stride=rows), :]
            k = kappa_ref[edge : edge + 1, s]
            m = jnp.where(ocean, mask_ref[edge : edge + 1, s].astype(jnp.float32), 1.0)
            acc = x + k * (xi + left[c] + right[c] - 4.0 * x)
            for q in range(levels):
                acc = acc + vmix[:, q : q + 1] * x[q : q + 1, :]
            pay.append((m * acc, x, m * k))
        pays.append(pay)
    for ref, flag in ((p1_ref, even), (p2_ref, jnp.logical_not(even))):
        for c in range(per):
            a, x, b = [jnp.where(flag, v, u) for u, v in zip(pays[0][c], pays[1][c])]
            ref[c * levels : (c + 1) * levels, :] = a
            ref[(per + c) * levels : (per + c + 1) * levels, :] = x
            ref[2 * per * levels + c : 2 * per * levels + c + 1, :] = b


def regrid_kernel(rows, buf_ref, matrix_ref, mask_ref, f_ref, e1_ref, e2_ref):
    slots = matrix_ref.shape[1]
    per = f_ref.shape[0]
    cap = buf_ref.shape[1] // FLUX
    wide = jnp.concatenate(
        [buf_ref[:, f * cap : (f + 1) * cap, :].reshape(slots, LANES) for f in range(FLUX)], axis=1
    )
    bh, bl = split(wide)
    wh, wl = split(matrix_ref[...])
    dot = functools.partial(jnp.dot, preferred_element_type=jnp.float32)
    out = dot(wh, bh) + (dot(wh, bl) + dot(wl, bh))
    for f in range(FLUX):
        for c in range(per):
            f_ref[c, f * rows : (f + 1) * rows, :] = out[
                c * rows : (c + 1) * rows, f * LANES : (f + 1) * LANES
            ]
    ocean = lax.axis_index("comp") != 0
    even = lax.rem(lax.axis_index("tile"), 2) == 0
    for c in range(per):
        s = slice(c * LANES, (c + 1) * LANES)
        edges = []
        for edge in (0, rows - 1):
            m = jnp.where(ocean, mask_ref[edge : edge + 1, s].astype(jnp.float32), 1.0)
            edges.append(m * f_ref[c, pl.ds(edge, FLUX, stride=rows), :])
        e1_ref[c * FLUX : (c + 1) * FLUX, :] = jnp.where(even, edges[1], edges[0])
        e2_ref[c * FLUX : (c + 1) * FLUX, :] = jnp.where(even, edges[0], edges[1])


def fetch_kernel(after_ref, basis_hbm, basis_ref, sems):
    copies = [
        pltpu.make_async_copy(basis_hbm.at[i], basis_ref.at[i], sems.at[i])
        for i in range(basis_ref.shape[0])
    ]
    for copy in copies:
        copy.start()
    for copy in copies:
        copy.wait()


def stencil(xs, kappa_ref, rows, prev, nxt, row):
    left, right = shifted(xs, True), shifted(xs, False)
    out = []
    for c, x in enumerate(xs):
        up = jnp.where(row == 0, prev(c), pltpu.roll(x, 1, 0))
        down = jnp.where(row == rows - 1, nxt(c), pltpu.roll(x, rows - 1, 0))
        k = kappa_ref[:, c * LANES : (c + 1) * LANES]
        out.append(k * (up + down + left[c] + right[c] - 4.0 * x))
    return out


def still_kernel(
    rows, x0_ref, h1_ref, h2_ref, kappa_ref, mask_ref, vmix_ref, x_ref, x1_ref, halo_ref
):
    per = x0_ref.shape[0]
    levels = x0_ref.shape[1] // rows
    ocean = lax.axis_index("comp") == 0
    even = lax.rem(lax.axis_index("tile"), 2) == 0
    for side in range(2):
        flag = even if side == 1 else jnp.logical_not(even)

        def take(lo, n):
            return jnp.where(flag, h1_ref[lo : lo + n, :], h2_ref[lo : lo + n, :])

        for c in range(per):
            edge = x0_ref[c, pl.ds(side * (rows - 1), levels, stride=rows), :]
            a = take(c * levels, levels)
            b = take(2 * per * levels + c, 1)
            halo_ref[side, c] = take((per + c) * levels, levels)
            halo_ref[2 + side, c] = a + b * edge
    row = lax.broadcasted_iota(jnp.int32, (rows, LANES), 0)

    def advance(src, dst, base):
        for l in range(levels):
            part = slice(l * rows, (l + 1) * rows)
            xs = [src[c, part, :] for c in range(per)]
            moved = stencil(
                xs, kappa_ref, rows,
                lambda c: halo_ref[base, c, l : l + 1, :],
                lambda c: halo_ref[base + 1, c, l : l + 1, :],
                row,
            )
            for c in range(per):
                acc = xs[c] + moved[c]
                for q in range(levels):
                    acc = acc + vmix_ref[l, q] * src[c, q * rows : (q + 1) * rows, :]
                s = slice(c * LANES, (c + 1) * LANES)
                mask = jnp.where(ocean, mask_ref[:, s].astype(jnp.float32), 1.0)
                dst[c, part, :] = mask * acc

    advance(x0_ref, x1_ref, 0)
    advance(x1_ref, x_ref, 2)


def step_kernel(
    rows, still_ref, f_ref, e1_ref, e2_ref, kappa_ref, mask_ref, vmix_ref, basis_ref, gram_ref,
    x_ref, sums_ref, f1_ref,
):
    per = still_ref.shape[0]
    levels = still_ref.shape[1] // rows
    vecs = basis_ref.shape[0]
    ocean = lax.axis_index("comp") == 0
    even = lax.rem(lax.axis_index("tile"), 2) == 0
    row = lax.broadcasted_iota(jnp.int32, (rows, LANES), 0)

    def mask(c):
        m = mask_ref[:, c * LANES : (c + 1) * LANES].astype(jnp.float32)
        return jnp.where(ocean, m, 1.0)

    for c in range(per):
        m = mask(c)
        for f in range(FLUX):
            part = slice(f * rows, (f + 1) * rows)
            f1_ref[c, part, :] = m * f_ref[c, part, :]
    for l in range(levels):
        part = slice(l * rows, (l + 1) * rows)
        if l < FLUX:
            fs = [f1_ref[c, part, :] for c in range(per)]

            def edge(c, flag):
                i = slice(c * FLUX + l, c * FLUX + l + 1)
                return jnp.where(flag, e1_ref[i, :], e2_ref[i, :])

            moved = stencil(
                fs, kappa_ref, rows,
                lambda c: edge(c, jnp.logical_not(even)), lambda c: edge(c, even), row,
            )
        for c in range(per):
            acc = fs[c] + moved[c] + f_ref[c, part, :] if l < FLUX else 0.0
            for q in range(FLUX):
                acc = acc + vmix_ref[l, q] * f1_ref[c, q * rows : (q + 1) * rows, :]
            x_ref[c, part, :] = still_ref[c, part, :] + mask(c) * acc

    def level(l, accs):
        accs = list(accs)
        for c in range(per):
            s = slice(c * LANES, (c + 1) * LANES)
            x = x_ref[c, pl.ds(l * rows, rows), :]
            for i in range(vecs):
                t = x * basis_ref[i, l, :, s].astype(jnp.float32)
                accs[i] = accs[i] + t.reshape(rows // 8, 8, LANES).sum(0)
            accs[vecs] = accs[vecs] + (x * x).reshape(rows // 8, 8, LANES).sum(0)
        return tuple(accs)

    zero = jnp.zeros((8, LANES), jnp.float32)
    accs = lax.fori_loop(0, levels, level, (zero,) * (vecs + 1))
    lane = lax.broadcasted_iota(jnp.int32, (1, LANES), 1)
    line = jnp.zeros((1, LANES), jnp.float32)
    for i in range(vecs + 1):
        tot = jnp.sum(jnp.sum(accs[i], axis=0, keepdims=True), axis=1, keepdims=True)
        line = line + jnp.where(lane == 64 + i, tot, 0.0)
    block = gram_ref[...] + jnp.concatenate([jnp.zeros((1, LANES), jnp.float32), line], axis=0)
    for d in range(sums_ref.shape[0]):
        sums_ref[d] = block


def finish_kernel(rows, total, x_ref, basis_ref, sums_ref, out_ref, coef_ref):
    per = x_ref.shape[0]
    levels = x_ref.shape[1] // rows
    vecs = basis_ref.shape[0]
    sums = jnp.sum(sums_ref[...], axis=0)
    lane = lax.broadcasted_iota(jnp.int32, (1, LANES), 1)
    tail = pltpu.roll(sums[1:2, :], 64, 1)
    coef = jnp.where(lane < vecs, tail, 0.0) / total
    coef_ref[...] = coef[:, :vecs]
    square = jnp.sum(jnp.where(lane == vecs, tail, 0.0), axis=1, keepdims=True)
    splat = [jnp.sum(jnp.where(lane == i, coef, 0.0), axis=1, keepdims=True) for i in range(vecs)]
    quad = jnp.zeros((1, LANES), jnp.float32)
    for i in range(vecs):
        shift = (LANES - 16 * (i % 8)) % LANES
        line = sums[i // 8 : i // 8 + 1, :]
        line = pltpu.roll(line, shift, 1) if shift else line
        quad = quad + splat[i] * jnp.where(lane < vecs, line, 0.0)
    extra = jnp.sum(coef * (quad - 2.0 * total * coef), axis=1, keepdims=True)
    scale = 1.0 / jnp.sqrt((square + extra) / total + 1e-06)
    wide = [jnp.broadcast_to(scale * s, (8, LANES)) for s in splat]
    scale = jnp.broadcast_to(scale, (8, LANES))

    def level(l, carry):
        for c in range(per):
            s = slice(c * LANES, (c + 1) * LANES)
            x = x_ref[c, pl.ds(l * rows, rows), :].reshape(rows // 8, 8, LANES) * scale
            for i in range(vecs):
                b = basis_ref[i, l, :, s].astype(jnp.float32).reshape(rows // 8, 8, LANES)
                x = x - wide[i] * b
            out_ref[pl.ds(l * rows, rows), s] = x.reshape(rows, LANES)
        return carry

    lax.fori_loop(0, levels, level, 0)


def body(state, basis, kappa, vmix, land_mask, send_rows, recv_slots, recv_weights):
    _, levels, rows, cols = state.shape
    vecs = basis.shape[0]
    bands, cap = send_rows.shape[2:]
    blocks, _ = recv_slots.shape[2:]
    per = cols // LANES
    comps = lax.axis_size("comp")
    devices = comps * bands
    total = float(levels * rows * cols * devices)
    f32 = jnp.float32
    flat = state.reshape(levels * rows, cols)
    vectors = basis[:, 0]
    kap, vm = kappa[0], vmix[0]

    field = jax.ShapeDtypeStruct((per, levels * rows, LANES), f32)
    import_field = jax.ShapeDtypeStruct((per, FLUX * rows, LANES), f32)
    pay = jax.ShapeDtypeStruct((2 * levels * per + per, LANES), f32)
    fringe = jax.ShapeDtypeStruct((per * FLUX, LANES), f32)
    pairs1 = [(i, i ^ 1) for i in range(bands)]
    pairs2 = [p for i in range(1, bands - 1, 2) for p in ((i, i + 1), (i + 1, i))]
    swap = [(i, i ^ 1) for i in range(comps)]

    def crossed(pairs):
        return [((c * bands) + i, (c ^ 1) * bands + k) for c in range(comps) for i, k in pairs]

    bucket, columns = call(
        functools.partial(gather_kernel, rows),
        (jax.ShapeDtypeStruct((bands * FLUX * cap, LANES), f32), field),
        [HBM, HBM],
        (VMEM, VMEM),
        scratch=(pltpu.SMEM((cap, bands), jnp.int32), pltpu.SemaphoreType.DMA((2 * per + 1,))),
    )(in_hbm(send_rows[0, 0].T), in_hbm(flat))
    moved = lax.all_to_all(bucket.reshape(bands, FLUX * cap, LANES), "tile", 0, 0)
    matrix, pay1, pay2 = call(
        functools.partial(early_kernel, rows),
        (jax.ShapeDtypeStruct((blocks, bands * cap), f32), pay, pay),
        [VMEM] * 6,
        (VMEM,) * 3,
    )(recv_slots[0, 0].T, recv_weights[0, 0].T, columns, kap, land_mask, vm)
    matrix = lax.ppermute(matrix, "comp", swap)
    got1 = lax.ppermute(pay1, "tile", pairs1)
    got2 = lax.ppermute(pay2, "tile", pairs2)
    gram = call(
        gram_kernel,
        jax.ShapeDtypeStruct((2, LANES), f32),
        [HBM],
        VMEM,
        scratch=(
            pltpu.VMEM(vectors.shape, vectors.dtype),
            pltpu.SemaphoreType.DMA((levels,)),
        ),
        cost=pl.CostEstimate(flops=10**9, bytes_accessed=4 << 20, transcendentals=0),
    )(in_hbm(vectors))
    still = call(
        functools.partial(still_kernel, rows),
        field,
        [VMEM] * 5 + [SMEM],
        VMEM,
        scratch=(
            pltpu.VMEM((per, levels * rows, LANES), f32),
            pltpu.VMEM((4, per, levels, LANES), f32),
        ),
    )(columns, got1, got2, kap, land_mask, vm)

    foreign, edge1, edge2 = call(
        functools.partial(regrid_kernel, rows),
        (import_field, fringe, fringe),
        [VMEM] * 3,
        (VMEM,) * 3,
    )(moved, matrix, land_mask)
    vectors = call(
        fetch_kernel,
        jax.ShapeDtypeStruct(vectors.shape, vectors.dtype),
        [pl.BlockSpec(memory_space=pl.ANY), HBM],
        VMEM,
        scratch=(pltpu.SemaphoreType.DMA((vecs,)),),
    )(edge1, in_hbm(vectors))
    imported = lax.ppermute(foreign, "comp", swap)
    edge1 = lax.ppermute(edge1, ("comp", "tile"), crossed(pairs1))
    edge2 = lax.ppermute(edge2, ("comp", "tile"), crossed(pairs2))
    x, sums = call(
        functools.partial(step_kernel, rows),
        (field, jax.ShapeDtypeStruct((devices, 2, LANES), f32)),
        [VMEM] * 6 + [SMEM] + [VMEM] * 2,
        (VMEM, VMEM),
        scratch=(pltpu.VMEM((per, FLUX * rows, LANES), f32),),
    )(still, imported, edge1, edge2, kap, land_mask, vm, vectors, gram)
    sums = lax.all_to_all(sums, ("comp", "tile"), 0, 0)
    direction, coefs = call(
        functools.partial(finish_kernel, rows, total),
        (
            jax.ShapeDtypeStruct((levels * rows, cols), f32),
            jax.ShapeDtypeStruct((1, vecs), f32),
        ),
        [VMEM] * 3,
        (VMEM, VMEM),
    )(x, vectors, sums)
    return direction.reshape(1, levels, rows, cols), coefs.reshape(vecs)


def solution(mesh):
    return jax.shard_map(
        body,
        mesh=mesh,
        in_specs=(
            P("comp", None, "tile", None),
            P(None, "comp", None, "tile", None),
            P("comp", "tile", None),
            P("comp", None, None),
            P("tile", None),
            P("comp", "tile", None, None),
            P("comp", "tile", None, None),
            P("comp", "tile", None, None),
        ),
        out_specs=(P("comp", None, "tile", None), P()),
        check_vma=False,
    )
```

```python
import functools

import jax
import jax.numpy as jnp
from jax import lax
from jax.experimental import pallas as pl
from jax.experimental.pallas import tpu as pltpu
from jax.sharding import PartitionSpec as P


FLUX = 4
LANES = 128
HBM = pl.BlockSpec(memory_space=pltpu.HBM)
VMEM = pl.BlockSpec(memory_space=pltpu.VMEM)
LIMIT = 24 << 20


def call(kernel, outs, in_specs, out_specs, scratch=(), cost=None):
    return pl.pallas_call(
        kernel,
        out_shape=outs,
        in_specs=in_specs,
        out_specs=out_specs,
        scratch_shapes=list(scratch),
        cost_estimate=cost,
        compiler_params=pltpu.CompilerParams(vmem_limit_bytes=LIMIT),
    )


def in_hbm(a):
    return pltpu.with_memory_space_constraint(a, pltpu.HBM)


def split(a):
    high = a.astype(jnp.bfloat16)
    return high, (a - high.astype(jnp.float32)).astype(jnp.bfloat16)


def block_place(b, per):
    if per & (per - 1) == 0:
        bits = per.bit_length() - 1
        return lax.shift_right_logical(b, bits), lax.bitwise_and(b, per - 1)
    return lax.div(b, per), lax.rem(b, per)


def gather_kernel(rows, index_ref, state_ref, *refs):
    small = (len(refs) - 4) // 2
    sides, out_ref, x_ref = refs[:small], refs[small], refs[small + 1]
    side_outs, (rows_ref, sems) = refs[small + 2 : 2 * small + 2], refs[2 * small + 2 :]
    cap, bands = rows_ref.shape
    per = x_ref.shape[0]
    top = FLUX * rows
    index = pltpu.make_async_copy(index_ref, rows_ref, sems.at[2 * per])
    index.start()
    copies = []
    for part, (lo, hi) in enumerate(((0, top), (top, x_ref.shape[1]))):
        for c in range(per):
            copies.append(
                pltpu.make_async_copy(
                    state_ref.at[lo:hi, c * LANES : (c + 1) * LANES],
                    x_ref.at[c, lo:hi, :],
                    sems.at[part * per + c],
                )
            )
    for k, (src, dst) in enumerate(zip(sides, side_outs)):
        copies.append(pltpu.make_async_copy(src, dst, sems.at[2 * per + 1 + k]))
    for copy in copies:
        copy.start()
    index.wait()
    for copy in copies[:per]:
        copy.wait()

    def band(d, carry):
        for j in range(cap):
            r, c = block_place(rows_ref[j, d], per)
            piece = x_ref[c, pl.ds(r, FLUX, stride=rows), :]
            out_ref[pl.ds(d * (cap * FLUX) + j, FLUX, stride=cap), :] = piece
        return carry

    lax.fori_loop(0, bands, band, 0, unroll=2)
    for copy in copies[per:]:
        copy.wait()


def gram_kernel(basis_hbm, gram_ref, basis_ref, sems):
    vecs, levels, rows, cols = basis_ref.shape
    ahead = 3
    copies = [
        pltpu.make_async_copy(basis_hbm.at[:, l], basis_ref.at[:, l], sems.at[l])
        for l in range(levels)
    ]
    for copy in copies[:ahead]:
        copy.start()
    n = vecs * rows
    total = jnp.zeros((n, n), jnp.float32)
    for l in range(levels):
        copies[l].wait()
        if l + ahead < levels:
            copies[l + ahead].start()
        a = basis_ref[:, l].reshape(n, cols)
        total = total + lax.dot_general(
            a, a, (((1,), (1,)), ((), ())), preferred_element_type=jnp.float32
        )
    i0 = lax.broadcasted_iota(jnp.int32, (n, n), 0)
    i1 = lax.broadcasted_iota(jnp.int32, (n, n), 1)
    total = jnp.where(lax.rem(i0, rows) == lax.rem(i1, rows), total, 0.0)
    part = jnp.sum(total.reshape(vecs, rows, n), axis=1)
    j0 = lax.broadcasted_iota(jnp.int32, (n, LANES), 0)
    j1 = lax.broadcasted_iota(jnp.int32, (n, LANES), 1)
    fold = jnp.where(lax.div(j0, rows) == j1, 1.0, 0.0)
    gram = jnp.dot(part, fold, precision=lax.Precision.HIGHEST)
    packed = [jnp.zeros((1, LANES), jnp.float32), jnp.zeros((1, LANES), jnp.float32)]
    for i in range(vecs):
        shift = 16 * (i % 8)
        line = gram[i : i + 1, :]
        packed[i // 8] = packed[i // 8] + (pltpu.roll(line, shift, 1) if shift else line)
    gram_ref[...] = jnp.concatenate(packed, axis=0)


def shifted(parts, up):
    n = len(parts)
    lane = lax.broadcasted_iota(jnp.int32, parts[0].shape, 1)
    rolled = [pltpu.roll(p, 1 if up else LANES - 1, 1) for p in parts]
    edge = 0 if up else LANES - 1
    step = -1 if up else 1
    return [jnp.where(lane == edge, rolled[(c + step) % n], rolled[c]) for c in range(n)]


def early_kernel(
    rows, slots_ref, weights_ref, x_ref, kappa_ref, mask_ref, vmix_ref,
    matrix_ref, p1_ref, p2_ref, table_ref,
):
    over, blocks = slots_ref.shape
    slots = matrix_ref.shape[1]
    per = x_ref.shape[0]
    levels = x_ref.shape[1] // rows
    row = lax.broadcasted_iota(jnp.int32, (slots, blocks), 0)
    mat = jnp.zeros((slots, blocks), jnp.float32)
    for k in range(over):
        mat = mat + jnp.where(slots_ref[k : k + 1, :] == row, weights_ref[k : k + 1, :], 0.0)
    b0 = lax.broadcasted_iota(jnp.int32, (blocks, blocks), 0)
    b1 = lax.broadcasted_iota(jnp.int32, (blocks, blocks), 1)
    order = jnp.where(lax.rem(b0, rows) * per + lax.div(b0, rows) == b1, 1.0, 0.0)
    matrix_ref[...] = jnp.dot(order, mat.T, precision=lax.Precision.HIGHEST)

    ocean = lax.axis_index("comp") == 0
    even = lax.rem(lax.axis_index("tile"), 2) == 0
    vmix = vmix_ref[...]
    d0 = lax.broadcasted_iota(jnp.int32, (levels, levels), 0)
    d1 = lax.broadcasted_iota(jnp.int32, (levels, levels), 1)
    for l in range(levels):
        column = jnp.sum(jnp.where(d0 == d1, vmix[l : l + 1, :], 0.0), axis=1, keepdims=True)
        table_ref[l * levels : (l + 1) * levels, :] = jnp.broadcast_to(column, (levels, LANES))
    pays = []
    for edge, inner in ((0, 1), (rows - 1, rows - 2)):
        xs = [x_ref[c, pl.ds(edge, levels, stride=rows), :] for c in range(per)]
        left, right = shifted(xs, True), shifted(xs, False)
        pay = []
        for c in range(per):
            s = slice(c * LANES, (c + 1) * LANES)
            x = xs[c]
            xi = x_ref[c, pl.ds(inner, levels, stride=rows), :]
            k = kappa_ref[edge : edge + 1, s]
            m = jnp.where(ocean, mask_ref[edge : edge + 1, s].astype(jnp.float32), 1.0)
            acc = x + k * (xi + left[c] + right[c] - 4.0 * x)
            for q in range(levels):
                acc = acc + vmix[:, q : q + 1] * x[q : q + 1, :]
            pay.append((m * acc, x, m * k))
        pays.append(pay)
    for ref, flag in ((p1_ref, even), (p2_ref, jnp.logical_not(even))):
        for c in range(per):
            a, x, b = [jnp.where(flag, v, u) for u, v in zip(pays[0][c], pays[1][c])]
            ref[c * levels : (c + 1) * levels, :] = a
            ref[(per + c) * levels : (per + c + 1) * levels, :] = x
            ref[2 * per * levels + c : 2 * per * levels + c + 1, :] = b


def regrid_kernel(rows, after1_ref, after2_ref, buf_ref, matrix_ref, mask_ref, f_ref, e1_ref, e2_ref):
    slots = matrix_ref.shape[1]
    per = f_ref.shape[0]
    cap = buf_ref.shape[1] // FLUX
    wide = jnp.concatenate(
        [buf_ref[:, f * cap : (f + 1) * cap, :].reshape(slots, LANES) for f in range(FLUX)], axis=1
    )
    bh, bl = split(wide)
    wh, wl = split(matrix_ref[...])
    dot = functools.partial(jnp.dot, preferred_element_type=jnp.float32)
    out = dot(wh, bh) + (dot(wh, bl) + dot(wl, bh))
    for f in range(FLUX):
        for c in range(per):
            f_ref[c, f * rows : (f + 1) * rows, :] = out[
                c * rows : (c + 1) * rows, f * LANES : (f + 1) * LANES
            ]
    ocean = lax.axis_index("comp") != 0
    even = lax.rem(lax.axis_index("tile"), 2) == 0
    for c in range(per):
        s = slice(c * LANES, (c + 1) * LANES)
        edges = []
        for edge in (0, rows - 1):
            m = jnp.where(ocean, mask_ref[edge : edge + 1, s].astype(jnp.float32), 1.0)
            edges.append(m * f_ref[c, pl.ds(edge, FLUX, stride=rows), :])
        e1_ref[c * FLUX : (c + 1) * FLUX, :] = jnp.where(even, edges[1], edges[0])
        e2_ref[c * FLUX : (c + 1) * FLUX, :] = jnp.where(even, edges[0], edges[1])


def stencil(xs, kappa_ref, rows, prev, nxt, row):
    left, right = shifted(xs, True), shifted(xs, False)
    out = []
    for c, x in enumerate(xs):
        up = jnp.where(row == 0, prev(c), pltpu.roll(x, 1, 0))
        down = jnp.where(row == rows - 1, nxt(c), pltpu.roll(x, rows - 1, 0))
        k = kappa_ref[:, c * LANES : (c + 1) * LANES]
        out.append(k * (up + down + left[c] + right[c] - 4.0 * x))
    return out


def still_kernel(
    rows, after_ref, basis_hbm, x0_ref, h1_ref, h2_ref, kappa_ref, mask_ref, table_ref,
    x_ref, basis_ref, x1_ref, halo_ref, sems,
):
    copies = [
        pltpu.make_async_copy(basis_hbm.at[i], basis_ref.at[i], sems.at[i])
        for i in range(basis_ref.shape[0])
    ]
    for copy in copies:
        copy.start()
    per = x0_ref.shape[0]
    levels = x0_ref.shape[1] // rows
    ocean = lax.axis_index("comp") == 0
    even = lax.rem(lax.axis_index("tile"), 2) == 0
    for side in range(2):
        flag = even if side == 1 else jnp.logical_not(even)

        def take(lo, n):
            return jnp.where(flag, h1_ref[lo : lo + n, :], h2_ref[lo : lo + n, :])

        for c in range(per):
            edge = x0_ref[c, pl.ds(side * (rows - 1), levels, stride=rows), :]
            a = take(c * levels, levels)
            b = take(2 * per * levels + c, 1)
            halo_ref[side, c] = take((per + c) * levels, levels)
            halo_ref[2 + side, c] = a + b * edge
    row = lax.broadcasted_iota(jnp.int32, (rows, LANES), 0)

    def advance(src, dst, base):
        for l in range(levels):
            part = slice(l * rows, (l + 1) * rows)
            xs = [src[c, part, :] for c in range(per)]
            moved = stencil(
                xs, kappa_ref, rows,
                lambda c: halo_ref[base, c, l : l + 1, :],
                lambda c: halo_ref[base + 1, c, l : l + 1, :],
                row,
            )
            for c in range(per):
                acc = xs[c] + moved[c]
                for q in range(levels):
                    v = table_ref[l * levels + q : l * levels + q + 1, :]
                    acc = acc + v * src[c, q * rows : (q + 1) * rows, :]
                s = slice(c * LANES, (c + 1) * LANES)
                mask = jnp.where(ocean, mask_ref[:, s].astype(jnp.float32), 1.0)
                dst[c, part, :] = mask * acc

    advance(x0_ref, x1_ref, 0)
    advance(x1_ref, x_ref, 2)
    for copy in copies:
        copy.wait()


def step_kernel(
    rows, still_ref, f_ref, e1_ref, e2_ref, kappa_ref, mask_ref, table_ref, basis_ref, gram_ref,
    x_ref, sums_ref, f1_ref,
):
    per = still_ref.shape[0]
    levels = still_ref.shape[1] // rows
    vecs = basis_ref.shape[0]
    ocean = lax.axis_index("comp") == 0
    even = lax.rem(lax.axis_index("tile"), 2) == 0
    row = lax.broadcasted_iota(jnp.int32, (rows, LANES), 0)

    def mask(c):
        m = mask_ref[:, c * LANES : (c + 1) * LANES].astype(jnp.float32)
        return jnp.where(ocean, m, 1.0)

    for c in range(per):
        m = mask(c)
        for f in range(FLUX):
            part = slice(f * rows, (f + 1) * rows)
            f1_ref[c, part, :] = m * f_ref[c, part, :]
    for l in range(levels):
        part = slice(l * rows, (l + 1) * rows)
        if l < FLUX:
            fs = [f1_ref[c, part, :] for c in range(per)]

            def edge(c, flag):
                i = slice(c * FLUX + l, c * FLUX + l + 1)
                return jnp.where(flag, e1_ref[i, :], e2_ref[i, :])

            moved = stencil(
                fs, kappa_ref, rows,
                lambda c: edge(c, jnp.logical_not(even)), lambda c: edge(c, even), row,
            )
        for c in range(per):
            acc = fs[c] + moved[c] + f_ref[c, part, :] if l < FLUX else 0.0
            for q in range(FLUX):
                v = table_ref[l * levels + q : l * levels + q + 1, :]
                acc = acc + v * f1_ref[c, q * rows : (q + 1) * rows, :]
            x_ref[c, part, :] = still_ref[c, part, :] + mask(c) * acc

    def level(l, accs):
        accs = list(accs)
        for c in range(per):
            s = slice(c * LANES, (c + 1) * LANES)
            x = x_ref[c, pl.ds(l * rows, rows), :]
            for i in range(vecs):
                t = x * basis_ref[i, l, :, s].astype(jnp.float32)
                accs[i] = accs[i] + t.reshape(rows // 8, 8, LANES).sum(0)
            accs[vecs] = accs[vecs] + (x * x).reshape(rows // 8, 8, LANES).sum(0)
        return tuple(accs)

    zero = jnp.zeros((8, LANES), jnp.float32)
    accs = lax.fori_loop(0, levels, level, (zero,) * (vecs + 1))
    lane = lax.broadcasted_iota(jnp.int32, (1, LANES), 1)
    line = jnp.zeros((1, LANES), jnp.float32)
    for i in range(vecs + 1):
        tot = jnp.sum(jnp.sum(accs[i], axis=0, keepdims=True), axis=1, keepdims=True)
        line = line + jnp.where(lane == 64 + i, tot, 0.0)
    block = gram_ref[...] + jnp.concatenate([jnp.zeros((1, LANES), jnp.float32), line], axis=0)
    for d in range(sums_ref.shape[0]):
        sums_ref[d] = block


def finish_kernel(rows, total, x_ref, basis_ref, sums_ref, out_hbm, coef_ref, out_ref, sems):
    per = x_ref.shape[0]
    levels = x_ref.shape[1] // rows
    vecs = basis_ref.shape[0]
    sums = jnp.sum(sums_ref[...], axis=0)
    lane = lax.broadcasted_iota(jnp.int32, (1, LANES), 1)
    tail = pltpu.roll(sums[1:2, :], 64, 1)
    coef = jnp.where(lane < vecs, tail, 0.0) / total
    coef_ref[...] = coef[:, :vecs]
    square = jnp.sum(jnp.where(lane == vecs, tail, 0.0), axis=1, keepdims=True)
    splat = [jnp.sum(jnp.where(lane == i, coef, 0.0), axis=1, keepdims=True) for i in range(vecs)]
    quad = jnp.zeros((1, LANES), jnp.float32)
    for i in range(vecs):
        shift = (LANES - 16 * (i % 8)) % LANES
        line = sums[i // 8 : i // 8 + 1, :]
        line = pltpu.roll(line, shift, 1) if shift else line
        quad = quad + splat[i] * jnp.where(lane < vecs, line, 0.0)
    extra = jnp.sum(coef * (quad - 2.0 * total * coef), axis=1, keepdims=True)
    scale = 1.0 / jnp.sqrt((square + extra) / total + 1e-06)
    wide = [jnp.broadcast_to(scale * s, (8, LANES)) for s in splat]
    scale = jnp.broadcast_to(scale, (8, LANES))

    def put(l):
        part = pl.ds(pl.multiple_of(l * rows, rows), rows)
        return pltpu.make_async_copy(out_ref.at[part, :], out_hbm.at[part, :], sems.at[l])

    def level(l, carry):
        for c in range(per):
            s = slice(c * LANES, (c + 1) * LANES)
            x = x_ref[c, pl.ds(l * rows, rows), :].reshape(rows // 8, 8, LANES) * scale
            for i in range(vecs):
                b = basis_ref[i, l, :, s].astype(jnp.float32).reshape(rows // 8, 8, LANES)
                x = x - wide[i] * b
            out_ref[pl.ds(l * rows, rows), s] = x.reshape(rows, LANES)
        put(l).start()
        return carry

    lax.fori_loop(0, levels, level, 0)
    for l in range(levels):
        put(l).wait()


def body(state, basis, kappa, vmix, land_mask, send_rows, recv_slots, recv_weights):
    _, levels, rows, cols = state.shape
    vecs = basis.shape[0]
    bands, cap = send_rows.shape[2:]
    blocks, _ = recv_slots.shape[2:]
    per = cols // LANES
    comps = lax.axis_size("comp")
    devices = comps * bands
    total = float(levels * rows * cols * devices)
    f32 = jnp.float32
    flat = state.reshape(levels * rows, cols)
    vectors = basis[:, 0]
    kap, vm = kappa[0], vmix[0]

    field = jax.ShapeDtypeStruct((per, levels * rows, LANES), f32)
    import_field = jax.ShapeDtypeStruct((per, FLUX * rows, LANES), f32)
    pay = jax.ShapeDtypeStruct((2 * levels * per + per, LANES), f32)
    fringe = jax.ShapeDtypeStruct((per * FLUX, LANES), f32)
    pairs1 = [(i, i ^ 1) for i in range(bands)]
    pairs2 = [p for i in range(1, bands - 1, 2) for p in ((i, i + 1), (i + 1, i))]
    swap = [(i, i ^ 1) for i in range(comps)]

    def crossed(pairs):
        return [((c * bands) + i, (c ^ 1) * bands + k) for c in range(comps) for i, k in pairs]

    sides = (kap, land_mask, recv_slots[0, 0].T, recv_weights[0, 0].T, vm)
    bucket, columns, kap, land_mask, slots, weights, vm = call(
        functools.partial(gather_kernel, rows),
        (jax.ShapeDtypeStruct((bands * FLUX * cap, LANES), f32), field)
        + tuple(jax.ShapeDtypeStruct(a.shape, a.dtype) for a in sides),
        [HBM] * (2 + len(sides)),
        (VMEM,) * (2 + len(sides)),
        scratch=(
            pltpu.SMEM((cap, bands), jnp.int32),
            pltpu.SemaphoreType.DMA((2 * per + 1 + len(sides),)),
        ),
    )(*[in_hbm(a) for a in (send_rows[0, 0].T, flat) + sides])
    moved = lax.all_to_all(bucket.reshape(bands, FLUX * cap, LANES), "tile", 0, 0)
    matrix, pay1, pay2, table = call(
        functools.partial(early_kernel, rows),
        (
            jax.ShapeDtypeStruct((blocks, bands * cap), f32),
            pay,
            pay,
            jax.ShapeDtypeStruct((levels * levels, LANES), f32),
        ),
        [VMEM] * 6,
        (VMEM,) * 4,
    )(slots, weights, columns, kap, land_mask, vm)
    matrix = lax.ppermute(matrix, "comp", swap)
    got1 = lax.ppermute(pay1, "tile", pairs1)
    got2 = lax.ppermute(pay2, "tile", pairs2)
    gram = call(
        gram_kernel,
        jax.ShapeDtypeStruct((2, LANES), f32),
        [HBM],
        VMEM,
        scratch=(
            pltpu.VMEM(vectors.shape, vectors.dtype),
            pltpu.SemaphoreType.DMA((levels,)),
        ),
        cost=pl.CostEstimate(flops=10**9, bytes_accessed=4 << 20, transcendentals=0),
    )(in_hbm(vectors))
    foreign, edge1, edge2 = call(
        functools.partial(regrid_kernel, rows),
        (import_field, fringe, fringe),
        [pl.BlockSpec(memory_space=pl.ANY)] * 2 + [VMEM] * 3,
        (VMEM,) * 3,
    )(got1, got2, moved, matrix, land_mask)
    still, vectors = call(
        functools.partial(still_kernel, rows),
        (field, jax.ShapeDtypeStruct(vectors.shape, vectors.dtype)),
        [pl.BlockSpec(memory_space=pl.ANY), HBM] + [VMEM] * 6,
        (VMEM, VMEM),
        scratch=(
            pltpu.VMEM((per, levels * rows, LANES), f32),
            pltpu.VMEM((4, per, levels, LANES), f32),
            pltpu.SemaphoreType.DMA((vecs,)),
        ),
    )(edge1, in_hbm(vectors), columns, got1, got2, kap, land_mask, table)
    imported = lax.ppermute(foreign, "comp", swap)
    edge1 = lax.ppermute(edge1, ("comp", "tile"), crossed(pairs1))
    edge2 = lax.ppermute(edge2, ("comp", "tile"), crossed(pairs2))
    x, sums = call(
        functools.partial(step_kernel, rows),
        (field, jax.ShapeDtypeStruct((devices, 2, LANES), f32)),
        [VMEM] * 9,
        (VMEM, VMEM),
        scratch=(pltpu.VMEM((per, FLUX * rows, LANES), f32),),
    )(still, imported, edge1, edge2, kap, land_mask, table, vectors, gram)
    sums = lax.all_to_all(sums, ("comp", "tile"), 0, 0)
    direction, coefs = call(
        functools.partial(finish_kernel, rows, total),
        (
            jax.ShapeDtypeStruct((levels * rows, cols), f32),
            jax.ShapeDtypeStruct((1, vecs), f32),
        ),
        [VMEM] * 3,
        (HBM, VMEM),
        scratch=(
            pltpu.VMEM((levels * rows, cols), f32),
            pltpu.SemaphoreType.DMA((levels,)),
        ),
    )(x, vectors, sums)
    return direction.reshape(1, levels, rows, cols), coefs.reshape(vecs)


def solution(mesh):
    return jax.shard_map(
        body,
        mesh=mesh,
        in_specs=(
            P("comp", None, "tile", None),
            P(None, "comp", None, "tile", None),
            P("comp", "tile", None),
            P("comp", None, None),
            P("tile", None),
            P("comp", "tile", None, None),
            P("comp", "tile", None, None),
            P("comp", "tile", None, None),
        ),
        out_specs=(P("comp", None, "tile", None), P()),
        check_vma=False,
    )
```

```python
import functools

import jax
import jax.numpy as jnp
from jax import lax
from jax.experimental import pallas as pl
from jax.experimental.pallas import tpu as pltpu
from jax.sharding import PartitionSpec as P


FLUX = 4
LANES = 128
HBM = pl.BlockSpec(memory_space=pltpu.HBM)
VMEM = pl.BlockSpec(memory_space=pltpu.VMEM)
LIMIT = 24 << 20


def call(kernel, outs, in_specs, out_specs, scratch=(), cost=None):
    return pl.pallas_call(
        kernel,
        out_shape=outs,
        in_specs=in_specs,
        out_specs=out_specs,
        scratch_shapes=list(scratch),
        cost_estimate=cost,
        compiler_params=pltpu.CompilerParams(vmem_limit_bytes=LIMIT),
    )


def in_hbm(a):
    return pltpu.with_memory_space_constraint(a, pltpu.HBM)


def split(a):
    high = a.astype(jnp.bfloat16)
    return high, (a - high.astype(jnp.float32)).astype(jnp.bfloat16)


def block_place(b, per):
    if per & (per - 1) == 0:
        bits = per.bit_length() - 1
        return lax.shift_right_logical(b, bits), lax.bitwise_and(b, per - 1)
    return lax.div(b, per), lax.rem(b, per)


def gather_kernel(rows, index_ref, state_ref, *refs):
    small = (len(refs) - 4) // 2
    sides, out_ref, x_ref = refs[:small], refs[small], refs[small + 1]
    side_outs, (rows_ref, sems) = refs[small + 2 : 2 * small + 2], refs[2 * small + 2 :]
    cap, bands = rows_ref.shape
    per = x_ref.shape[0]
    top = FLUX * rows
    index = pltpu.make_async_copy(index_ref, rows_ref, sems.at[2 * per])
    index.start()
    copies = []
    for part, (lo, hi) in enumerate(((0, top), (top, x_ref.shape[1]))):
        for c in range(per):
            copies.append(
                pltpu.make_async_copy(
                    state_ref.at[lo:hi, c * LANES : (c + 1) * LANES],
                    x_ref.at[c, lo:hi, :],
                    sems.at[part * per + c],
                )
            )
    for k, (src, dst) in enumerate(zip(sides, side_outs)):
        copies.append(pltpu.make_async_copy(src, dst, sems.at[2 * per + 1 + k]))
    for copy in copies:
        copy.start()
    index.wait()
    for copy in copies[:per]:
        copy.wait()

    def band(d, carry):
        for j in range(cap):
            r, c = block_place(rows_ref[j, d], per)
            piece = x_ref[c, pl.ds(r, FLUX, stride=rows), :]
            out_ref[pl.ds(d * (cap * FLUX) + j, FLUX, stride=cap), :] = piece
        return carry

    lax.fori_loop(0, bands, band, 0, unroll=2)
    for copy in copies[per:]:
        copy.wait()


def gram_kernel(after_ref, basis_hbm, basis_ref, gram_ref, sems):
    vecs, levels, rows, cols = basis_ref.shape
    copies = [
        pltpu.make_async_copy(basis_hbm.at[:, l], basis_ref.at[:, l], sems.at[l])
        for l in range(levels)
    ]
    for copy in copies:
        copy.start()
    n = vecs * rows
    total = jnp.zeros((n, n), jnp.float32)
    for l in range(levels):
        copies[l].wait()
        a = basis_ref[:, l].reshape(n, cols)
        total = total + lax.dot_general(
            a, a, (((1,), (1,)), ((), ())), preferred_element_type=jnp.float32
        )
    i0 = lax.broadcasted_iota(jnp.int32, (n, n), 0)
    i1 = lax.broadcasted_iota(jnp.int32, (n, n), 1)
    total = jnp.where(lax.rem(i0, rows) == lax.rem(i1, rows), total, 0.0)
    part = jnp.sum(total.reshape(vecs, rows, n), axis=1)
    j0 = lax.broadcasted_iota(jnp.int32, (n, LANES), 0)
    j1 = lax.broadcasted_iota(jnp.int32, (n, LANES), 1)
    fold = jnp.where(lax.div(j0, rows) == j1, 1.0, 0.0)
    gram = jnp.dot(part, fold, precision=lax.Precision.HIGHEST)
    packed = [jnp.zeros((1, LANES), jnp.float32), jnp.zeros((1, LANES), jnp.float32)]
    for i in range(vecs):
        shift = 16 * (i % 8)
        line = gram[i : i + 1, :]
        packed[i // 8] = packed[i // 8] + (pltpu.roll(line, shift, 1) if shift else line)
    gram_ref[...] = jnp.concatenate(packed, axis=0)


def shifted(parts, up):
    n = len(parts)
    lane = lax.broadcasted_iota(jnp.int32, parts[0].shape, 1)
    rolled = [pltpu.roll(p, 1 if up else LANES - 1, 1) for p in parts]
    edge = 0 if up else LANES - 1
    step = -1 if up else 1
    return [jnp.where(lane == edge, rolled[(c + step) % n], rolled[c]) for c in range(n)]


def early_kernel(
    rows, slots_ref, weights_ref, x_ref, kappa_ref, mask_ref, vmix_ref,
    matrix_ref, p1_ref, p2_ref, table_ref,
):
    over, blocks = slots_ref.shape
    slots = matrix_ref.shape[1]
    per = x_ref.shape[0]
    levels = x_ref.shape[1] // rows
    row = lax.broadcasted_iota(jnp.int32, (slots, blocks), 0)
    mat = jnp.zeros((slots, blocks), jnp.float32)
    for k in range(over):
        mat = mat + jnp.where(slots_ref[k : k + 1, :] == row, weights_ref[k : k + 1, :], 0.0)
    b0 = lax.broadcasted_iota(jnp.int32, (blocks, blocks), 0)
    b1 = lax.broadcasted_iota(jnp.int32, (blocks, blocks), 1)
    order = jnp.where(lax.rem(b0, rows) * per + lax.div(b0, rows) == b1, 1.0, 0.0)
    matrix_ref[...] = jnp.dot(order, mat.T, precision=lax.Precision.HIGHEST)

    ocean = lax.axis_index("comp") == 0
    even = lax.rem(lax.axis_index("tile"), 2) == 0
    vmix = vmix_ref[...]
    d0 = lax.broadcasted_iota(jnp.int32, (levels, levels), 0)
    d1 = lax.broadcasted_iota(jnp.int32, (levels, levels), 1)
    for l in range(levels):
        column = jnp.sum(jnp.where(d0 == d1, vmix[l : l + 1, :], 0.0), axis=1, keepdims=True)
        table_ref[l * levels : (l + 1) * levels, :] = jnp.broadcast_to(column, (levels, LANES))
    pays = []
    for edge, inner in ((0, 1), (rows - 1, rows - 2)):
        xs = [x_ref[c, pl.ds(edge, levels, stride=rows), :] for c in range(per)]
        left, right = shifted(xs, True), shifted(xs, False)
        pay = []
        for c in range(per):
            s = slice(c * LANES, (c + 1) * LANES)
            x = xs[c]
            xi = x_ref[c, pl.ds(inner, levels, stride=rows), :]
            k = kappa_ref[edge : edge + 1, s]
            m = jnp.where(ocean, mask_ref[edge : edge + 1, s].astype(jnp.float32), 1.0)
            acc = x + k * (xi + left[c] + right[c] - 4.0 * x)
            for q in range(levels):
                acc = acc + vmix[:, q : q + 1] * x[q : q + 1, :]
            pay.append((m * acc, x, m * k))
        pays.append(pay)
    for ref, flag in ((p1_ref, even), (p2_ref, jnp.logical_not(even))):
        for c in range(per):
            a, x, b = [jnp.where(flag, v, u) for u, v in zip(pays[0][c], pays[1][c])]
            ref[c * levels : (c + 1) * levels, :] = a
            ref[(per + c) * levels : (per + c + 1) * levels, :] = x
            ref[2 * per * levels + c : 2 * per * levels + c + 1, :] = b


def regrid_kernel(rows, buf_ref, matrix_ref, mask_ref, f_ref, e1_ref, e2_ref):
    slots = matrix_ref.shape[1]
    per = f_ref.shape[0]
    cap = buf_ref.shape[1] // FLUX
    wide = jnp.concatenate(
        [buf_ref[:, f * cap : (f + 1) * cap, :].reshape(slots, LANES) for f in range(FLUX)], axis=1
    )
    bh, bl = split(wide)
    wh, wl = split(matrix_ref[...])
    dot = functools.partial(jnp.dot, preferred_element_type=jnp.float32)
    out = dot(wh, bh) + (dot(wh, bl) + dot(wl, bh))
    for f in range(FLUX):
        for c in range(per):
            f_ref[c, f * rows : (f + 1) * rows, :] = out[
                c * rows : (c + 1) * rows, f * LANES : (f + 1) * LANES
            ]
    ocean = lax.axis_index("comp") != 0
    even = lax.rem(lax.axis_index("tile"), 2) == 0
    for c in range(per):
        s = slice(c * LANES, (c + 1) * LANES)
        edges = []
        for edge in (0, rows - 1):
            m = jnp.where(ocean, mask_ref[edge : edge + 1, s].astype(jnp.float32), 1.0)
            edges.append(m * f_ref[c, pl.ds(edge, FLUX, stride=rows), :])
        e1_ref[c * FLUX : (c + 1) * FLUX, :] = jnp.where(even, edges[1], edges[0])
        e2_ref[c * FLUX : (c + 1) * FLUX, :] = jnp.where(even, edges[0], edges[1])


def stencil(xs, kappa_ref, rows, prev, nxt, row):
    left, right = shifted(xs, True), shifted(xs, False)
    out = []
    for c, x in enumerate(xs):
        up = jnp.where(row == 0, prev(c), pltpu.roll(x, 1, 0))
        down = jnp.where(row == rows - 1, nxt(c), pltpu.roll(x, rows - 1, 0))
        k = kappa_ref[:, c * LANES : (c + 1) * LANES]
        out.append(k * (up + down + left[c] + right[c] - 4.0 * x))
    return out


def still_kernel(
    rows, x0_ref, h1_ref, h2_ref, kappa_ref, mask_ref, table_ref, x_ref, x1_ref, halo_ref
):
    per = x0_ref.shape[0]
    levels = x0_ref.shape[1] // rows
    ocean = lax.axis_index("comp") == 0
    even = lax.rem(lax.axis_index("tile"), 2) == 0
    for side in range(2):
        flag = even if side == 1 else jnp.logical_not(even)

        def take(lo, n):
            return jnp.where(flag, h1_ref[lo : lo + n, :], h2_ref[lo : lo + n, :])

        for c in range(per):
            edge = x0_ref[c, pl.ds(side * (rows - 1), levels, stride=rows), :]
            a = take(c * levels, levels)
            b = take(2 * per * levels + c, 1)
            halo_ref[side, c] = take((per + c) * levels, levels)
            halo_ref[2 + side, c] = a + b * edge
    row = lax.broadcasted_iota(jnp.int32, (rows, LANES), 0)

    def advance(src, dst, base):
        for l in range(levels):
            part = slice(l * rows, (l + 1) * rows)
            xs = [src[c, part, :] for c in range(per)]
            moved = stencil(
                xs, kappa_ref, rows,
                lambda c: halo_ref[base, c, l : l + 1, :],
                lambda c: halo_ref[base + 1, c, l : l + 1, :],
                row,
            )
            for c in range(per):
                acc = xs[c] + moved[c]
                for q in range(levels):
                    v = table_ref[l * levels + q : l * levels + q + 1, :]
                    acc = acc + v * src[c, q * rows : (q + 1) * rows, :]
                s = slice(c * LANES, (c + 1) * LANES)
                mask = jnp.where(ocean, mask_ref[:, s].astype(jnp.float32), 1.0)
                dst[c, part, :] = mask * acc

    advance(x0_ref, x1_ref, 0)
    advance(x1_ref, x_ref, 2)


def step_kernel(
    rows, still_ref, f_ref, e1_ref, e2_ref, kappa_ref, mask_ref, table_ref, basis_ref, gram_ref,
    x_ref, sums_ref, f1_ref,
):
    per = still_ref.shape[0]
    levels = still_ref.shape[1] // rows
    vecs = basis_ref.shape[0]
    ocean = lax.axis_index("comp") == 0
    even = lax.rem(lax.axis_index("tile"), 2) == 0
    row = lax.broadcasted_iota(jnp.int32, (rows, LANES), 0)

    def mask(c):
        m = mask_ref[:, c * LANES : (c + 1) * LANES].astype(jnp.float32)
        return jnp.where(ocean, m, 1.0)

    for c in range(per):
        m = mask(c)
        for f in range(FLUX):
            part = slice(f * rows, (f + 1) * rows)
            f1_ref[c, part, :] = m * f_ref[c, part, :]
    for l in range(levels):
        part = slice(l * rows, (l + 1) * rows)
        if l < FLUX:
            fs = [f1_ref[c, part, :] for c in range(per)]

            def edge(c, flag):
                i = slice(c * FLUX + l, c * FLUX + l + 1)
                return jnp.where(flag, e1_ref[i, :], e2_ref[i, :])

            moved = stencil(
                fs, kappa_ref, rows,
                lambda c: edge(c, jnp.logical_not(even)), lambda c: edge(c, even), row,
            )
        for c in range(per):
            acc = fs[c] + moved[c] + f_ref[c, part, :] if l < FLUX else 0.0
            for q in range(FLUX):
                v = table_ref[l * levels + q : l * levels + q + 1, :]
                acc = acc + v * f1_ref[c, q * rows : (q + 1) * rows, :]
            x_ref[c, part, :] = still_ref[c, part, :] + mask(c) * acc

    def level(l, accs):
        accs = list(accs)
        for c in range(per):
            s = slice(c * LANES, (c + 1) * LANES)
            x = x_ref[c, pl.ds(l * rows, rows), :]
            for i in range(vecs):
                t = x * basis_ref[i, l, :, s].astype(jnp.float32)
                accs[i] = accs[i] + t.reshape(rows // 8, 8, LANES).sum(0)
            accs[vecs] = accs[vecs] + (x * x).reshape(rows // 8, 8, LANES).sum(0)
        return tuple(accs)

    zero = jnp.zeros((8, LANES), jnp.float32)
    accs = lax.fori_loop(0, levels, level, (zero,) * (vecs + 1))
    lane = lax.broadcasted_iota(jnp.int32, (1, LANES), 1)
    line = jnp.zeros((1, LANES), jnp.float32)
    for i in range(vecs + 1):
        tot = jnp.sum(jnp.sum(accs[i], axis=0, keepdims=True), axis=1, keepdims=True)
        line = line + jnp.where(lane == 64 + i, tot, 0.0)
    block = gram_ref[...] + jnp.concatenate([jnp.zeros((1, LANES), jnp.float32), line], axis=0)
    for d in range(sums_ref.shape[0]):
        sums_ref[d] = block


def finish_kernel(rows, total, x_ref, basis_ref, sums_ref, out_ref, coef_ref):
    per = x_ref.shape[0]
    levels = x_ref.shape[1] // rows
    vecs = basis_ref.shape[0]
    sums = jnp.sum(sums_ref[...], axis=0)
    lane = lax.broadcasted_iota(jnp.int32, (1, LANES), 1)
    tail = pltpu.roll(sums[1:2, :], 64, 1)
    coef = jnp.where(lane < vecs, tail, 0.0) / total
    coef_ref[...] = coef[:, :vecs]
    square = jnp.sum(jnp.where(lane == vecs, tail, 0.0), axis=1, keepdims=True)
    splat = [jnp.sum(jnp.where(lane == i, coef, 0.0), axis=1, keepdims=True) for i in range(vecs)]
    quad = jnp.zeros((1, LANES), jnp.float32)
    for i in range(vecs):
        shift = (LANES - 16 * (i % 8)) % LANES
        line = sums[i // 8 : i // 8 + 1, :]
        line = pltpu.roll(line, shift, 1) if shift else line
        quad = quad + splat[i] * jnp.where(lane < vecs, line, 0.0)
    extra = jnp.sum(coef * (quad - 2.0 * total * coef), axis=1, keepdims=True)
    scale = 1.0 / jnp.sqrt((square + extra) / total + 1e-06)
    wide = [jnp.broadcast_to(scale * s, (8, LANES)) for s in splat]
    scale = jnp.broadcast_to(scale, (8, LANES))

    def level(l, carry):
        for c in range(per):
            s = slice(c * LANES, (c + 1) * LANES)
            x = x_ref[c, pl.ds(l * rows, rows), :].reshape(rows // 8, 8, LANES) * scale
            for i in range(vecs):
                b = basis_ref[i, l, :, s].astype(jnp.float32).reshape(rows // 8, 8, LANES)
                x = x - wide[i] * b
            out_ref[pl.ds(l * rows, rows), s] = x.reshape(rows, LANES)
        return carry

    lax.fori_loop(0, levels, level, 0)


def body(state, basis, kappa, vmix, land_mask, send_rows, recv_slots, recv_weights):
    _, levels, rows, cols = state.shape
    vecs = basis.shape[0]
    bands, cap = send_rows.shape[2:]
    blocks, _ = recv_slots.shape[2:]
    per = cols // LANES
    comps = lax.axis_size("comp")
    devices = comps * bands
    total = float(levels * rows * cols * devices)
    f32 = jnp.float32
    flat = state.reshape(levels * rows, cols)
    vectors = basis[:, 0]
    kap, vm = kappa[0], vmix[0]

    field = jax.ShapeDtypeStruct((per, levels * rows, LANES), f32)
    import_field = jax.ShapeDtypeStruct((per, FLUX * rows, LANES), f32)
    pay = jax.ShapeDtypeStruct((2 * levels * per + per, LANES), f32)
    fringe = jax.ShapeDtypeStruct((per * FLUX, LANES), f32)
    pairs1 = [(i, i ^ 1) for i in range(bands)]
    pairs2 = [p for i in range(1, bands - 1, 2) for p in ((i, i + 1), (i + 1, i))]
    swap = [(i, i ^ 1) for i in range(comps)]

    def crossed(pairs):
        return [((c * bands) + i, (c ^ 1) * bands + k) for c in range(comps) for i, k in pairs]

    sides = (kap, land_mask, recv_slots[0, 0].T, recv_weights[0, 0].T, vm)
    bucket, columns, kap, land_mask, slots, weights, vm = call(
        functools.partial(gather_kernel, rows),
        (jax.ShapeDtypeStruct((bands * FLUX * cap, LANES), f32), field)
        + tuple(jax.ShapeDtypeStruct(a.shape, a.dtype) for a in sides),
        [HBM] * (2 + len(sides)),
        (VMEM,) * (2 + len(sides)),
        scratch=(
            pltpu.SMEM((cap, bands), jnp.int32),
            pltpu.SemaphoreType.DMA((2 * per + 1 + len(sides),)),
        ),
    )(*[in_hbm(a) for a in (send_rows[0, 0].T, flat) + sides])
    moved = lax.all_to_all(bucket.reshape(bands, FLUX * cap, LANES), "tile", 0, 0)
    matrix, pay1, pay2, table = call(
        functools.partial(early_kernel, rows),
        (
            jax.ShapeDtypeStruct((blocks, bands * cap), f32),
            pay,
            pay,
            jax.ShapeDtypeStruct((levels * levels, LANES), f32),
        ),
        [VMEM] * 6,
        (VMEM,) * 4,
    )(slots, weights, columns, kap, land_mask, vm)
    matrix = lax.ppermute(matrix, "comp", swap)
    got1 = lax.ppermute(pay1, "tile", pairs1)
    got2 = lax.ppermute(pay2, "tile", pairs2)
    still = call(
        functools.partial(still_kernel, rows),
        field,
        [VMEM] * 6,
        VMEM,
        scratch=(
            pltpu.VMEM((per, levels * rows, LANES), f32),
            pltpu.VMEM((4, per, levels, LANES), f32),
        ),
    )(columns, got1, got2, kap, land_mask, table)
    foreign, edge1, edge2 = call(
        functools.partial(regrid_kernel, rows),
        (import_field, fringe, fringe),
        [VMEM] * 3,
        (VMEM,) * 3,
    )(moved, matrix, land_mask)
    vectors, gram = call(
        gram_kernel,
        (jax.ShapeDtypeStruct(vectors.shape, vectors.dtype), jax.ShapeDtypeStruct((2, LANES), f32)),
        [pl.BlockSpec(memory_space=pl.ANY), HBM],
        (VMEM, VMEM),
        scratch=(pltpu.SemaphoreType.DMA((levels,)),),
    )(edge1, in_hbm(vectors))
    imported = lax.ppermute(foreign, "comp", swap)
    edge1 = lax.ppermute(edge1, ("comp", "tile"), crossed(pairs1))
    edge2 = lax.ppermute(edge2, ("comp", "tile"), crossed(pairs2))
    x, sums = call(
        functools.partial(step_kernel, rows),
        (field, jax.ShapeDtypeStruct((devices, 2, LANES), f32)),
        [VMEM] * 9,
        (VMEM, VMEM),
        scratch=(pltpu.VMEM((per, FLUX * rows, LANES), f32),),
    )(still, imported, edge1, edge2, kap, land_mask, table, vectors, gram)
    sums = lax.all_to_all(sums, ("comp", "tile"), 0, 0)
    direction, coefs = call(
        functools.partial(finish_kernel, rows, total),
        (
            jax.ShapeDtypeStruct((levels * rows, cols), f32),
            jax.ShapeDtypeStruct((1, vecs), f32),
        ),
        [VMEM] * 3,
        (VMEM, VMEM),
    )(x, vectors, sums)
    return direction.reshape(1, levels, rows, cols), coefs.reshape(vecs)


def solution(mesh):
    return jax.shard_map(
        body,
        mesh=mesh,
        in_specs=(
            P("comp", None, "tile", None),
            P(None, "comp", None, "tile", None),
            P("comp", "tile", None),
            P("comp", None, None),
            P("tile", None),
            P("comp", "tile", None, None),
            P("comp", "tile", None, None),
            P("comp", "tile", None, None),
        ),
        out_specs=(P("comp", None, "tile", None), P()),
        check_vma=False,
    )
```

```python
import functools

import jax
import jax.numpy as jnp
from jax import lax
from jax.experimental import pallas as pl
from jax.experimental.pallas import tpu as pltpu
from jax.sharding import PartitionSpec as P


FLUX = 4
LANES = 128
HBM = pl.BlockSpec(memory_space=pltpu.HBM)
VMEM = pl.BlockSpec(memory_space=pltpu.VMEM)
LIMIT = 24 << 20


def call(kernel, outs, in_specs, out_specs, scratch=(), cost=None):
    return pl.pallas_call(
        kernel,
        out_shape=outs,
        in_specs=in_specs,
        out_specs=out_specs,
        scratch_shapes=list(scratch),
        cost_estimate=cost,
        compiler_params=pltpu.CompilerParams(vmem_limit_bytes=LIMIT),
    )


def in_hbm(a):
    return pltpu.with_memory_space_constraint(a, pltpu.HBM)


def split(a):
    high = a.astype(jnp.bfloat16)
    return high, (a - high.astype(jnp.float32)).astype(jnp.bfloat16)


def payload_rows(levels, per):
    return 2 * levels * per + per


def block_place(b, per):
    if per & (per - 1) == 0:
        bits = per.bit_length() - 1
        return lax.shift_right_logical(b, bits), lax.bitwise_and(b, per - 1)
    return lax.div(b, per), lax.rem(b, per)


def gather_kernel(rows, index_ref, state_ref, *refs):
    small = (len(refs) - 4) // 2
    sides, out_ref, x_ref = refs[:small], refs[small], refs[small + 1]
    side_outs, (rows_ref, sems) = refs[small + 2 : 2 * small + 2], refs[2 * small + 2 :]
    cap, bands = rows_ref.shape
    per = x_ref.shape[0]
    top = FLUX * rows
    index = pltpu.make_async_copy(index_ref, rows_ref, sems.at[2 * per])
    index.start()
    copies = []
    for part, (lo, hi) in enumerate(((0, top), (top, x_ref.shape[1]))):
        for c in range(per):
            copies.append(
                pltpu.make_async_copy(
                    state_ref.at[lo:hi, c * LANES : (c + 1) * LANES],
                    x_ref.at[c, lo:hi, :],
                    sems.at[part * per + c],
                )
            )
    for k, (src, dst) in enumerate(zip(sides, side_outs)):
        copies.append(pltpu.make_async_copy(src, dst, sems.at[2 * per + 1 + k]))
    for copy in copies:
        copy.start()
    index.wait()
    for copy in copies[:per]:
        copy.wait()

    def band(d, carry):
        for j in range(cap):
            r, c = block_place(rows_ref[j, d], per)
            piece = x_ref[c, pl.ds(r, FLUX, stride=rows), :]
            out_ref[pl.ds(d * (cap * FLUX) + j, FLUX, stride=cap), :] = piece
        return carry

    lax.fori_loop(0, bands, band, 0, unroll=2)
    for copy in copies[per:]:
        copy.wait()


def fetch_kernel(after_ref, basis_hbm, basis_ref, sems):
    copies = [
        pltpu.make_async_copy(basis_hbm.at[i], basis_ref.at[i], sems.at[i])
        for i in range(basis_ref.shape[0])
    ]
    for copy in copies:
        copy.start()
    for copy in copies:
        copy.wait()


def gram_kernel(basis_hbm, gram_ref, basis_ref, sems):
    vecs, levels, rows, cols = basis_ref.shape
    copies = [
        pltpu.make_async_copy(basis_hbm.at[:, l], basis_ref.at[:, l], sems.at[l])
        for l in range(levels)
    ]
    for copy in copies:
        copy.start()
    n = vecs * rows
    total = jnp.zeros((n, n), jnp.float32)
    for l in range(levels):
        copies[l].wait()
        a = basis_ref[:, l].reshape(n, cols)
        total = total + lax.dot_general(
            a, a, (((1,), (1,)), ((), ())), preferred_element_type=jnp.float32
        )
    i0 = lax.broadcasted_iota(jnp.int32, (n, n), 0)
    i1 = lax.broadcasted_iota(jnp.int32, (n, n), 1)
    total = jnp.where(lax.rem(i0, rows) == lax.rem(i1, rows), total, 0.0)
    part = jnp.sum(total.reshape(vecs, rows, n), axis=1)
    j0 = lax.broadcasted_iota(jnp.int32, (n, LANES), 0)
    j1 = lax.broadcasted_iota(jnp.int32, (n, LANES), 1)
    fold = jnp.where(lax.div(j0, rows) == j1, 1.0, 0.0)
    gram = jnp.dot(part, fold, precision=lax.Precision.HIGHEST)
    packed = [jnp.zeros((1, LANES), jnp.float32), jnp.zeros((1, LANES), jnp.float32)]
    for i in range(vecs):
        shift = 16 * (i % 8)
        line = gram[i : i + 1, :]
        packed[i // 8] = packed[i // 8] + (pltpu.roll(line, shift, 1) if shift else line)
    gram_ref[...] = jnp.concatenate(packed, axis=0)


def shifted(parts, up):
    n = len(parts)
    lane = lax.broadcasted_iota(jnp.int32, parts[0].shape, 1)
    rolled = [pltpu.roll(p, 1 if up else LANES - 1, 1) for p in parts]
    edge = 0 if up else LANES - 1
    step = -1 if up else 1
    return [jnp.where(lane == edge, rolled[(c + step) % n], rolled[c]) for c in range(n)]


def early_kernel(
    rows, slots_ref, weights_ref, x_ref, kappa_ref, mask_ref, vmix_ref,
    pack_ref, table_ref,
):
    over, blocks = slots_ref.shape
    per = x_ref.shape[0]
    levels = x_ref.shape[1] // rows
    size = payload_rows(levels, per)
    slots = (pack_ref.shape[0] - 2 * size) // blocks * LANES
    row = lax.broadcasted_iota(jnp.int32, (slots, blocks), 0)
    mat = jnp.zeros((slots, blocks), jnp.float32)
    for k in range(over):
        mat = mat + jnp.where(slots_ref[k : k + 1, :] == row, weights_ref[k : k + 1, :], 0.0)
    b0 = lax.broadcasted_iota(jnp.int32, (blocks, blocks), 0)
    b1 = lax.broadcasted_iota(jnp.int32, (blocks, blocks), 1)
    order = jnp.where(lax.rem(b0, rows) * per + lax.div(b0, rows) == b1, 1.0, 0.0)
    mat = jnp.dot(order, mat.T, precision=lax.Precision.HIGHEST)
    for p in range(slots // LANES):
        pack_ref[p * blocks : (p + 1) * blocks, :] = mat[:, p * LANES : (p + 1) * LANES]

    ocean = lax.axis_index("comp") == 0
    even = lax.rem(lax.axis_index("tile"), 2) == 0
    vmix = vmix_ref[...]
    d0 = lax.broadcasted_iota(jnp.int32, (levels, levels), 0)
    d1 = lax.broadcasted_iota(jnp.int32, (levels, levels), 1)
    for l in range(levels):
        column = jnp.sum(jnp.where(d0 == d1, vmix[l : l + 1, :], 0.0), axis=1, keepdims=True)
        table_ref[l * levels : (l + 1) * levels, :] = jnp.broadcast_to(column, (levels, LANES))
    pays = []
    for edge, inner in ((0, 1), (rows - 1, rows - 2)):
        xs = [x_ref[c, pl.ds(edge, levels, stride=rows), :] for c in range(per)]
        left, right = shifted(xs, True), shifted(xs, False)
        pay = []
        for c in range(per):
            s = slice(c * LANES, (c + 1) * LANES)
            x = xs[c]
            xi = x_ref[c, pl.ds(inner, levels, stride=rows), :]
            k = kappa_ref[edge : edge + 1, s]
            m = jnp.where(ocean, mask_ref[edge : edge + 1, s].astype(jnp.float32), 1.0)
            acc = x + k * (xi + left[c] + right[c] - 4.0 * x)
            for q in range(levels):
                acc = acc + vmix[:, q : q + 1] * x[q : q + 1, :]
            pay.append((m * acc, x, m * k))
        pays.append(pay)
    base = slots // LANES * blocks
    for n, flag in ((0, even), (1, jnp.logical_not(even))):
        ref = pack_ref.at[base + n * size : base + (n + 1) * size, :]
        for c in range(per):
            a, x, b = [jnp.where(flag, v, u) for u, v in zip(pays[0][c], pays[1][c])]
            ref[c * levels : (c + 1) * levels, :] = a
            ref[(per + c) * levels : (per + c + 1) * levels, :] = x
            ref[2 * per * levels + c : 2 * per * levels + c + 1, :] = b


def regrid_kernel(rows, levels, buf_ref, pack_ref, mask_ref, f_ref, e1_ref, e2_ref):
    per = f_ref.shape[0]
    cap = buf_ref.shape[1] // FLUX
    slots = buf_ref.shape[0] * cap
    blocks = rows * per
    size = payload_rows(levels, per)
    wide = jnp.concatenate(
        [buf_ref[:, f * cap : (f + 1) * cap, :].reshape(slots, LANES) for f in range(FLUX)], axis=1
    )
    bh, bl = split(wide)
    pieces = [pack_ref[p * blocks : (p + 1) * blocks, :] for p in range(slots // LANES)]
    wh, wl = split(jnp.concatenate(pieces, axis=1))
    dot = functools.partial(jnp.dot, preferred_element_type=jnp.float32)
    out = dot(wh, bh) + (dot(wh, bl) + dot(wl, bh))
    for f in range(FLUX):
        for c in range(per):
            f_ref[c, f * rows : (f + 1) * rows, :] = out[
                c * rows : (c + 1) * rows, f * LANES : (f + 1) * LANES
            ]
    ocean = lax.axis_index("comp") != 0
    even = lax.rem(lax.axis_index("tile"), 2) == 0
    base = slots // LANES * blocks
    for n, ref in enumerate((e1_ref, e2_ref)):
        ref[per * levels :, :] = pack_ref[base + n * size + per * levels : base + (n + 1) * size, :]
    for c in range(per):
        s = slice(c * LANES, (c + 1) * LANES)
        edges = []
        for edge in (0, rows - 1):
            m = jnp.where(ocean, mask_ref[edge : edge + 1, s].astype(jnp.float32), 1.0)
            forced = m * f_ref[c, pl.ds(edge, FLUX, stride=rows), :]
            still = jnp.zeros((levels - FLUX, LANES), jnp.float32)
            edges.append(jnp.concatenate([forced, still], axis=0))
        for n, (ref, forced) in enumerate(
            ((e1_ref, jnp.where(even, edges[1], edges[0])), (e2_ref, jnp.where(even, edges[0], edges[1])))
        ):
            at = base + n * size + c * levels
            ref[c * levels : (c + 1) * levels, :] = pack_ref[at : at + levels, :] + forced


def stencil(xs, kappa_ref, rows):
    left, right = shifted(xs, True), shifted(xs, False)
    row = lax.broadcasted_iota(jnp.int32, (rows, LANES), 0)
    out = []
    for c, x in enumerate(xs):
        up = jnp.where(row == 0, 0.0, pltpu.roll(x, 1, 0))
        down = jnp.where(row == rows - 1, 0.0, pltpu.roll(x, rows - 1, 0))
        k = kappa_ref[:, c * LANES : (c + 1) * LANES]
        out.append(k * (up + down + left[c] + right[c] - 4.0 * x))
    return out


def still_kernel(rows, x0_ref, kappa_ref, mask_ref, table_ref, x_ref, x1_ref):
    per = x0_ref.shape[0]
    levels = x0_ref.shape[1] // rows
    ocean = lax.axis_index("comp") == 0

    def advance(src, dst):
        for l in range(levels):
            part = slice(l * rows, (l + 1) * rows)
            xs = [src[c, part, :] for c in range(per)]
            moved = stencil(xs, kappa_ref, rows)
            for c in range(per):
                acc = xs[c] + moved[c]
                for q in range(levels):
                    v = table_ref[l * levels + q : l * levels + q + 1, :]
                    acc = acc + v * src[c, q * rows : (q + 1) * rows, :]
                s = slice(c * LANES, (c + 1) * LANES)
                mask = jnp.where(ocean, mask_ref[:, s].astype(jnp.float32), 1.0)
                dst[c, part, :] = mask * acc

    advance(x0_ref, x1_ref)
    advance(x1_ref, x_ref)


def step_kernel(
    rows, still_ref, x0_ref, f_ref, h1_ref, h2_ref, kappa_ref, mask_ref, vmix_ref, table_ref,
    basis_ref, gram_ref, x_ref, sums_ref, f1_ref,
):
    per = still_ref.shape[0]
    levels = still_ref.shape[1] // rows
    vecs = basis_ref.shape[0]
    ocean = lax.axis_index("comp") == 0
    even = lax.rem(lax.axis_index("tile"), 2) == 0

    def mask(c, part=slice(None)):
        m = mask_ref[part, c * LANES : (c + 1) * LANES].astype(jnp.float32)
        return jnp.where(ocean, m, 1.0)

    for c in range(per):
        m = mask(c)
        for f in range(FLUX):
            part = slice(f * rows, (f + 1) * rows)
            f1_ref[c, part, :] = m * f_ref[c, part, :]
    for l in range(levels):
        part = slice(l * rows, (l + 1) * rows)
        if l < FLUX:
            fs = [f1_ref[c, part, :] for c in range(per)]
            moved = stencil(fs, kappa_ref, rows)
        for c in range(per):
            acc = fs[c] + moved[c] + f_ref[c, part, :] if l < FLUX else 0.0
            for q in range(FLUX):
                v = table_ref[l * levels + q : l * levels + q + 1, :]
                acc = acc + v * f1_ref[c, q * rows : (q + 1) * rows, :]
            x_ref[c, part, :] = still_ref[c, part, :] + mask(c) * acc

    vmix = vmix_ref[...]
    for side, edge, inner in ((0, 0, 1), (1, rows - 1, rows - 2)):
        flag = even if side == 1 else jnp.logical_not(even)

        def take(lo, n):
            return jnp.where(flag, h1_ref[lo : lo + n, :], h2_ref[lo : lo + n, :])

        def factor(c, r):
            r = slice(r, r + 1)
            return mask(c, r), mask(c, r) * kappa_ref[r, c * LANES : (c + 1) * LANES]

        ds = [factor(c, edge)[1] * take((per + c) * levels, levels) for c in range(per)]
        left, right = shifted(ds, True), shifted(ds, False)
        for c in range(per):
            d = ds[c]
            own = x0_ref[c, pl.ds(edge, levels, stride=rows), :]
            foreign = take(c * levels, levels) + take(2 * per * levels + c, 1) * own
            m, mk = factor(c, edge)
            mixed = d
            for q in range(levels):
                mixed = mixed + vmix[:, q : q + 1] * d[q : q + 1, :]
            at = pl.ds(edge, levels, stride=rows)
            change = m * mixed + mk * (left[c] + right[c] - 4.0 * d + foreign)
            x_ref[c, at, :] = x_ref[c, at, :] + change
            at = pl.ds(inner, levels, stride=rows)
            x_ref[c, at, :] = x_ref[c, at, :] + factor(c, inner)[1] * d

    def level(l, accs):
        accs = list(accs)
        for c in range(per):
            s = slice(c * LANES, (c + 1) * LANES)
            x = x_ref[c, pl.ds(l * rows, rows), :]
            for i in range(vecs):
                t = x * basis_ref[i, l, :, s].astype(jnp.float32)
                accs[i] = accs[i] + t.reshape(rows // 8, 8, LANES).sum(0)
            accs[vecs] = accs[vecs] + (x * x).reshape(rows // 8, 8, LANES).sum(0)
        return tuple(accs)

    zero = jnp.zeros((8, LANES), jnp.float32)
    accs = lax.fori_loop(0, levels, level, (zero,) * (vecs + 1))
    lane = lax.broadcasted_iota(jnp.int32, (1, LANES), 1)
    line = jnp.zeros((1, LANES), jnp.float32)
    for i in range(vecs + 1):
        tot = jnp.sum(jnp.sum(accs[i], axis=0, keepdims=True), axis=1, keepdims=True)
        line = line + jnp.where(lane == 64 + i, tot, 0.0)
    block = gram_ref[...] + jnp.concatenate([jnp.zeros((1, LANES), jnp.float32), line], axis=0)
    for d in range(sums_ref.shape[0]):
        sums_ref[d] = block


def finish_kernel(rows, total, x_ref, basis_ref, sums_ref, out_ref, coef_ref):
    per = x_ref.shape[0]
    levels = x_ref.shape[1] // rows
    vecs = basis_ref.shape[0]
    sums = jnp.sum(sums_ref[...], axis=0)
    lane = lax.broadcasted_iota(jnp.int32, (1, LANES), 1)
    tail = pltpu.roll(sums[1:2, :], 64, 1)
    coef = jnp.where(lane < vecs, tail, 0.0) / total
    coef_ref[...] = coef[:, :vecs]
    square = jnp.sum(jnp.where(lane == vecs, tail, 0.0), axis=1, keepdims=True)
    splat = [jnp.sum(jnp.where(lane == i, coef, 0.0), axis=1, keepdims=True) for i in range(vecs)]
    quad = jnp.zeros((1, LANES), jnp.float32)
    for i in range(vecs):
        shift = (LANES - 16 * (i % 8)) % LANES
        line = sums[i // 8 : i // 8 + 1, :]
        line = pltpu.roll(line, shift, 1) if shift else line
        quad = quad + splat[i] * jnp.where(lane < vecs, line, 0.0)
    extra = jnp.sum(coef * (quad - 2.0 * total * coef), axis=1, keepdims=True)
    scale = 1.0 / jnp.sqrt((square + extra) / total + 1e-06)
    wide = [jnp.broadcast_to(scale * s, (8, LANES)) for s in splat]
    scale = jnp.broadcast_to(scale, (8, LANES))

    def level(l, carry):
        for c in range(per):
            s = slice(c * LANES, (c + 1) * LANES)
            x = x_ref[c, pl.ds(l * rows, rows), :].reshape(rows // 8, 8, LANES) * scale
            for i in range(vecs):
                b = basis_ref[i, l, :, s].astype(jnp.float32).reshape(rows // 8, 8, LANES)
                x = x - wide[i] * b
            out_ref[pl.ds(l * rows, rows), s] = x.reshape(rows, LANES)
        return carry

    lax.fori_loop(0, levels, level, 0)


def body(state, basis, kappa, vmix, land_mask, send_rows, recv_slots, recv_weights):
    _, levels, rows, cols = state.shape
    vecs = basis.shape[0]
    bands, cap = send_rows.shape[2:]
    blocks, _ = recv_slots.shape[2:]
    per = cols // LANES
    comps = lax.axis_size("comp")
    devices = comps * bands
    total = float(levels * rows * cols * devices)
    f32 = jnp.float32
    flat = state.reshape(levels * rows, cols)
    vectors = basis[:, 0]
    kap, vm = kappa[0], vmix[0]

    field = jax.ShapeDtypeStruct((per, levels * rows, LANES), f32)
    import_field = jax.ShapeDtypeStruct((per, FLUX * rows, LANES), f32)
    pay = jax.ShapeDtypeStruct((payload_rows(levels, per), LANES), f32)
    pairs1 = [(i, i ^ 1) for i in range(bands)]
    pairs2 = [p for i in range(1, bands - 1, 2) for p in ((i, i + 1), (i + 1, i))]
    swap = [(i, i ^ 1) for i in range(comps)]

    def crossed(pairs):
        return [((c * bands) + i, (c ^ 1) * bands + k) for c in range(comps) for i, k in pairs]

    sides = (kap, land_mask, recv_slots[0, 0].T, recv_weights[0, 0].T, vm)
    bucket, columns, kap, land_mask, slots, weights, vm = call(
        functools.partial(gather_kernel, rows),
        (jax.ShapeDtypeStruct((bands * FLUX * cap, LANES), f32), field)
        + tuple(jax.ShapeDtypeStruct(a.shape, a.dtype) for a in sides),
        [HBM] * (2 + len(sides)),
        (VMEM,) * (2 + len(sides)),
        scratch=(
            pltpu.SMEM((cap, bands), jnp.int32),
            pltpu.SemaphoreType.DMA((2 * per + 1 + len(sides),)),
        ),
    )(*[in_hbm(a) for a in (send_rows[0, 0].T, flat) + sides])
    moved = lax.all_to_all(bucket.reshape(bands, FLUX * cap, LANES), "tile", 0, 0)
    pack, table = call(
        functools.partial(early_kernel, rows),
        (
            jax.ShapeDtypeStruct((bands * cap // LANES * blocks + 2 * pay.shape[0], LANES), f32),
            jax.ShapeDtypeStruct((levels * levels, LANES), f32),
        ),
        [VMEM] * 6,
        (VMEM,) * 2,
    )(slots, weights, columns, kap, land_mask, vm)
    pack = lax.ppermute(pack, "comp", swap)
    gram = call(
        gram_kernel,
        jax.ShapeDtypeStruct((2, LANES), f32),
        [HBM],
        VMEM,
        scratch=(
            pltpu.VMEM(vectors.shape, vectors.dtype),
            pltpu.SemaphoreType.DMA((levels,)),
        ),
    )(in_hbm(vectors))
    still = call(
        functools.partial(still_kernel, rows),
        field,
        [VMEM] * 4,
        VMEM,
        scratch=(pltpu.VMEM((per, levels * rows, LANES), f32),),
    )(columns, kap, land_mask, table)

    foreign, edge1, edge2 = call(
        functools.partial(regrid_kernel, rows, levels),
        (import_field, pay, pay),
        [VMEM] * 3,
        (VMEM,) * 3,
    )(moved, pack, land_mask)
    vectors = call(
        fetch_kernel,
        jax.ShapeDtypeStruct(vectors.shape, vectors.dtype),
        [pl.BlockSpec(memory_space=pl.ANY), HBM],
        VMEM,
        scratch=(pltpu.SemaphoreType.DMA((vecs,)),),
    )(edge1, in_hbm(vectors))
    imported = lax.ppermute(foreign, "comp", swap)
    edge1 = lax.ppermute(edge1, ("comp", "tile"), crossed(pairs1))
    edge2 = lax.ppermute(edge2, ("comp", "tile"), crossed(pairs2))
    x, sums = call(
        functools.partial(step_kernel, rows),
        (field, jax.ShapeDtypeStruct((devices, 2, LANES), f32)),
        [VMEM] * 11,
        (VMEM, VMEM),
        scratch=(pltpu.VMEM((per, FLUX * rows, LANES), f32),),
    )(still, columns, imported, edge1, edge2, kap, land_mask, vm, table, vectors, gram)
    sums = lax.all_to_all(sums, ("comp", "tile"), 0, 0)
    direction, coefs = call(
        functools.partial(finish_kernel, rows, total),
        (
            jax.ShapeDtypeStruct((levels * rows, cols), f32),
            jax.ShapeDtypeStruct((1, vecs), f32),
        ),
        [VMEM] * 3,
        (VMEM, VMEM),
    )(x, vectors, sums)
    return direction.reshape(1, levels, rows, cols), coefs.reshape(vecs)


def solution(mesh):
    return jax.shard_map(
        body,
        mesh=mesh,
        in_specs=(
            P("comp", None, "tile", None),
            P(None, "comp", None, "tile", None),
            P("comp", "tile", None),
            P("comp", None, None),
            P("tile", None),
            P("comp", "tile", None, None),
            P("comp", "tile", None, None),
            P("comp", "tile", None, None),
        ),
        out_specs=(P("comp", None, "tile", None), P()),
        check_vma=False,
    )
```

```python
import functools

import jax
import jax.numpy as jnp
from jax import lax
from jax.experimental import pallas as pl
from jax.experimental.pallas import tpu as pltpu
from jax.sharding import PartitionSpec as P


FLUX = 4
LANES = 128
HBM = pl.BlockSpec(memory_space=pltpu.HBM)
VMEM = pl.BlockSpec(memory_space=pltpu.VMEM)
LIMIT = 24 << 20


def call(kernel, outs, in_specs, out_specs, scratch=(), cost=None):
    return pl.pallas_call(
        kernel,
        out_shape=outs,
        in_specs=in_specs,
        out_specs=out_specs,
        scratch_shapes=list(scratch),
        cost_estimate=cost,
        compiler_params=pltpu.CompilerParams(vmem_limit_bytes=LIMIT),
    )


def in_hbm(a):
    return pltpu.with_memory_space_constraint(a, pltpu.HBM)


def split(a):
    high = a.astype(jnp.bfloat16)
    return high, (a - high.astype(jnp.float32)).astype(jnp.bfloat16)


def payload_rows(levels, per):
    return 2 * levels * per + per


def block_place(b, per):
    if per & (per - 1) == 0:
        bits = per.bit_length() - 1
        return lax.shift_right_logical(b, bits), lax.bitwise_and(b, per - 1)
    return lax.div(b, per), lax.rem(b, per)


def gather_kernel(rows, lead, index_ref, state_ref, *refs):
    small = (len(refs) - 4) // 2
    sides, out_ref, x_ref = refs[:small], refs[small], refs[small + 1]
    side_outs, (rows_ref, sems) = refs[small + 2 : 2 * small + 2], refs[2 * small + 2 :]
    cap, bands = rows_ref.shape
    per = x_ref.shape[0]
    top = FLUX * rows
    index = pltpu.make_async_copy(index_ref, rows_ref, sems.at[2 * per])
    index.start()
    copies = []
    for part, (lo, hi) in enumerate(((0, top), (top, x_ref.shape[1]))):
        for c in range(per):
            copies.append(
                pltpu.make_async_copy(
                    state_ref.at[lo:hi, c * LANES : (c + 1) * LANES],
                    x_ref.at[c, lo:hi, :],
                    sems.at[part * per + c],
                )
            )
    for k, (src, dst) in enumerate(zip(sides, side_outs)):
        copies.append(pltpu.make_async_copy(src, dst, sems.at[2 * per + 1 + k]))
    for copy in copies:
        copy.start()
    index.wait()
    for copy in copies[:per]:
        copy.wait()

    def band(n, carry):
        d = n + lead
        d = jnp.where(d >= bands, d - bands, d)
        for j in range(cap):
            r, c = block_place(rows_ref[j, d], per)
            piece = x_ref[c, pl.ds(r, FLUX, stride=rows), :]
            out_ref[pl.ds(n * (cap * FLUX) + j, FLUX, stride=cap), :] = piece
        return carry

    lax.fori_loop(0, bands, band, 0, unroll=2)
    for copy in copies[per:]:
        copy.wait()


def fetch_kernel(after_ref, basis_hbm, basis_ref, sems):
    copies = [
        pltpu.make_async_copy(basis_hbm.at[i], basis_ref.at[i], sems.at[i])
        for i in range(basis_ref.shape[0])
    ]
    for copy in copies:
        copy.start()
    for copy in copies:
        copy.wait()


def gram_kernel(basis_hbm, gram_ref, basis_ref, sems):
    vecs, levels, rows, cols = basis_ref.shape
    copies = [
        pltpu.make_async_copy(basis_hbm.at[:, l], basis_ref.at[:, l], sems.at[l])
        for l in range(levels)
    ]
    for copy in copies:
        copy.start()
    n = vecs * rows
    total = jnp.zeros((n, n), jnp.float32)
    for l in range(levels):
        copies[l].wait()
        a = basis_ref[:, l].reshape(n, cols)
        total = total + lax.dot_general(
            a, a, (((1,), (1,)), ((), ())), preferred_element_type=jnp.float32
        )
    i0 = lax.broadcasted_iota(jnp.int32, (n, n), 0)
    i1 = lax.broadcasted_iota(jnp.int32, (n, n), 1)
    total = jnp.where(lax.rem(i0, rows) == lax.rem(i1, rows), total, 0.0)
    part = jnp.sum(total.reshape(vecs, rows, n), axis=1)
    j0 = lax.broadcasted_iota(jnp.int32, (n, LANES), 0)
    j1 = lax.broadcasted_iota(jnp.int32, (n, LANES), 1)
    fold = jnp.where(lax.div(j0, rows) == j1, 1.0, 0.0)
    gram = jnp.dot(part, fold, precision=lax.Precision.HIGHEST)
    packed = [jnp.zeros((1, LANES), jnp.float32), jnp.zeros((1, LANES), jnp.float32)]
    for i in range(vecs):
        shift = 16 * (i % 8)
        line = gram[i : i + 1, :]
        packed[i // 8] = packed[i // 8] + (pltpu.roll(line, shift, 1) if shift else line)
    gram_ref[...] = jnp.concatenate(packed, axis=0)


def shifted(parts, up):
    n = len(parts)
    lane = lax.broadcasted_iota(jnp.int32, parts[0].shape, 1)
    rolled = [pltpu.roll(p, 1 if up else LANES - 1, 1) for p in parts]
    edge = 0 if up else LANES - 1
    step = -1 if up else 1
    return [jnp.where(lane == edge, rolled[(c + step) % n], rolled[c]) for c in range(n)]


def early_kernel(
    rows, skip, slots_ref, weights_ref, x_ref, kappa_ref, mask_ref, vmix_ref,
    pack_ref, table_ref,
):
    over, blocks = slots_ref.shape
    per = x_ref.shape[0]
    levels = x_ref.shape[1] // rows
    size = payload_rows(levels, per)
    slots = (pack_ref.shape[0] - 2 * size) // blocks * LANES
    row = lax.broadcasted_iota(jnp.int32, (slots, blocks), 0) + skip
    row = jnp.where(row >= slots, row - slots, row)
    mat = jnp.zeros((slots, blocks), jnp.float32)
    for k in range(over):
        mat = mat + jnp.where(slots_ref[k : k + 1, :] == row, weights_ref[k : k + 1, :], 0.0)
    b0 = lax.broadcasted_iota(jnp.int32, (blocks, blocks), 0)
    b1 = lax.broadcasted_iota(jnp.int32, (blocks, blocks), 1)
    order = jnp.where(lax.rem(b0, rows) * per + lax.div(b0, rows) == b1, 1.0, 0.0)
    mat = jnp.dot(order, mat.T, precision=lax.Precision.HIGHEST)
    for p in range(slots // LANES):
        pack_ref[p * blocks : (p + 1) * blocks, :] = mat[:, p * LANES : (p + 1) * LANES]

    ocean = lax.axis_index("comp") == 0
    even = lax.rem(lax.axis_index("tile"), 2) == 0
    vmix = vmix_ref[...]
    d0 = lax.broadcasted_iota(jnp.int32, (levels, levels), 0)
    d1 = lax.broadcasted_iota(jnp.int32, (levels, levels), 1)
    for l in range(levels):
        column = jnp.sum(jnp.where(d0 == d1, vmix[l : l + 1, :], 0.0), axis=1, keepdims=True)
        table_ref[l * levels : (l + 1) * levels, :] = jnp.broadcast_to(column, (levels, LANES))
    pays = []
    for edge, inner in ((0, 1), (rows - 1, rows - 2)):
        xs = [x_ref[c, pl.ds(edge, levels, stride=rows), :] for c in range(per)]
        left, right = shifted(xs, True), shifted(xs, False)
        pay = []
        for c in range(per):
            s = slice(c * LANES, (c + 1) * LANES)
            x = xs[c]
            xi = x_ref[c, pl.ds(inner, levels, stride=rows), :]
            k = kappa_ref[edge : edge + 1, s]
            m = jnp.where(ocean, mask_ref[edge : edge + 1, s].astype(jnp.float32), 1.0)
            acc = x + k * (xi + left[c] + right[c] - 4.0 * x)
            for q in range(levels):
                acc = acc + vmix[:, q : q + 1] * x[q : q + 1, :]
            pay.append((m * acc, x, m * k))
        pays.append(pay)
    base = slots // LANES * blocks
    for n, flag in ((0, even), (1, jnp.logical_not(even))):
        ref = pack_ref.at[base + n * size : base + (n + 1) * size, :]
        for c in range(per):
            a, x, b = [jnp.where(flag, v, u) for u, v in zip(pays[0][c], pays[1][c])]
            ref[c * levels : (c + 1) * levels, :] = a
            ref[(per + c) * levels : (per + c + 1) * levels, :] = x
            ref[2 * per * levels + c : 2 * per * levels + c + 1, :] = b


def regrid_kernel(rows, levels, buf_ref, pack_ref, mask_ref, f_ref, e1_ref, e2_ref):
    per = f_ref.shape[0]
    cap = buf_ref.shape[1] // FLUX
    slots = buf_ref.shape[0] * cap
    blocks = rows * per
    size = payload_rows(levels, per)
    wide = jnp.concatenate(
        [buf_ref[:, f * cap : (f + 1) * cap, :].reshape(slots, LANES) for f in range(FLUX)], axis=1
    )
    bh, bl = split(wide)
    pieces = [pack_ref[p * blocks : (p + 1) * blocks, :] for p in range(slots // LANES)]
    wh, wl = split(jnp.concatenate(pieces, axis=1))
    dot = functools.partial(jnp.dot, preferred_element_type=jnp.float32)
    out = dot(wh, bh) + (dot(wh, bl) + dot(wl, bh))
    for f in range(FLUX):
        for c in range(per):
            f_ref[c, f * rows : (f + 1) * rows, :] = out[
                c * rows : (c + 1) * rows, f * LANES : (f + 1) * LANES
            ]
    ocean = lax.axis_index("comp") != 0
    even = lax.rem(lax.axis_index("tile"), 2) == 0
    base = slots // LANES * blocks
    for n, ref in enumerate((e1_ref, e2_ref)):
        ref[per * levels :, :] = pack_ref[base + n * size + per * levels : base + (n + 1) * size, :]
    for c in range(per):
        s = slice(c * LANES, (c + 1) * LANES)
        edges = []
        for edge in (0, rows - 1):
            m = jnp.where(ocean, mask_ref[edge : edge + 1, s].astype(jnp.float32), 1.0)
            forced = m * f_ref[c, pl.ds(edge, FLUX, stride=rows), :]
            still = jnp.zeros((levels - FLUX, LANES), jnp.float32)
            edges.append(jnp.concatenate([forced, still], axis=0))
        for n, (ref, forced) in enumerate(
            ((e1_ref, jnp.where(even, edges[1], edges[0])), (e2_ref, jnp.where(even, edges[0], edges[1])))
        ):
            at = base + n * size + c * levels
            ref[c * levels : (c + 1) * levels, :] = pack_ref[at : at + levels, :] + forced


def stencil(xs, kappa_ref, rows):
    left, right = shifted(xs, True), shifted(xs, False)
    row = lax.broadcasted_iota(jnp.int32, (rows, LANES), 0)
    out = []
    for c, x in enumerate(xs):
        up = jnp.where(row == 0, 0.0, pltpu.roll(x, 1, 0))
        down = jnp.where(row == rows - 1, 0.0, pltpu.roll(x, rows - 1, 0))
        k = kappa_ref[:, c * LANES : (c + 1) * LANES]
        out.append(k * (up + down + left[c] + right[c] - 4.0 * x))
    return out


def still_kernel(rows, x0_ref, kappa_ref, mask_ref, table_ref, x_ref, x1_ref):
    per = x0_ref.shape[0]
    levels = x0_ref.shape[1] // rows
    ocean = lax.axis_index("comp") == 0

    def advance(src, dst):
        for l in range(levels):
            part = slice(l * rows, (l + 1) * rows)
            xs = [src[c, part, :] for c in range(per)]
            moved = stencil(xs, kappa_ref, rows)
            for c in range(per):
                acc = xs[c] + moved[c]
                for q in range(levels):
                    v = table_ref[l * levels + q : l * levels + q + 1, :]
                    acc = acc + v * src[c, q * rows : (q + 1) * rows, :]
                s = slice(c * LANES, (c + 1) * LANES)
                mask = jnp.where(ocean, mask_ref[:, s].astype(jnp.float32), 1.0)
                dst[c, part, :] = mask * acc

    advance(x0_ref, x1_ref)
    advance(x1_ref, x_ref)


def step_kernel(
    rows, still_ref, x0_ref, f_ref, h1_ref, h2_ref, kappa_ref, mask_ref, vmix_ref, table_ref,
    basis_ref, gram_ref, x_ref, sums_ref, f1_ref,
):
    per = still_ref.shape[0]
    levels = still_ref.shape[1] // rows
    vecs = basis_ref.shape[0]
    ocean = lax.axis_index("comp") == 0
    even = lax.rem(lax.axis_index("tile"), 2) == 0

    def mask(c, part=slice(None)):
        m = mask_ref[part, c * LANES : (c + 1) * LANES].astype(jnp.float32)
        return jnp.where(ocean, m, 1.0)

    for c in range(per):
        m = mask(c)
        for f in range(FLUX):
            part = slice(f * rows, (f + 1) * rows)
            f1_ref[c, part, :] = m * f_ref[c, part, :]
    for l in range(levels):
        part = slice(l * rows, (l + 1) * rows)
        if l < FLUX:
            fs = [f1_ref[c, part, :] for c in range(per)]
            moved = stencil(fs, kappa_ref, rows)
        for c in range(per):
            acc = fs[c] + moved[c] + f_ref[c, part, :] if l < FLUX else 0.0
            for q in range(FLUX):
                v = table_ref[l * levels + q : l * levels + q + 1, :]
                acc = acc + v * f1_ref[c, q * rows : (q + 1) * rows, :]
            x_ref[c, part, :] = still_ref[c, part, :] + mask(c) * acc

    vmix = vmix_ref[...]
    for side, edge, inner in ((0, 0, 1), (1, rows - 1, rows - 2)):
        flag = even if side == 1 else jnp.logical_not(even)

        def take(lo, n):
            return jnp.where(flag, h1_ref[lo : lo + n, :], h2_ref[lo : lo + n, :])

        def factor(c, r):
            r = slice(r, r + 1)
            return mask(c, r), mask(c, r) * kappa_ref[r, c * LANES : (c + 1) * LANES]

        ds = [factor(c, edge)[1] * take((per + c) * levels, levels) for c in range(per)]
        left, right = shifted(ds, True), shifted(ds, False)
        for c in range(per):
            d = ds[c]
            own = x0_ref[c, pl.ds(edge, levels, stride=rows), :]
            foreign = take(c * levels, levels) + take(2 * per * levels + c, 1) * own
            m, mk = factor(c, edge)
            mixed = d
            for q in range(levels):
                mixed = mixed + vmix[:, q : q + 1] * d[q : q + 1, :]
            at = pl.ds(edge, levels, stride=rows)
            change = m * mixed + mk * (left[c] + right[c] - 4.0 * d + foreign)
            x_ref[c, at, :] = x_ref[c, at, :] + change
            at = pl.ds(inner, levels, stride=rows)
            x_ref[c, at, :] = x_ref[c, at, :] + factor(c, inner)[1] * d

    def level(l, accs):
        accs = list(accs)
        for c in range(per):
            s = slice(c * LANES, (c + 1) * LANES)
            x = x_ref[c, pl.ds(l * rows, rows), :]
            for i in range(vecs):
                t = x * basis_ref[i, l, :, s].astype(jnp.float32)
                accs[i] = accs[i] + t.reshape(rows // 8, 8, LANES).sum(0)
            accs[vecs] = accs[vecs] + (x * x).reshape(rows // 8, 8, LANES).sum(0)
        return tuple(accs)

    zero = jnp.zeros((8, LANES), jnp.float32)
    accs = lax.fori_loop(0, levels, level, (zero,) * (vecs + 1))
    lane = lax.broadcasted_iota(jnp.int32, (1, LANES), 1)
    line = jnp.zeros((1, LANES), jnp.float32)
    for i in range(vecs + 1):
        tot = jnp.sum(jnp.sum(accs[i], axis=0, keepdims=True), axis=1, keepdims=True)
        line = line + jnp.where(lane == 64 + i, tot, 0.0)
    block = gram_ref[...] + jnp.concatenate([jnp.zeros((1, LANES), jnp.float32), line], axis=0)
    for d in range(sums_ref.shape[0]):
        sums_ref[d] = block


def finish_kernel(rows, total, x_ref, basis_ref, sums_ref, out_ref, coef_ref):
    per = x_ref.shape[0]
    levels = x_ref.shape[1] // rows
    vecs = basis_ref.shape[0]
    sums = jnp.sum(sums_ref[...], axis=0)
    lane = lax.broadcasted_iota(jnp.int32, (1, LANES), 1)
    tail = pltpu.roll(sums[1:2, :], 64, 1)
    coef = jnp.where(lane < vecs, tail, 0.0) / total
    coef_ref[...] = coef[:, :vecs]
    square = jnp.sum(jnp.where(lane == vecs, tail, 0.0), axis=1, keepdims=True)
    splat = [jnp.sum(jnp.where(lane == i, coef, 0.0), axis=1, keepdims=True) for i in range(vecs)]
    quad = jnp.zeros((1, LANES), jnp.float32)
    for i in range(vecs):
        shift = (LANES - 16 * (i % 8)) % LANES
        line = sums[i // 8 : i // 8 + 1, :]
        line = pltpu.roll(line, shift, 1) if shift else line
        quad = quad + splat[i] * jnp.where(lane < vecs, line, 0.0)
    extra = jnp.sum(coef * (quad - 2.0 * total * coef), axis=1, keepdims=True)
    scale = 1.0 / jnp.sqrt((square + extra) / total + 1e-06)
    wide = [jnp.broadcast_to(scale * s, (8, LANES)) for s in splat]
    scale = jnp.broadcast_to(scale, (8, LANES))

    def level(l, carry):
        for c in range(per):
            s = slice(c * LANES, (c + 1) * LANES)
            x = x_ref[c, pl.ds(l * rows, rows), :].reshape(rows // 8, 8, LANES) * scale
            for i in range(vecs):
                b = basis_ref[i, l, :, s].astype(jnp.float32).reshape(rows // 8, 8, LANES)
                x = x - wide[i] * b
            out_ref[pl.ds(l * rows, rows), s] = x.reshape(rows, LANES)
        return carry

    lax.fori_loop(0, levels, level, 0)


def body(state, basis, kappa, vmix, land_mask, send_rows, recv_slots, recv_weights):
    _, levels, rows, cols = state.shape
    vecs = basis.shape[0]
    bands, cap = send_rows.shape[2:]
    blocks, _ = recv_slots.shape[2:]
    per = cols // LANES
    comps = lax.axis_size("comp")
    devices = comps * bands
    total = float(levels * rows * cols * devices)
    f32 = jnp.float32
    flat = state.reshape(levels * rows, cols)
    vectors = basis[:, 0]
    kap, vm = kappa[0], vmix[0]

    field = jax.ShapeDtypeStruct((per, levels * rows, LANES), f32)
    import_field = jax.ShapeDtypeStruct((per, FLUX * rows, LANES), f32)
    pay = jax.ShapeDtypeStruct((payload_rows(levels, per), LANES), f32)
    pairs1 = [(i, i ^ 1) for i in range(bands)]
    pairs2 = [p for i in range(1, bands - 1, 2) for p in ((i, i + 1), (i + 1, i))]
    swap = [(i, i ^ 1) for i in range(comps)]

    def crossed(pairs):
        return [((c * bands) + i, (c ^ 1) * bands + k) for c in range(comps) for i, k in pairs]

    sides = (kap, land_mask, recv_slots[0, 0].T, recv_weights[0, 0].T, vm)
    lead = bands * 5 // 16
    bucket, columns, kap, land_mask, slots, weights, vm = call(
        functools.partial(gather_kernel, rows, lead),
        (jax.ShapeDtypeStruct((bands * FLUX * cap, LANES), f32), field)
        + tuple(jax.ShapeDtypeStruct(a.shape, a.dtype) for a in sides),
        [HBM] * (2 + len(sides)),
        (VMEM,) * (2 + len(sides)),
        scratch=(
            pltpu.SMEM((cap, bands), jnp.int32),
            pltpu.SemaphoreType.DMA((2 * per + 1 + len(sides),)),
        ),
    )(*[in_hbm(a) for a in (send_rows[0, 0].T, flat) + sides])
    group = [(lead + n) % bands for n in range(bands)]
    moved = lax.all_to_all(
        bucket.reshape(bands, FLUX * cap, LANES), "tile", 0, 0, axis_index_groups=[group]
    )
    pack, table = call(
        functools.partial(early_kernel, rows, lead * cap),
        (
            jax.ShapeDtypeStruct((bands * cap // LANES * blocks + 2 * pay.shape[0], LANES), f32),
            jax.ShapeDtypeStruct((levels * levels, LANES), f32),
        ),
        [VMEM] * 6,
        (VMEM,) * 2,
    )(slots, weights, columns, kap, land_mask, vm)
    pack = lax.ppermute(pack, "comp", swap)
    gram = call(
        gram_kernel,
        jax.ShapeDtypeStruct((2, LANES), f32),
        [HBM],
        VMEM,
        scratch=(
            pltpu.VMEM(vectors.shape, vectors.dtype),
            pltpu.SemaphoreType.DMA((levels,)),
        ),
    )(in_hbm(vectors))
    still = call(
        functools.partial(still_kernel, rows),
        field,
        [VMEM] * 4,
        VMEM,
        scratch=(pltpu.VMEM((per, levels * rows, LANES), f32),),
    )(columns, kap, land_mask, table)

    foreign, edge1, edge2 = call(
        functools.partial(regrid_kernel, rows, levels),
        (import_field, pay, pay),
        [VMEM] * 3,
        (VMEM,) * 3,
    )(moved, pack, land_mask)
    vectors = call(
        fetch_kernel,
        jax.ShapeDtypeStruct(vectors.shape, vectors.dtype),
        [pl.BlockSpec(memory_space=pl.ANY), HBM],
        VMEM,
        scratch=(pltpu.SemaphoreType.DMA((vecs,)),),
    )(edge1, in_hbm(vectors))
    imported = lax.ppermute(foreign, "comp", swap)
    edge1 = lax.ppermute(edge1, ("comp", "tile"), crossed(pairs1))
    edge2 = lax.ppermute(edge2, ("comp", "tile"), crossed(pairs2))
    x, sums = call(
        functools.partial(step_kernel, rows),
        (field, jax.ShapeDtypeStruct((devices, 2, LANES), f32)),
        [VMEM] * 11,
        (VMEM, VMEM),
        scratch=(pltpu.VMEM((per, FLUX * rows, LANES), f32),),
    )(still, columns, imported, edge1, edge2, kap, land_mask, vm, table, vectors, gram)
    sums = lax.all_to_all(sums, ("comp", "tile"), 0, 0)
    direction, coefs = call(
        functools.partial(finish_kernel, rows, total),
        (
            jax.ShapeDtypeStruct((levels * rows, cols), f32),
            jax.ShapeDtypeStruct((1, vecs), f32),
        ),
        [VMEM] * 3,
        (VMEM, VMEM),
    )(x, vectors, sums)
    return direction.reshape(1, levels, rows, cols), coefs.reshape(vecs)


def solution(mesh):
    return jax.shard_map(
        body,
        mesh=mesh,
        in_specs=(
            P("comp", None, "tile", None),
            P(None, "comp", None, "tile", None),
            P("comp", "tile", None),
            P("comp", None, None),
            P("tile", None),
            P("comp", "tile", None, None),
            P("comp", "tile", None, None),
            P("comp", "tile", None, None),
        ),
        out_specs=(P("comp", None, "tile", None), P()),
        check_vma=False,
    )
```

```python
import functools

import jax
import jax.numpy as jnp
from jax import lax
from jax.experimental import pallas as pl
from jax.experimental.pallas import tpu as pltpu
from jax.sharding import PartitionSpec as P


FLUX = 4
LANES = 128
HBM = pl.BlockSpec(memory_space=pltpu.HBM)
VMEM = pl.BlockSpec(memory_space=pltpu.VMEM)
LIMIT = 24 << 20
PUTS = 4
OUTPARTS = 4


def call(kernel, outs, in_specs, out_specs, scratch=(), aliases={}):
    return pl.pallas_call(
        kernel,
        out_shape=outs,
        in_specs=in_specs,
        out_specs=out_specs,
        scratch_shapes=list(scratch),
        input_output_aliases=aliases,
        compiler_params=pltpu.CompilerParams(vmem_limit_bytes=LIMIT),
    )


def in_hbm(a):
    return pltpu.with_memory_space_constraint(a, pltpu.HBM)


def split(a):
    high = a.astype(jnp.bfloat16)
    return high, (a - high.astype(jnp.float32)).astype(jnp.bfloat16)


def payload_rows(levels, per):
    return 2 * levels * per + per


def block_place(b, per):
    if per & (per - 1) == 0:
        bits = per.bit_length() - 1
        return lax.shift_right_logical(b, bits), lax.bitwise_and(b, per - 1)
    return lax.div(b, per), lax.rem(b, per)


def gather_kernel(rows, lead, index_ref, state_ref, *refs):
    small = (len(refs) - 5) // 2
    sides, out_hbm, x_ref = refs[:small], refs[small], refs[small + 1]
    side_outs, (rows_ref, out_ref, sems) = refs[small + 2 : 2 * small + 2], refs[2 * small + 2 :]
    cap, bands = rows_ref.shape
    per = x_ref.shape[0]
    top = FLUX * rows
    index = pltpu.make_async_copy(index_ref, rows_ref, sems.at[2 * per])
    index.start()
    copies = []
    for part, (lo, hi) in enumerate(((0, top), (top, x_ref.shape[1]))):
        for c in range(per):
            copies.append(
                pltpu.make_async_copy(
                    state_ref.at[lo:hi, c * LANES : (c + 1) * LANES],
                    x_ref.at[c, lo:hi, :],
                    sems.at[part * per + c],
                )
            )
    for k, (src, dst) in enumerate(zip(sides, side_outs)):
        copies.append(pltpu.make_async_copy(src, dst, sems.at[2 * per + 1 + k]))
    for copy in copies:
        copy.start()
    index.wait()
    for copy in copies[:per]:
        copy.wait()

    def band(n, carry):
        d = n + lead
        d = jnp.where(d >= bands, d - bands, d)
        for j in range(cap):
            r, c = block_place(rows_ref[j, d], per)
            piece = x_ref[c, pl.ds(r, FLUX, stride=rows), :]
            out_ref[pl.ds(n * (cap * FLUX) + j, FLUX, stride=cap), :] = piece
        return carry

    span = bands // OUTPARTS
    size = span * cap * FLUX
    for p in range(OUTPARTS):
        lax.fori_loop(p * span, (p + 1) * span, band, 0, unroll=2)
        part = slice(p * size, (p + 1) * size)
        copy = pltpu.make_async_copy(
            out_ref.at[part, :], out_hbm.at[part, :], sems.at[2 * per + 1 + small + p]
        )
        copy.start()
        copies.append(copy)
    for copy in copies[per:]:
        copy.wait()


def fetch_kernel(after_ref, basis_hbm, basis_ref, sems):
    copies = [
        pltpu.make_async_copy(basis_hbm.at[i], basis_ref.at[i], sems.at[i])
        for i in range(basis_ref.shape[0])
    ]
    for copy in copies:
        copy.start()
    for copy in copies:
        copy.wait()


def gram_kernel(basis_hbm, gram_ref, basis_ref, sems):
    vecs, levels, rows, cols = basis_ref.shape
    copies = [
        pltpu.make_async_copy(basis_hbm.at[:, l], basis_ref.at[:, l], sems.at[l])
        for l in range(levels)
    ]
    for copy in copies:
        copy.start()
    n = vecs * rows
    total = jnp.zeros((n, n), jnp.float32)
    for l in range(levels):
        copies[l].wait()
        a = basis_ref[:, l].reshape(n, cols)
        total = total + lax.dot_general(
            a, a, (((1,), (1,)), ((), ())), preferred_element_type=jnp.float32
        )
    i0 = lax.broadcasted_iota(jnp.int32, (n, n), 0)
    i1 = lax.broadcasted_iota(jnp.int32, (n, n), 1)
    total = jnp.where(lax.rem(i0, rows) == lax.rem(i1, rows), total, 0.0)
    part = jnp.sum(total.reshape(vecs, rows, n), axis=1)
    j0 = lax.broadcasted_iota(jnp.int32, (n, LANES), 0)
    j1 = lax.broadcasted_iota(jnp.int32, (n, LANES), 1)
    fold = jnp.where(lax.div(j0, rows) == j1, 1.0, 0.0)
    gram = jnp.dot(part, fold, precision=lax.Precision.HIGHEST)
    packed = [jnp.zeros((1, LANES), jnp.float32), jnp.zeros((1, LANES), jnp.float32)]
    for i in range(vecs):
        shift = 16 * (i % 8)
        line = gram[i : i + 1, :]
        packed[i // 8] = packed[i // 8] + (pltpu.roll(line, shift, 1) if shift else line)
    gram_ref[...] = jnp.concatenate(packed, axis=0)


def shifted(parts, up):
    n = len(parts)
    lane = lax.broadcasted_iota(jnp.int32, parts[0].shape, 1)
    rolled = [pltpu.roll(p, 1 if up else LANES - 1, 1) for p in parts]
    edge = 0 if up else LANES - 1
    step = -1 if up else 1
    return [jnp.where(lane == edge, rolled[(c + step) % n], rolled[c]) for c in range(n)]


def early_kernel(
    rows, skip, slots_ref, weights_ref, x_ref, kappa_ref, mask_ref, vmix_ref,
    pack_ref, table_ref,
):
    over, blocks = slots_ref.shape
    per = x_ref.shape[0]
    levels = x_ref.shape[1] // rows
    size = payload_rows(levels, per)
    slots = (pack_ref.shape[0] - 2 * size) // blocks * LANES
    row = lax.broadcasted_iota(jnp.int32, (slots, blocks), 0) + skip
    row = jnp.where(row >= slots, row - slots, row)
    mat = jnp.zeros((slots, blocks), jnp.float32)
    for k in range(over):
        mat = mat + jnp.where(slots_ref[k : k + 1, :] == row, weights_ref[k : k + 1, :], 0.0)
    b0 = lax.broadcasted_iota(jnp.int32, (blocks, blocks), 0)
    b1 = lax.broadcasted_iota(jnp.int32, (blocks, blocks), 1)
    order = jnp.where(lax.rem(b0, rows) * per + lax.div(b0, rows) == b1, 1.0, 0.0)
    mat = jnp.dot(order, mat.T, precision=lax.Precision.HIGHEST)
    for p in range(slots // LANES):
        pack_ref[p * blocks : (p + 1) * blocks, :] = mat[:, p * LANES : (p + 1) * LANES]

    ocean = lax.axis_index("comp") == 0
    even = lax.rem(lax.axis_index("tile"), 2) == 0
    vmix = vmix_ref[...]
    d0 = lax.broadcasted_iota(jnp.int32, (levels, levels), 0)
    d1 = lax.broadcasted_iota(jnp.int32, (levels, levels), 1)
    for l in range(levels):
        column = jnp.sum(jnp.where(d0 == d1, vmix[l : l + 1, :], 0.0), axis=1, keepdims=True)
        table_ref[l * levels : (l + 1) * levels, :] = jnp.broadcast_to(column, (levels, LANES))
    pays = []
    for edge, inner in ((0, 1), (rows - 1, rows - 2)):
        xs = [x_ref[c, pl.ds(edge, levels, stride=rows), :] for c in range(per)]
        left, right = shifted(xs, True), shifted(xs, False)
        pay = []
        for c in range(per):
            s = slice(c * LANES, (c + 1) * LANES)
            x = xs[c]
            xi = x_ref[c, pl.ds(inner, levels, stride=rows), :]
            k = kappa_ref[edge : edge + 1, s]
            m = jnp.where(ocean, mask_ref[edge : edge + 1, s].astype(jnp.float32), 1.0)
            acc = x + k * (xi + left[c] + right[c] - 4.0 * x)
            for q in range(levels):
                acc = acc + vmix[:, q : q + 1] * x[q : q + 1, :]
            pay.append((m * acc, x, m * k))
        pays.append(pay)
    base = slots // LANES * blocks
    for n, flag in ((0, even), (1, jnp.logical_not(even))):
        ref = pack_ref.at[base + n * size : base + (n + 1) * size, :]
        for c in range(per):
            a, x, b = [jnp.where(flag, v, u) for u, v in zip(pays[0][c], pays[1][c])]
            ref[c * levels : (c + 1) * levels, :] = a
            ref[(per + c) * levels : (per + c + 1) * levels, :] = x
            ref[2 * per * levels + c : 2 * per * levels + c + 1, :] = b


def regrid_kernel(rows, levels, buf_ref, pack_ref, mask_ref, f_ref, e1_ref, e2_ref):
    per = f_ref.shape[0]
    cap = buf_ref.shape[1] // FLUX
    slots = buf_ref.shape[0] * cap
    blocks = rows * per
    size = payload_rows(levels, per)
    wide = jnp.concatenate(
        [buf_ref[:, f * cap : (f + 1) * cap, :].reshape(slots, LANES) for f in range(FLUX)], axis=1
    )
    bh, bl = split(wide)
    pieces = [pack_ref[p * blocks : (p + 1) * blocks, :] for p in range(slots // LANES)]
    wh, wl = split(jnp.concatenate(pieces, axis=1))
    dot = functools.partial(jnp.dot, preferred_element_type=jnp.float32)
    out = dot(wh, bh) + (dot(wh, bl) + dot(wl, bh))
    for f in range(FLUX):
        for c in range(per):
            f_ref[c, f * rows : (f + 1) * rows, :] = out[
                c * rows : (c + 1) * rows, f * LANES : (f + 1) * LANES
            ]
    ocean = lax.axis_index("comp") != 0
    even = lax.rem(lax.axis_index("tile"), 2) == 0
    base = slots // LANES * blocks
    for n, ref in enumerate((e1_ref, e2_ref)):
        ref[per * levels :, :] = pack_ref[base + n * size + per * levels : base + (n + 1) * size, :]
    for c in range(per):
        s = slice(c * LANES, (c + 1) * LANES)
        edges = []
        for edge in (0, rows - 1):
            m = jnp.where(ocean, mask_ref[edge : edge + 1, s].astype(jnp.float32), 1.0)
            forced = m * f_ref[c, pl.ds(edge, FLUX, stride=rows), :]
            still = jnp.zeros((levels - FLUX, LANES), jnp.float32)
            edges.append(jnp.concatenate([forced, still], axis=0))
        for n, (ref, forced) in enumerate(
            ((e1_ref, jnp.where(even, edges[1], edges[0])), (e2_ref, jnp.where(even, edges[0], edges[1])))
        ):
            at = base + n * size + c * levels
            ref[c * levels : (c + 1) * levels, :] = pack_ref[at : at + levels, :] + forced


def stencil(xs, kappa_ref, rows):
    left, right = shifted(xs, True), shifted(xs, False)
    row = lax.broadcasted_iota(jnp.int32, (rows, LANES), 0)
    out = []
    for c, x in enumerate(xs):
        up = jnp.where(row == 0, 0.0, pltpu.roll(x, 1, 0))
        down = jnp.where(row == rows - 1, 0.0, pltpu.roll(x, rows - 1, 0))
        k = kappa_ref[:, c * LANES : (c + 1) * LANES]
        out.append(k * (up + down + left[c] + right[c] - 4.0 * x))
    return out


def still_kernel(rows, x0_ref, kappa_ref, mask_ref, table_ref, x_ref, x1_ref):
    per = x0_ref.shape[0]
    levels = x0_ref.shape[1] // rows
    ocean = lax.axis_index("comp") == 0

    def advance(src, dst):
        for l in range(levels):
            part = slice(l * rows, (l + 1) * rows)
            xs = [src[c, part, :] for c in range(per)]
            moved = stencil(xs, kappa_ref, rows)
            for c in range(per):
                acc = xs[c] + moved[c]
                for q in range(levels):
                    v = table_ref[l * levels + q : l * levels + q + 1, :]
                    acc = acc + v * src[c, q * rows : (q + 1) * rows, :]
                s = slice(c * LANES, (c + 1) * LANES)
                mask = jnp.where(ocean, mask_ref[:, s].astype(jnp.float32), 1.0)
                dst[c, part, :] = mask * acc

    advance(x0_ref, x1_ref)
    advance(x1_ref, x_ref)


def forced_kernel(rows, still_ref, f_ref, kappa_ref, mask_ref, table_ref, x_ref, f1_ref):
    per = still_ref.shape[0]
    levels = still_ref.shape[1] // rows
    ocean = lax.axis_index("comp") == 0

    def mask(c):
        m = mask_ref[:, c * LANES : (c + 1) * LANES].astype(jnp.float32)
        return jnp.where(ocean, m, 1.0)

    for c in range(per):
        m = mask(c)
        for f in range(FLUX):
            part = slice(f * rows, (f + 1) * rows)
            f1_ref[c, part, :] = m * f_ref[c, part, :]
    for l in range(levels):
        part = slice(l * rows, (l + 1) * rows)
        if l < FLUX:
            fs = [f1_ref[c, part, :] for c in range(per)]
            moved = stencil(fs, kappa_ref, rows)
        for c in range(per):
            acc = fs[c] + moved[c] + f_ref[c, part, :] if l < FLUX else 0.0
            for q in range(FLUX):
                v = table_ref[l * levels + q : l * levels + q + 1, :]
                acc = acc + v * f1_ref[c, q * rows : (q + 1) * rows, :]
            x_ref[c, part, :] = still_ref[c, part, :] + mask(c) * acc


def step_kernel(
    rows, most_ref, x0_ref, h1_ref, h2_ref, kappa_ref, mask_ref, vmix_ref,
    basis_ref, gram_ref, x_ref, sums_ref,
):
    per = x_ref.shape[0]
    levels = x_ref.shape[1] // rows
    vecs = basis_ref.shape[0]
    ocean = lax.axis_index("comp") == 0
    even = lax.rem(lax.axis_index("tile"), 2) == 0

    def mask(c, part):
        m = mask_ref[part, c * LANES : (c + 1) * LANES].astype(jnp.float32)
        return jnp.where(ocean, m, 1.0)

    vmix = vmix_ref[...]
    for side, edge, inner in ((0, 0, 1), (1, rows - 1, rows - 2)):
        flag = even if side == 1 else jnp.logical_not(even)

        def take(lo, n):
            return jnp.where(flag, h1_ref[lo : lo + n, :], h2_ref[lo : lo + n, :])

        def factor(c, r):
            r = slice(r, r + 1)
            return mask(c, r), mask(c, r) * kappa_ref[r, c * LANES : (c + 1) * LANES]

        ds = [factor(c, edge)[1] * take((per + c) * levels, levels) for c in range(per)]
        left, right = shifted(ds, True), shifted(ds, False)
        for c in range(per):
            d = ds[c]
            own = x0_ref[c, pl.ds(edge, levels, stride=rows), :]
            foreign = take(c * levels, levels) + take(2 * per * levels + c, 1) * own
            m, mk = factor(c, edge)
            mixed = d
            for q in range(levels):
                mixed = mixed + vmix[:, q : q + 1] * d[q : q + 1, :]
            at = pl.ds(edge, levels, stride=rows)
            change = m * mixed + mk * (left[c] + right[c] - 4.0 * d + foreign)
            x_ref[c, at, :] = x_ref[c, at, :] + change
            at = pl.ds(inner, levels, stride=rows)
            x_ref[c, at, :] = x_ref[c, at, :] + factor(c, inner)[1] * d

    def level(l, accs):
        accs = list(accs)
        for c in range(per):
            s = slice(c * LANES, (c + 1) * LANES)
            x = x_ref[c, pl.ds(l * rows, rows), :]
            for i in range(vecs):
                t = x * basis_ref[i, l, :, s].astype(jnp.float32)
                accs[i] = accs[i] + t.reshape(rows // 8, 8, LANES).sum(0)
            accs[vecs] = accs[vecs] + (x * x).reshape(rows // 8, 8, LANES).sum(0)
        return tuple(accs)

    zero = jnp.zeros((8, LANES), jnp.float32)
    accs = lax.fori_loop(0, levels, level, (zero,) * (vecs + 1))
    lane = lax.broadcasted_iota(jnp.int32, (1, LANES), 1)
    line = jnp.zeros((1, LANES), jnp.float32)
    for i in range(vecs + 1):
        tot = jnp.sum(jnp.sum(accs[i], axis=0, keepdims=True), axis=1, keepdims=True)
        line = line + jnp.where(lane == 64 + i, tot, 0.0)
    block = gram_ref[...] + jnp.concatenate([jnp.zeros((1, LANES), jnp.float32), line], axis=0)
    for d in range(sums_ref.shape[0]):
        sums_ref[d] = block


def finish_kernel(
    rows, total, x_ref, basis_ref, sums_ref, out_hbm, coef_hbm, out_ref, coef_ref, sems
):
    per = x_ref.shape[0]
    levels = x_ref.shape[1] // rows
    vecs = basis_ref.shape[0]
    sums = jnp.sum(sums_ref[...], axis=0)
    lane = lax.broadcasted_iota(jnp.int32, (1, LANES), 1)
    tail = pltpu.roll(sums[1:2, :], 64, 1)
    coef = jnp.where(lane < vecs, tail, 0.0) / total
    coef_ref[...] = coef[:, :vecs]
    copies = [pltpu.make_async_copy(coef_ref, coef_hbm, sems.at[PUTS])]
    copies[0].start()
    square = jnp.sum(jnp.where(lane == vecs, tail, 0.0), axis=1, keepdims=True)
    splat = [jnp.sum(jnp.where(lane == i, coef, 0.0), axis=1, keepdims=True) for i in range(vecs)]
    quad = jnp.zeros((1, LANES), jnp.float32)
    for i in range(vecs):
        shift = (LANES - 16 * (i % 8)) % LANES
        line = sums[i // 8 : i // 8 + 1, :]
        line = pltpu.roll(line, shift, 1) if shift else line
        quad = quad + splat[i] * jnp.where(lane < vecs, line, 0.0)
    extra = jnp.sum(coef * (quad - 2.0 * total * coef), axis=1, keepdims=True)
    scale = 1.0 / jnp.sqrt((square + extra) / total + 1e-06)
    wide = [jnp.broadcast_to(scale * s, (8, LANES)) for s in splat]
    scale = jnp.broadcast_to(scale, (8, LANES))

    def level(l, carry):
        for c in range(per):
            s = slice(c * LANES, (c + 1) * LANES)
            x = x_ref[c, pl.ds(l * rows, rows), :].reshape(rows // 8, 8, LANES) * scale
            for i in range(vecs):
                b = basis_ref[i, l, :, s].astype(jnp.float32).reshape(rows // 8, 8, LANES)
                x = x - wide[i] * b
            out_ref[pl.ds(l * rows, rows), s] = x.reshape(rows, LANES)
        return carry

    span = levels // PUTS
    for p in range(PUTS):
        lax.fori_loop(p * span, (p + 1) * span, level, 0)
        part = slice(p * span * rows, (p + 1) * span * rows)
        copy = pltpu.make_async_copy(out_ref.at[part, :], out_hbm.at[part, :], sems.at[p])
        copy.start()
        copies.append(copy)
    for copy in copies:
        copy.wait()


def body(state, basis, kappa, vmix, land_mask, send_rows, recv_slots, recv_weights):
    _, levels, rows, cols = state.shape
    vecs = basis.shape[0]
    bands, cap = send_rows.shape[2:]
    blocks, _ = recv_slots.shape[2:]
    per = cols // LANES
    comps = lax.axis_size("comp")
    devices = comps * bands
    total = float(levels * rows * cols * devices)
    f32 = jnp.float32
    flat = state.reshape(levels * rows, cols)
    vectors = basis[:, 0]
    kap, vm = kappa[0], vmix[0]

    field = jax.ShapeDtypeStruct((per, levels * rows, LANES), f32)
    import_field = jax.ShapeDtypeStruct((per, FLUX * rows, LANES), f32)
    pay = jax.ShapeDtypeStruct((payload_rows(levels, per), LANES), f32)
    pairs1 = [(i, i ^ 1) for i in range(bands)]
    pairs2 = [p for i in range(1, bands - 1, 2) for p in ((i, i + 1), (i + 1, i))]
    swap = [(i, i ^ 1) for i in range(comps)]

    def crossed(pairs):
        return [((c * bands) + i, (c ^ 1) * bands + k) for c in range(comps) for i, k in pairs]

    sides = (kap, land_mask, recv_slots[0, 0].T, recv_weights[0, 0].T, vm)
    lead = bands * 5 // 16
    bucket, columns, kap, land_mask, slots, weights, vm = call(
        functools.partial(gather_kernel, rows, lead),
        (jax.ShapeDtypeStruct((bands * FLUX * cap, LANES), f32), field)
        + tuple(jax.ShapeDtypeStruct(a.shape, a.dtype) for a in sides),
        [HBM] * (2 + len(sides)),
        (HBM,) + (VMEM,) * (1 + len(sides)),
        scratch=(
            pltpu.SMEM((cap, bands), jnp.int32),
            pltpu.VMEM((bands * FLUX * cap, LANES), f32),
            pltpu.SemaphoreType.DMA((2 * per + 1 + len(sides) + OUTPARTS,)),
        ),
    )(*[in_hbm(a) for a in (send_rows[0, 0].T, flat) + sides])
    group = [(lead + n) % bands for n in range(bands)]
    moved = lax.all_to_all(
        bucket.reshape(bands, FLUX * cap, LANES), "tile", 0, 0, axis_index_groups=[group]
    )
    pack, table = call(
        functools.partial(early_kernel, rows, lead * cap),
        (
            jax.ShapeDtypeStruct((bands * cap // LANES * blocks + 2 * pay.shape[0], LANES), f32),
            jax.ShapeDtypeStruct((levels * levels, LANES), f32),
        ),
        [VMEM] * 6,
        (VMEM,) * 2,
    )(slots, weights, columns, kap, land_mask, vm)
    pack = lax.ppermute(pack, "comp", swap)
    gram = call(
        gram_kernel,
        jax.ShapeDtypeStruct((2, LANES), f32),
        [HBM],
        VMEM,
        scratch=(
            pltpu.VMEM(vectors.shape, vectors.dtype),
            pltpu.SemaphoreType.DMA((levels,)),
        ),
    )(in_hbm(vectors))
    still = call(
        functools.partial(still_kernel, rows),
        field,
        [VMEM] * 4,
        VMEM,
        scratch=(pltpu.VMEM((per, levels * rows, LANES), f32),),
    )(columns, kap, land_mask, table)

    foreign, edge1, edge2 = call(
        functools.partial(regrid_kernel, rows, levels),
        (import_field, pay, pay),
        [VMEM] * 3,
        (VMEM,) * 3,
    )(moved, pack, land_mask)
    vectors = call(
        fetch_kernel,
        jax.ShapeDtypeStruct(vectors.shape, vectors.dtype),
        [pl.BlockSpec(memory_space=pl.ANY), HBM],
        VMEM,
        scratch=(pltpu.SemaphoreType.DMA((vecs,)),),
    )(edge1, in_hbm(vectors))
    imported = lax.ppermute(foreign, "comp", swap)
    edge1 = lax.ppermute(edge1, ("comp", "tile"), crossed(pairs1))
    edge2 = lax.ppermute(edge2, ("comp", "tile"), crossed(pairs2))
    most = call(
        functools.partial(forced_kernel, rows),
        field,
        [VMEM] * 5,
        VMEM,
        scratch=(pltpu.VMEM((per, FLUX * rows, LANES), f32),),
    )(still, imported, kap, land_mask, table)
    x, sums = call(
        functools.partial(step_kernel, rows),
        (field, jax.ShapeDtypeStruct((devices, 2, LANES), f32)),
        [VMEM] * 9,
        (VMEM, VMEM),
        aliases={0: 0},
    )(most, columns, edge1, edge2, kap, land_mask, vm, vectors, gram)
    sums = lax.all_to_all(sums, ("comp", "tile"), 0, 0)
    direction, coefs = call(
        functools.partial(finish_kernel, rows, total),
        (
            jax.ShapeDtypeStruct((levels * rows, cols), f32),
            jax.ShapeDtypeStruct((1, vecs), f32),
        ),
        [VMEM] * 3,
        (HBM, HBM),
        scratch=(
            pltpu.VMEM((levels * rows, cols), f32),
            pltpu.VMEM((1, vecs), f32),
            pltpu.SemaphoreType.DMA((PUTS + 1,)),
        ),
    )(x, vectors, sums)
    return direction.reshape(1, levels, rows, cols), coefs.reshape(vecs)


def solution(mesh):
    return jax.shard_map(
        body,
        mesh=mesh,
        in_specs=(
            P("comp", None, "tile", None),
            P(None, "comp", None, "tile", None),
            P("comp", "tile", None),
            P("comp", None, None),
            P("tile", None),
            P("comp", "tile", None, None),
            P("comp", "tile", None, None),
            P("comp", "tile", None, None),
        ),
        out_specs=(P("comp", None, "tile", None), P()),
        check_vma=False,
    )
```

```python
import functools

import jax
import jax.numpy as jnp
from jax import lax
from jax.experimental import pallas as pl
from jax.experimental.pallas import tpu as pltpu
from jax.sharding import PartitionSpec as P


FLUX = 4
LANES = 128
HBM = pl.BlockSpec(memory_space=pltpu.HBM)
VMEM = pl.BlockSpec(memory_space=pltpu.VMEM)
LIMIT = 24 << 20
PUTS = 4
OUTPARTS = 4


def call(kernel, outs, in_specs, out_specs, scratch=(), aliases={}):
    return pl.pallas_call(
        kernel,
        out_shape=outs,
        in_specs=in_specs,
        out_specs=out_specs,
        scratch_shapes=list(scratch),
        input_output_aliases=aliases,
        compiler_params=pltpu.CompilerParams(vmem_limit_bytes=LIMIT),
    )


def in_hbm(a):
    return pltpu.with_memory_space_constraint(a, pltpu.HBM)


def split(a):
    high = a.astype(jnp.bfloat16)
    return high, (a - high.astype(jnp.float32)).astype(jnp.bfloat16)


def payload_rows(levels, per):
    return 2 * levels * per + per


def block_place(b, per):
    if per & (per - 1) == 0:
        bits = per.bit_length() - 1
        return lax.shift_right_logical(b, bits), lax.bitwise_and(b, per - 1)
    return lax.div(b, per), lax.rem(b, per)


def gather_kernel(rows, group, index_ref, state_ref, *refs):
    small = (len(refs) - 5) // 2
    sides, out_hbm, x_ref = refs[:small], refs[small], refs[small + 1]
    side_outs, (rows_ref, out_ref, sems) = refs[small + 2 : 2 * small + 2], refs[2 * small + 2 :]
    cap, bands = rows_ref.shape
    per = x_ref.shape[0]
    top = FLUX * rows
    index = pltpu.make_async_copy(index_ref, rows_ref, sems.at[2 * per])
    index.start()
    copies = []
    for part, (lo, hi) in enumerate(((0, top), (top, x_ref.shape[1]))):
        for c in range(per):
            copies.append(
                pltpu.make_async_copy(
                    state_ref.at[lo:hi, c * LANES : (c + 1) * LANES],
                    x_ref.at[c, lo:hi, :],
                    sems.at[part * per + c],
                )
            )
    for k, (src, dst) in enumerate(zip(sides, side_outs)):
        copies.append(pltpu.make_async_copy(src, dst, sems.at[2 * per + 1 + k]))
    for copy in copies:
        copy.start()
    index.wait()
    for copy in copies[:per]:
        copy.wait()

    def band(n):
        for j in range(cap):
            r, c = block_place(rows_ref[j, group[n]], per)
            piece = x_ref[c, pl.ds(r, FLUX, stride=rows), :]
            out_ref[pl.ds(n * (cap * FLUX) + j, FLUX, stride=cap), :] = piece

    span = bands // OUTPARTS
    size = span * cap * FLUX
    for p in range(OUTPARTS):
        for n in range(p * span, (p + 1) * span):
            band(n)
        part = slice(p * size, (p + 1) * size)
        copy = pltpu.make_async_copy(
            out_ref.at[part, :], out_hbm.at[part, :], sems.at[2 * per + 1 + small + p]
        )
        copy.start()
        copies.append(copy)
    for copy in copies[per:]:
        copy.wait()


def fetch_kernel(after_ref, basis_hbm, basis_ref, sems):
    copies = [
        pltpu.make_async_copy(basis_hbm.at[i], basis_ref.at[i], sems.at[i])
        for i in range(basis_ref.shape[0])
    ]
    for copy in copies:
        copy.start()
    for copy in copies:
        copy.wait()


def gram_kernel(basis_hbm, gram_ref, basis_ref, sems):
    vecs, levels, rows, cols = basis_ref.shape
    copies = [
        pltpu.make_async_copy(basis_hbm.at[:, l], basis_ref.at[:, l], sems.at[l])
        for l in range(levels)
    ]
    for copy in copies:
        copy.start()
    n = vecs * rows
    total = jnp.zeros((n, n), jnp.float32)
    for l in range(levels):
        copies[l].wait()
        a = basis_ref[:, l].reshape(n, cols)
        total = total + lax.dot_general(
            a, a, (((1,), (1,)), ((), ())), preferred_element_type=jnp.float32
        )
    i0 = lax.broadcasted_iota(jnp.int32, (n, n), 0)
    i1 = lax.broadcasted_iota(jnp.int32, (n, n), 1)
    total = jnp.where(lax.rem(i0, rows) == lax.rem(i1, rows), total, 0.0)
    part = jnp.sum(total.reshape(vecs, rows, n), axis=1)
    j0 = lax.broadcasted_iota(jnp.int32, (n, LANES), 0)
    j1 = lax.broadcasted_iota(jnp.int32, (n, LANES), 1)
    fold = jnp.where(lax.div(j0, rows) == j1, 1.0, 0.0)
    gram = jnp.dot(part, fold, precision=lax.Precision.HIGHEST)
    packed = [jnp.zeros((1, LANES), jnp.float32), jnp.zeros((1, LANES), jnp.float32)]
    for i in range(vecs):
        shift = 16 * (i % 8)
        line = gram[i : i + 1, :]
        packed[i // 8] = packed[i // 8] + (pltpu.roll(line, shift, 1) if shift else line)
    gram_ref[...] = jnp.concatenate(packed, axis=0)


def shifted(parts, up):
    n = len(parts)
    lane = lax.broadcasted_iota(jnp.int32, parts[0].shape, 1)
    rolled = [pltpu.roll(p, 1 if up else LANES - 1, 1) for p in parts]
    edge = 0 if up else LANES - 1
    step = -1 if up else 1
    return [jnp.where(lane == edge, rolled[(c + step) % n], rolled[c]) for c in range(n)]


def early_kernel(
    rows, group, slots_ref, weights_ref, x_ref, kappa_ref, mask_ref, vmix_ref,
    pack_ref, table_ref,
):
    over, blocks = slots_ref.shape
    per = x_ref.shape[0]
    levels = x_ref.shape[1] // rows
    size = payload_rows(levels, per)
    slots = (pack_ref.shape[0] - 2 * size) // blocks * LANES
    cap = slots // len(group)
    row = lax.broadcasted_iota(jnp.int32, (cap, blocks), 0)
    mat = []
    for d in group:
        part = jnp.zeros((cap, blocks), jnp.float32)
        for k in range(over):
            hit = slots_ref[k : k + 1, :] == row + d * cap
            part = part + jnp.where(hit, weights_ref[k : k + 1, :], 0.0)
        mat.append(part)
    mat = jnp.concatenate(mat, axis=0)
    b0 = lax.broadcasted_iota(jnp.int32, (blocks, blocks), 0)
    b1 = lax.broadcasted_iota(jnp.int32, (blocks, blocks), 1)
    order = jnp.where(lax.rem(b0, rows) * per + lax.div(b0, rows) == b1, 1.0, 0.0)
    mat = jnp.dot(order, mat.T, precision=lax.Precision.HIGHEST)
    for p in range(slots // LANES):
        pack_ref[p * blocks : (p + 1) * blocks, :] = mat[:, p * LANES : (p + 1) * LANES]

    ocean = lax.axis_index("comp") == 0
    even = lax.rem(lax.axis_index("tile"), 2) == 0
    vmix = vmix_ref[...]
    d0 = lax.broadcasted_iota(jnp.int32, (levels, levels), 0)
    d1 = lax.broadcasted_iota(jnp.int32, (levels, levels), 1)
    for l in range(levels):
        column = jnp.sum(jnp.where(d0 == d1, vmix[l : l + 1, :], 0.0), axis=1, keepdims=True)
        table_ref[l * levels : (l + 1) * levels, :] = jnp.broadcast_to(column, (levels, LANES))
    pays = []
    for edge, inner in ((0, 1), (rows - 1, rows - 2)):
        xs = [x_ref[c, pl.ds(edge, levels, stride=rows), :] for c in range(per)]
        left, right = shifted(xs, True), shifted(xs, False)
        pay = []
        for c in range(per):
            s = slice(c * LANES, (c + 1) * LANES)
            x = xs[c]
            xi = x_ref[c, pl.ds(inner, levels, stride=rows), :]
            k = kappa_ref[edge : edge + 1, s]
            m = jnp.where(ocean, mask_ref[edge : edge + 1, s].astype(jnp.float32), 1.0)
            acc = x + k * (xi + left[c] + right[c] - 4.0 * x)
            for q in range(levels):
                acc = acc + vmix[:, q : q + 1] * x[q : q + 1, :]
            pay.append((m * acc, x, m * k))
        pays.append(pay)
    base = slots // LANES * blocks
    for n, flag in ((0, even), (1, jnp.logical_not(even))):
        ref = pack_ref.at[base + n * size : base + (n + 1) * size, :]
        for c in range(per):
            a, x, b = [jnp.where(flag, v, u) for u, v in zip(pays[0][c], pays[1][c])]
            ref[c * levels : (c + 1) * levels, :] = a
            ref[(per + c) * levels : (per + c + 1) * levels, :] = x
            ref[2 * per * levels + c : 2 * per * levels + c + 1, :] = b


def regrid_kernel(rows, levels, buf_ref, pack_ref, mask_ref, f_ref, e1_ref, e2_ref):
    per = f_ref.shape[0]
    cap = buf_ref.shape[1] // FLUX
    slots = buf_ref.shape[0] * cap
    blocks = rows * per
    size = payload_rows(levels, per)
    wide = jnp.concatenate(
        [buf_ref[:, f * cap : (f + 1) * cap, :].reshape(slots, LANES) for f in range(FLUX)], axis=1
    )
    bh, bl = split(wide)
    pieces = [pack_ref[p * blocks : (p + 1) * blocks, :] for p in range(slots // LANES)]
    wh, wl = split(jnp.concatenate(pieces, axis=1))
    dot = functools.partial(jnp.dot, preferred_element_type=jnp.float32)
    out = dot(wh, bh) + (dot(wh, bl) + dot(wl, bh))
    for f in range(FLUX):
        for c in range(per):
            f_ref[c, f * rows : (f + 1) * rows, :] = out[
                c * rows : (c + 1) * rows, f * LANES : (f + 1) * LANES
            ]
    ocean = lax.axis_index("comp") != 0
    even = lax.rem(lax.axis_index("tile"), 2) == 0
    base = slots // LANES * blocks
    for n, ref in enumerate((e1_ref, e2_ref)):
        ref[per * levels :, :] = pack_ref[base + n * size + per * levels : base + (n + 1) * size, :]
    for c in range(per):
        s = slice(c * LANES, (c + 1) * LANES)
        edges = []
        for edge in (0, rows - 1):
            m = jnp.where(ocean, mask_ref[edge : edge + 1, s].astype(jnp.float32), 1.0)
            forced = m * f_ref[c, pl.ds(edge, FLUX, stride=rows), :]
            still = jnp.zeros((levels - FLUX, LANES), jnp.float32)
            edges.append(jnp.concatenate([forced, still], axis=0))
        for n, (ref, forced) in enumerate(
            ((e1_ref, jnp.where(even, edges[1], edges[0])), (e2_ref, jnp.where(even, edges[0], edges[1])))
        ):
            at = base + n * size + c * levels
            ref[c * levels : (c + 1) * levels, :] = pack_ref[at : at + levels, :] + forced


def stencil(xs, kappa_ref, rows):
    left, right = shifted(xs, True), shifted(xs, False)
    row = lax.broadcasted_iota(jnp.int32, (rows, LANES), 0)
    out = []
    for c, x in enumerate(xs):
        up = jnp.where(row == 0, 0.0, pltpu.roll(x, 1, 0))
        down = jnp.where(row == rows - 1, 0.0, pltpu.roll(x, rows - 1, 0))
        k = kappa_ref[:, c * LANES : (c + 1) * LANES]
        out.append(k * (up + down + left[c] + right[c] - 4.0 * x))
    return out


def still_kernel(rows, x0_ref, kappa_ref, mask_ref, table_ref, x_ref, x1_ref):
    per = x0_ref.shape[0]
    levels = x0_ref.shape[1] // rows
    ocean = lax.axis_index("comp") == 0

    def advance(src, dst):
        for l in range(levels):
            part = slice(l * rows, (l + 1) * rows)
            xs = [src[c, part, :] for c in range(per)]
            moved = stencil(xs, kappa_ref, rows)
            for c in range(per):
                acc = xs[c] + moved[c]
                for q in range(levels):
                    v = table_ref[l * levels + q : l * levels + q + 1, :]
                    acc = acc + v * src[c, q * rows : (q + 1) * rows, :]
                s = slice(c * LANES, (c + 1) * LANES)
                mask = jnp.where(ocean, mask_ref[:, s].astype(jnp.float32), 1.0)
                dst[c, part, :] = mask * acc

    advance(x0_ref, x1_ref)
    advance(x1_ref, x_ref)


def forced_kernel(rows, still_ref, f_ref, kappa_ref, mask_ref, table_ref, x_ref, f1_ref):
    per = still_ref.shape[0]
    levels = still_ref.shape[1] // rows
    ocean = lax.axis_index("comp") == 0

    def mask(c):
        m = mask_ref[:, c * LANES : (c + 1) * LANES].astype(jnp.float32)
        return jnp.where(ocean, m, 1.0)

    for c in range(per):
        m = mask(c)
        for f in range(FLUX):
            part = slice(f * rows, (f + 1) * rows)
            f1_ref[c, part, :] = m * f_ref[c, part, :]
    for l in range(levels):
        part = slice(l * rows, (l + 1) * rows)
        if l < FLUX:
            fs = [f1_ref[c, part, :] for c in range(per)]
            moved = stencil(fs, kappa_ref, rows)
        for c in range(per):
            acc = fs[c] + moved[c] + f_ref[c, part, :] if l < FLUX else 0.0
            for q in range(FLUX):
                v = table_ref[l * levels + q : l * levels + q + 1, :]
                acc = acc + v * f1_ref[c, q * rows : (q + 1) * rows, :]
            x_ref[c, part, :] = still_ref[c, part, :] + mask(c) * acc


def step_kernel(
    rows, most_ref, x0_ref, h1_ref, h2_ref, kappa_ref, mask_ref, vmix_ref,
    basis_ref, gram_ref, x_ref, sums_ref,
):
    per = x_ref.shape[0]
    levels = x_ref.shape[1] // rows
    vecs = basis_ref.shape[0]
    ocean = lax.axis_index("comp") == 0
    even = lax.rem(lax.axis_index("tile"), 2) == 0

    def mask(c, part):
        m = mask_ref[part, c * LANES : (c + 1) * LANES].astype(jnp.float32)
        return jnp.where(ocean, m, 1.0)

    vmix = vmix_ref[...]
    for side, edge, inner in ((0, 0, 1), (1, rows - 1, rows - 2)):
        flag = even if side == 1 else jnp.logical_not(even)

        def take(lo, n):
            return jnp.where(flag, h1_ref[lo : lo + n, :], h2_ref[lo : lo + n, :])

        def factor(c, r):
            r = slice(r, r + 1)
            return mask(c, r), mask(c, r) * kappa_ref[r, c * LANES : (c + 1) * LANES]

        ds = [factor(c, edge)[1] * take((per + c) * levels, levels) for c in range(per)]
        left, right = shifted(ds, True), shifted(ds, False)
        for c in range(per):
            d = ds[c]
            own = x0_ref[c, pl.ds(edge, levels, stride=rows), :]
            foreign = take(c * levels, levels) + take(2 * per * levels + c, 1) * own
            m, mk = factor(c, edge)
            mixed = d
            for q in range(levels):
                mixed = mixed + vmix[:, q : q + 1] * d[q : q + 1, :]
            at = pl.ds(edge, levels, stride=rows)
            change = m * mixed + mk * (left[c] + right[c] - 4.0 * d + foreign)
            x_ref[c, at, :] = x_ref[c, at, :] + change
            at = pl.ds(inner, levels, stride=rows)
            x_ref[c, at, :] = x_ref[c, at, :] + factor(c, inner)[1] * d

    def level(l, accs):
        accs = list(accs)
        for c in range(per):
            s = slice(c * LANES, (c + 1) * LANES)
            x = x_ref[c, pl.ds(l * rows, rows), :]
            for i in range(vecs):
                t = x * basis_ref[i, l, :, s].astype(jnp.float32)
                accs[i] = accs[i] + t.reshape(rows // 8, 8, LANES).sum(0)
            accs[vecs] = accs[vecs] + (x * x).reshape(rows // 8, 8, LANES).sum(0)
        return tuple(accs)

    zero = jnp.zeros((8, LANES), jnp.float32)
    accs = lax.fori_loop(0, levels, level, (zero,) * (vecs + 1))
    lane = lax.broadcasted_iota(jnp.int32, (1, LANES), 1)
    line = jnp.zeros((1, LANES), jnp.float32)
    for i in range(vecs + 1):
        tot = jnp.sum(jnp.sum(accs[i], axis=0, keepdims=True), axis=1, keepdims=True)
        line = line + jnp.where(lane == 64 + i, tot, 0.0)
    block = gram_ref[...] + jnp.concatenate([jnp.zeros((1, LANES), jnp.float32), line], axis=0)
    for d in range(sums_ref.shape[0]):
        sums_ref[d] = block


def finish_kernel(
    rows, total, x_ref, basis_ref, sums_ref, out_hbm, coef_hbm, out_ref, coef_ref, sems
):
    per = x_ref.shape[0]
    levels = x_ref.shape[1] // rows
    vecs = basis_ref.shape[0]
    sums = jnp.sum(sums_ref[...], axis=0)
    lane = lax.broadcasted_iota(jnp.int32, (1, LANES), 1)
    tail = pltpu.roll(sums[1:2, :], 64, 1)
    coef = jnp.where(lane < vecs, tail, 0.0) / total
    coef_ref[...] = coef[:, :vecs]
    copies = [pltpu.make_async_copy(coef_ref, coef_hbm, sems.at[PUTS])]
    copies[0].start()
    square = jnp.sum(jnp.where(lane == vecs, tail, 0.0), axis=1, keepdims=True)
    splat = [jnp.sum(jnp.where(lane == i, coef, 0.0), axis=1, keepdims=True) for i in range(vecs)]
    quad = jnp.zeros((1, LANES), jnp.float32)
    for i in range(vecs):
        shift = (LANES - 16 * (i % 8)) % LANES
        line = sums[i // 8 : i // 8 + 1, :]
        line = pltpu.roll(line, shift, 1) if shift else line
        quad = quad + splat[i] * jnp.where(lane < vecs, line, 0.0)
    extra = jnp.sum(coef * (quad - 2.0 * total * coef), axis=1, keepdims=True)
    scale = 1.0 / jnp.sqrt((square + extra) / total + 1e-06)
    wide = [jnp.broadcast_to(scale * s, (8, LANES)) for s in splat]
    scale = jnp.broadcast_to(scale, (8, LANES))

    def level(l, carry):
        for c in range(per):
            s = slice(c * LANES, (c + 1) * LANES)
            x = x_ref[c, pl.ds(l * rows, rows), :].reshape(rows // 8, 8, LANES) * scale
            for i in range(vecs):
                b = basis_ref[i, l, :, s].astype(jnp.float32).reshape(rows // 8, 8, LANES)
                x = x - wide[i] * b
            out_ref[pl.ds(l * rows, rows), s] = x.reshape(rows, LANES)
        return carry

    span = levels // PUTS
    for p in range(PUTS):
        lax.fori_loop(p * span, (p + 1) * span, level, 0)
        part = slice(p * span * rows, (p + 1) * span * rows)
        copy = pltpu.make_async_copy(out_ref.at[part, :], out_hbm.at[part, :], sems.at[p])
        copy.start()
        copies.append(copy)
    for copy in copies:
        copy.wait()


def body(state, basis, kappa, vmix, land_mask, send_rows, recv_slots, recv_weights):
    _, levels, rows, cols = state.shape
    vecs = basis.shape[0]
    bands, cap = send_rows.shape[2:]
    blocks, _ = recv_slots.shape[2:]
    per = cols // LANES
    comps = lax.axis_size("comp")
    devices = comps * bands
    total = float(levels * rows * cols * devices)
    f32 = jnp.float32
    flat = state.reshape(levels * rows, cols)
    vectors = basis[:, 0]
    kap, vm = kappa[0], vmix[0]

    field = jax.ShapeDtypeStruct((per, levels * rows, LANES), f32)
    import_field = jax.ShapeDtypeStruct((per, FLUX * rows, LANES), f32)
    pay = jax.ShapeDtypeStruct((payload_rows(levels, per), LANES), f32)
    pairs1 = [(i, i ^ 1) for i in range(bands)]
    pairs2 = [p for i in range(1, bands - 1, 2) for p in ((i, i + 1), (i + 1, i))]
    swap = [(i, i ^ 1) for i in range(comps)]

    def crossed(pairs):
        return [((c * bands) + i, (c ^ 1) * bands + k) for c in range(comps) for i, k in pairs]

    sides = (kap, land_mask, recv_slots[0, 0].T, recv_weights[0, 0].T, vm)
    lead = bands * 7 // 16
    group = [lead] + [n for n in reversed(range(bands)) if n != lead]
    bucket, columns, kap, land_mask, slots, weights, vm = call(
        functools.partial(gather_kernel, rows, group),
        (jax.ShapeDtypeStruct((bands * FLUX * cap, LANES), f32), field)
        + tuple(jax.ShapeDtypeStruct(a.shape, a.dtype) for a in sides),
        [HBM] * (2 + len(sides)),
        (HBM,) + (VMEM,) * (1 + len(sides)),
        scratch=(
            pltpu.SMEM((cap, bands), jnp.int32),
            pltpu.VMEM((bands * FLUX * cap, LANES), f32),
            pltpu.SemaphoreType.DMA((2 * per + 1 + len(sides) + OUTPARTS,)),
        ),
    )(*[in_hbm(a) for a in (send_rows[0, 0].T, flat) + sides])
    moved = lax.all_to_all(
        bucket.reshape(bands, FLUX * cap, LANES), "tile", 0, 0, axis_index_groups=[group]
    )
    pack, table = call(
        functools.partial(early_kernel, rows, group),
        (
            jax.ShapeDtypeStruct((bands * cap // LANES * blocks + 2 * pay.shape[0], LANES), f32),
            jax.ShapeDtypeStruct((levels * levels, LANES), f32),
        ),
        [VMEM] * 6,
        (VMEM,) * 2,
    )(slots, weights, columns, kap, land_mask, vm)
    pack = lax.ppermute(pack, "comp", swap)
    gram = call(
        gram_kernel,
        jax.ShapeDtypeStruct((2, LANES), f32),
        [HBM],
        VMEM,
        scratch=(
            pltpu.VMEM(vectors.shape, vectors.dtype),
            pltpu.SemaphoreType.DMA((levels,)),
        ),
    )(in_hbm(vectors))
    still = call(
        functools.partial(still_kernel, rows),
        field,
        [VMEM] * 4,
        VMEM,
        scratch=(pltpu.VMEM((per, levels * rows, LANES), f32),),
    )(columns, kap, land_mask, table)

    foreign, edge1, edge2 = call(
        functools.partial(regrid_kernel, rows, levels),
        (import_field, pay, pay),
        [VMEM] * 3,
        (VMEM,) * 3,
    )(moved, pack, land_mask)
    vectors = call(
        fetch_kernel,
        jax.ShapeDtypeStruct(vectors.shape, vectors.dtype),
        [pl.BlockSpec(memory_space=pl.ANY), HBM],
        VMEM,
        scratch=(pltpu.SemaphoreType.DMA((vecs,)),),
    )(edge1, in_hbm(vectors))
    imported = lax.ppermute(foreign, "comp", swap)
    edge1 = lax.ppermute(edge1, ("comp", "tile"), crossed(pairs1))
    edge2 = lax.ppermute(edge2, ("comp", "tile"), crossed(pairs2))
    most = call(
        functools.partial(forced_kernel, rows),
        field,
        [VMEM] * 5,
        VMEM,
        scratch=(pltpu.VMEM((per, FLUX * rows, LANES), f32),),
    )(still, imported, kap, land_mask, table)
    x, sums = call(
        functools.partial(step_kernel, rows),
        (field, jax.ShapeDtypeStruct((devices, 2, LANES), f32)),
        [VMEM] * 9,
        (VMEM, VMEM),
        aliases={0: 0},
    )(most, columns, edge1, edge2, kap, land_mask, vm, vectors, gram)
    sums = lax.all_to_all(sums, ("comp", "tile"), 0, 0)
    direction, coefs = call(
        functools.partial(finish_kernel, rows, total),
        (
            jax.ShapeDtypeStruct((levels * rows, cols), f32),
            jax.ShapeDtypeStruct((1, vecs), f32),
        ),
        [VMEM] * 3,
        (HBM, HBM),
        scratch=(
            pltpu.VMEM((levels * rows, cols), f32),
            pltpu.VMEM((1, vecs), f32),
            pltpu.SemaphoreType.DMA((PUTS + 1,)),
        ),
    )(x, vectors, sums)
    return direction.reshape(1, levels, rows, cols), coefs.reshape(vecs)


def solution(mesh):
    return jax.shard_map(
        body,
        mesh=mesh,
        in_specs=(
            P("comp", None, "tile", None),
            P(None, "comp", None, "tile", None),
            P("comp", "tile", None),
            P("comp", None, None),
            P("tile", None),
            P("comp", "tile", None, None),
            P("comp", "tile", None, None),
            P("comp", "tile", None, None),
        ),
        out_specs=(P("comp", None, "tile", None), P()),
        check_vma=False,
    )
```

```python
import functools

import jax
import jax.numpy as jnp
from jax import lax
from jax.experimental import pallas as pl
from jax.experimental.pallas import tpu as pltpu
from jax.sharding import PartitionSpec as P


FLUX = 4
LANES = 128
HBM = pl.BlockSpec(memory_space=pltpu.HBM)
VMEM = pl.BlockSpec(memory_space=pltpu.VMEM)
LIMIT = 24 << 20
PUTS = 4
OUTPARTS = 4


def call(kernel, outs, in_specs, out_specs, scratch=(), aliases={}):
    return pl.pallas_call(
        kernel,
        out_shape=outs,
        in_specs=in_specs,
        out_specs=out_specs,
        scratch_shapes=list(scratch),
        input_output_aliases=aliases,
        compiler_params=pltpu.CompilerParams(vmem_limit_bytes=LIMIT),
    )


def in_hbm(a):
    return pltpu.with_memory_space_constraint(a, pltpu.HBM)


def split(a):
    high = a.astype(jnp.bfloat16)
    return high, (a - high.astype(jnp.float32)).astype(jnp.bfloat16)


def payload_rows(levels, per):
    return 2 * levels * per + per


def block_place(b, per):
    if per & (per - 1) == 0:
        bits = per.bit_length() - 1
        return lax.shift_right_logical(b, bits), lax.bitwise_and(b, per - 1)
    return lax.div(b, per), lax.rem(b, per)


def gather_kernel(rows, group, index_ref, state_ref, *refs):
    small = (len(refs) - 5) // 2
    sides, out_hbm, x_ref = refs[:small], refs[small], refs[small + 1]
    side_outs, (rows_ref, out_ref, sems) = refs[small + 2 : 2 * small + 2], refs[2 * small + 2 :]
    cap, bands = rows_ref.shape
    per = x_ref.shape[0]
    top = FLUX * rows
    index = pltpu.make_async_copy(index_ref, rows_ref, sems.at[2 * per])
    index.start()
    copies = []
    for part, (lo, hi) in enumerate(((0, top), (top, x_ref.shape[1]))):
        for c in range(per):
            copies.append(
                pltpu.make_async_copy(
                    state_ref.at[lo:hi, c * LANES : (c + 1) * LANES],
                    x_ref.at[c, lo:hi, :],
                    sems.at[part * per + c],
                )
            )
    for k, (src, dst) in enumerate(zip(sides, side_outs)):
        copies.append(pltpu.make_async_copy(src, dst, sems.at[2 * per + 1 + k]))
    for copy in copies:
        copy.start()
    index.wait()
    for copy in copies[:per]:
        copy.wait()

    def band(n):
        for j in range(cap):
            r, c = block_place(rows_ref[j, group[n]], per)
            piece = x_ref[c, pl.ds(r, FLUX, stride=rows), :]
            out_ref[pl.ds(n * (cap * FLUX) + j, FLUX, stride=cap), :] = piece

    span = bands // OUTPARTS
    size = span * cap * FLUX
    for p in range(OUTPARTS):
        for n in range(p * span, (p + 1) * span):
            band(n)
        part = slice(p * size, (p + 1) * size)
        copy = pltpu.make_async_copy(
            out_ref.at[part, :], out_hbm.at[part, :], sems.at[2 * per + 1 + small + p]
        )
        copy.start()
        copies.append(copy)
    for copy in copies[per:]:
        copy.wait()


def fetch_kernel(after_ref, basis_hbm, basis_ref, sems):
    copies = [
        pltpu.make_async_copy(basis_hbm.at[i], basis_ref.at[i], sems.at[i])
        for i in range(basis_ref.shape[0])
    ]
    for copy in copies:
        copy.start()
    for copy in copies:
        copy.wait()


def gram_kernel(basis_hbm, gram_ref, basis_ref, sems):
    vecs, levels, rows, cols = basis_ref.shape
    copies = [
        pltpu.make_async_copy(basis_hbm.at[:, l], basis_ref.at[:, l], sems.at[l])
        for l in range(levels)
    ]
    for copy in copies:
        copy.start()
    n = vecs * rows
    total = jnp.zeros((n, n), jnp.float32)
    for l in range(levels):
        copies[l].wait()
        a = basis_ref[:, l].reshape(n, cols)
        total = total + lax.dot_general(
            a, a, (((1,), (1,)), ((), ())), preferred_element_type=jnp.float32
        )
    i0 = lax.broadcasted_iota(jnp.int32, (n, n), 0)
    i1 = lax.broadcasted_iota(jnp.int32, (n, n), 1)
    total = jnp.where(lax.rem(i0, rows) == lax.rem(i1, rows), total, 0.0)
    part = jnp.sum(total.reshape(vecs, rows, n), axis=1)
    j0 = lax.broadcasted_iota(jnp.int32, (n, LANES), 0)
    j1 = lax.broadcasted_iota(jnp.int32, (n, LANES), 1)
    fold = jnp.where(lax.div(j0, rows) == j1, 1.0, 0.0)
    gram = jnp.dot(part, fold, precision=lax.Precision.HIGHEST)
    packed = [jnp.zeros((1, LANES), jnp.float32), jnp.zeros((1, LANES), jnp.float32)]
    for i in range(vecs):
        shift = 16 * (i % 8)
        line = gram[i : i + 1, :]
        packed[i // 8] = packed[i // 8] + (pltpu.roll(line, shift, 1) if shift else line)
    gram_ref[...] = jnp.concatenate(packed, axis=0)


def shifted(parts, up):
    n = len(parts)
    lane = lax.broadcasted_iota(jnp.int32, parts[0].shape, 1)
    rolled = [pltpu.roll(p, 1 if up else LANES - 1, 1) for p in parts]
    edge = 0 if up else LANES - 1
    step = -1 if up else 1
    return [jnp.where(lane == edge, rolled[(c + step) % n], rolled[c]) for c in range(n)]


def early_kernel(
    rows, group, slots_ref, weights_ref, x_ref, kappa_ref, mask_ref, vmix_ref,
    pack_ref, table_ref,
):
    over, blocks = slots_ref.shape
    per = x_ref.shape[0]
    levels = x_ref.shape[1] // rows
    size = payload_rows(levels, per)
    slots = (pack_ref.shape[0] - 2 * size) // blocks * LANES
    cap = slots // len(group)
    row = lax.broadcasted_iota(jnp.int32, (cap, blocks), 0)
    mat = []
    for d in group:
        part = jnp.zeros((cap, blocks), jnp.float32)
        for k in range(over):
            hit = slots_ref[k : k + 1, :] == row + d * cap
            part = part + jnp.where(hit, weights_ref[k : k + 1, :], 0.0)
        mat.append(part)
    mat = jnp.concatenate(mat, axis=0)
    b0 = lax.broadcasted_iota(jnp.int32, (blocks, blocks), 0)
    b1 = lax.broadcasted_iota(jnp.int32, (blocks, blocks), 1)
    order = jnp.where(lax.rem(b0, rows) * per + lax.div(b0, rows) == b1, 1.0, 0.0)
    mat = jnp.dot(order, mat.T, precision=lax.Precision.HIGHEST)
    for p in range(slots // LANES):
        pack_ref[p * blocks : (p + 1) * blocks, :] = mat[:, p * LANES : (p + 1) * LANES]

    ocean = lax.axis_index("comp") == 0
    even = lax.rem(lax.axis_index("tile"), 2) == 0
    vmix = vmix_ref[...]
    d0 = lax.broadcasted_iota(jnp.int32, (levels, levels), 0)
    d1 = lax.broadcasted_iota(jnp.int32, (levels, levels), 1)
    for l in range(levels):
        column = jnp.sum(jnp.where(d0 == d1, vmix[l : l + 1, :], 0.0), axis=1, keepdims=True)
        table_ref[l * levels : (l + 1) * levels, :] = jnp.broadcast_to(column, (levels, LANES))
    pays = []
    for edge, inner in ((0, 1), (rows - 1, rows - 2)):
        xs = [x_ref[c, pl.ds(edge, levels, stride=rows), :] for c in range(per)]
        left, right = shifted(xs, True), shifted(xs, False)
        pay = []
        for c in range(per):
            s = slice(c * LANES, (c + 1) * LANES)
            x = xs[c]
            xi = x_ref[c, pl.ds(inner, levels, stride=rows), :]
            k = kappa_ref[edge : edge + 1, s]
            m = jnp.where(ocean, mask_ref[edge : edge + 1, s].astype(jnp.float32), 1.0)
            acc = x + k * (xi + left[c] + right[c] - 4.0 * x)
            for q in range(levels):
                acc = acc + vmix[:, q : q + 1] * x[q : q + 1, :]
            pay.append((m * acc, x, m * k))
        pays.append(pay)
    base = slots // LANES * blocks
    for n, flag in ((0, even), (1, jnp.logical_not(even))):
        ref = pack_ref.at[base + n * size : base + (n + 1) * size, :]
        for c in range(per):
            a, x, b = [jnp.where(flag, v, u) for u, v in zip(pays[0][c], pays[1][c])]
            ref[c * levels : (c + 1) * levels, :] = a
            ref[(per + c) * levels : (per + c + 1) * levels, :] = x
            ref[2 * per * levels + c : 2 * per * levels + c + 1, :] = b


def regrid_kernel(rows, levels, buf_ref, pack_ref, mask_ref, f_ref, e1_ref, e2_ref):
    per = f_ref.shape[0]
    cap = buf_ref.shape[1] // FLUX
    slots = buf_ref.shape[0] * cap
    blocks = rows * per
    size = payload_rows(levels, per)
    wide = jnp.concatenate(
        [buf_ref[:, f * cap : (f + 1) * cap, :].reshape(slots, LANES) for f in range(FLUX)], axis=1
    )
    bh, bl = split(wide)
    pieces = [pack_ref[p * blocks : (p + 1) * blocks, :] for p in range(slots // LANES)]
    wh, wl = split(jnp.concatenate(pieces, axis=1))
    dot = functools.partial(jnp.dot, preferred_element_type=jnp.float32)
    out = dot(wh, bh) + (dot(wh, bl) + dot(wl, bh))
    for f in range(FLUX):
        for c in range(per):
            f_ref[c, f * rows : (f + 1) * rows, :] = out[
                c * rows : (c + 1) * rows, f * LANES : (f + 1) * LANES
            ]
    ocean = lax.axis_index("comp") != 0
    even = lax.rem(lax.axis_index("tile"), 2) == 0
    base = slots // LANES * blocks
    for n, ref in enumerate((e1_ref, e2_ref)):
        ref[per * levels :, :] = pack_ref[base + n * size + per * levels : base + (n + 1) * size, :]
    for c in range(per):
        s = slice(c * LANES, (c + 1) * LANES)
        edges = []
        for edge in (0, rows - 1):
            m = jnp.where(ocean, mask_ref[edge : edge + 1, s].astype(jnp.float32), 1.0)
            forced = m * f_ref[c, pl.ds(edge, FLUX, stride=rows), :]
            still = jnp.zeros((levels - FLUX, LANES), jnp.float32)
            edges.append(jnp.concatenate([forced, still], axis=0))
        for n, (ref, forced) in enumerate(
            ((e1_ref, jnp.where(even, edges[1], edges[0])), (e2_ref, jnp.where(even, edges[0], edges[1])))
        ):
            at = base + n * size + c * levels
            ref[c * levels : (c + 1) * levels, :] = pack_ref[at : at + levels, :] + forced


def stencil(xs, kappa_ref, rows):
    left, right = shifted(xs, True), shifted(xs, False)
    row = lax.broadcasted_iota(jnp.int32, (rows, LANES), 0)
    out = []
    for c, x in enumerate(xs):
        up = jnp.where(row == 0, 0.0, pltpu.roll(x, 1, 0))
        down = jnp.where(row == rows - 1, 0.0, pltpu.roll(x, rows - 1, 0))
        k = kappa_ref[:, c * LANES : (c + 1) * LANES]
        out.append(k * (up + down + left[c] + right[c] - 4.0 * x))
    return out


def still_kernel(rows, x0_ref, kappa_ref, mask_ref, table_ref, x_ref, x1_ref):
    per = x0_ref.shape[0]
    levels = x0_ref.shape[1] // rows
    ocean = lax.axis_index("comp") == 0

    def advance(src, dst):
        for l in range(levels):
            part = slice(l * rows, (l + 1) * rows)
            xs = [src[c, part, :] for c in range(per)]
            moved = stencil(xs, kappa_ref, rows)
            for c in range(per):
                acc = xs[c] + moved[c]
                for q in range(levels):
                    v = table_ref[l * levels + q : l * levels + q + 1, :]
                    acc = acc + v * src[c, q * rows : (q + 1) * rows, :]
                s = slice(c * LANES, (c + 1) * LANES)
                mask = jnp.where(ocean, mask_ref[:, s].astype(jnp.float32), 1.0)
                dst[c, part, :] = mask * acc

    advance(x0_ref, x1_ref)
    advance(x1_ref, x_ref)


def forced_kernel(rows, still_ref, f_ref, kappa_ref, mask_ref, table_ref, x_ref, f1_ref):
    per = still_ref.shape[0]
    levels = still_ref.shape[1] // rows
    ocean = lax.axis_index("comp") == 0

    def mask(c):
        m = mask_ref[:, c * LANES : (c + 1) * LANES].astype(jnp.float32)
        return jnp.where(ocean, m, 1.0)

    for c in range(per):
        m = mask(c)
        for f in range(FLUX):
            part = slice(f * rows, (f + 1) * rows)
            f1_ref[c, part, :] = m * f_ref[c, part, :]
    for l in range(levels):
        part = slice(l * rows, (l + 1) * rows)
        if l < FLUX:
            fs = [f1_ref[c, part, :] for c in range(per)]
            moved = stencil(fs, kappa_ref, rows)
        for c in range(per):
            acc = fs[c] + moved[c] + f_ref[c, part, :] if l < FLUX else 0.0
            for q in range(FLUX):
                v = table_ref[l * levels + q : l * levels + q + 1, :]
                acc = acc + v * f1_ref[c, q * rows : (q + 1) * rows, :]
            x_ref[c, part, :] = still_ref[c, part, :] + mask(c) * acc


def step_kernel(
    rows, most_ref, x0_ref, h1_ref, h2_ref, kappa_ref, mask_ref, vmix_ref,
    basis_ref, gram_ref, x_ref, sums_ref,
):
    per = x_ref.shape[0]
    levels = x_ref.shape[1] // rows
    vecs = basis_ref.shape[0]
    ocean = lax.axis_index("comp") == 0
    even = lax.rem(lax.axis_index("tile"), 2) == 0

    def mask(c, part):
        m = mask_ref[part, c * LANES : (c + 1) * LANES].astype(jnp.float32)
        return jnp.where(ocean, m, 1.0)

    vmix = vmix_ref[...]
    for side, edge, inner in ((0, 0, 1), (1, rows - 1, rows - 2)):
        flag = even if side == 1 else jnp.logical_not(even)

        def take(lo, n):
            return jnp.where(flag, h1_ref[lo : lo + n, :], h2_ref[lo : lo + n, :])

        def factor(c, r):
            r = slice(r, r + 1)
            return mask(c, r), mask(c, r) * kappa_ref[r, c * LANES : (c + 1) * LANES]

        ds = [factor(c, edge)[1] * take((per + c) * levels, levels) for c in range(per)]
        left, right = shifted(ds, True), shifted(ds, False)
        for c in range(per):
            d = ds[c]
            own = x0_ref[c, pl.ds(edge, levels, stride=rows), :]
            foreign = take(c * levels, levels) + take(2 * per * levels + c, 1) * own
            m, mk = factor(c, edge)
            mixed = d
            for q in range(levels):
                mixed = mixed + vmix[:, q : q + 1] * d[q : q + 1, :]
            at = pl.ds(edge, levels, stride=rows)
            change = m * mixed + mk * (left[c] + right[c] - 4.0 * d + foreign)
            x_ref[c, at, :] = x_ref[c, at, :] + change
            at = pl.ds(inner, levels, stride=rows)
            x_ref[c, at, :] = x_ref[c, at, :] + factor(c, inner)[1] * d

    def level(l, accs):
        accs = list(accs)
        for c in range(per):
            s = slice(c * LANES, (c + 1) * LANES)
            x = x_ref[c, pl.ds(l * rows, rows), :]
            for i in range(vecs):
                t = x * basis_ref[i, l, :, s].astype(jnp.float32)
                accs[i] = accs[i] + t.reshape(rows // 8, 8, LANES).sum(0)
            accs[vecs] = accs[vecs] + (x * x).reshape(rows // 8, 8, LANES).sum(0)
        return tuple(accs)

    zero = jnp.zeros((8, LANES), jnp.float32)
    accs = (zero,) * (vecs + 1)
    for l in range(levels):
        accs = level(l, accs)
    lane = lax.broadcasted_iota(jnp.int32, (1, LANES), 1)
    line = jnp.zeros((1, LANES), jnp.float32)
    for i in range(vecs + 1):
        tot = jnp.sum(jnp.sum(accs[i], axis=0, keepdims=True), axis=1, keepdims=True)
        line = line + jnp.where(lane == 64 + i, tot, 0.0)
    block = gram_ref[...] + jnp.concatenate([jnp.zeros((1, LANES), jnp.float32), line], axis=0)
    for d in range(sums_ref.shape[0]):
        sums_ref[d] = block


def finish_kernel(
    rows, total, x_ref, basis_ref, sums_ref, out_hbm, coef_hbm, out_ref, coef_ref, sems
):
    per = x_ref.shape[0]
    levels = x_ref.shape[1] // rows
    vecs = basis_ref.shape[0]
    sums = jnp.sum(sums_ref[...], axis=0)
    lane = lax.broadcasted_iota(jnp.int32, (1, LANES), 1)
    tail = pltpu.roll(sums[1:2, :], 64, 1)
    coef = jnp.where(lane < vecs, tail, 0.0) / total
    coef_ref[...] = coef[:, :vecs]
    copies = [pltpu.make_async_copy(coef_ref, coef_hbm, sems.at[PUTS])]
    copies[0].start()
    square = jnp.sum(jnp.where(lane == vecs, tail, 0.0), axis=1, keepdims=True)
    splat = [jnp.sum(jnp.where(lane == i, coef, 0.0), axis=1, keepdims=True) for i in range(vecs)]
    quad = jnp.zeros((1, LANES), jnp.float32)
    for i in range(vecs):
        shift = (LANES - 16 * (i % 8)) % LANES
        line = sums[i // 8 : i // 8 + 1, :]
        line = pltpu.roll(line, shift, 1) if shift else line
        quad = quad + splat[i] * jnp.where(lane < vecs, line, 0.0)
    extra = jnp.sum(coef * (quad - 2.0 * total * coef), axis=1, keepdims=True)
    scale = 1.0 / jnp.sqrt((square + extra) / total + 1e-06)
    wide = [jnp.broadcast_to(s, (8, LANES)) for s in splat]
    scale = jnp.broadcast_to(scale, (8, LANES))

    def level(l, carry):
        for c in range(per):
            s = slice(c * LANES, (c + 1) * LANES)
            x = x_ref[c, pl.ds(l * rows, rows), :].reshape(rows // 8, 8, LANES)
            for i in range(vecs):
                b = basis_ref[i, l, :, s].astype(jnp.float32).reshape(rows // 8, 8, LANES)
                x = x - wide[i] * b
            out_ref[pl.ds(l * rows, rows), s] = (x * scale).reshape(rows, LANES)
        return carry

    span = levels // PUTS
    for p in range(PUTS):
        for l in range(p * span, (p + 1) * span):
            level(l, 0)
        part = slice(p * span * rows, (p + 1) * span * rows)
        copy = pltpu.make_async_copy(out_ref.at[part, :], out_hbm.at[part, :], sems.at[p])
        copy.start()
        copies.append(copy)
    for copy in copies:
        copy.wait()


def body(state, basis, kappa, vmix, land_mask, send_rows, recv_slots, recv_weights):
    _, levels, rows, cols = state.shape
    vecs = basis.shape[0]
    bands, cap = send_rows.shape[2:]
    blocks, _ = recv_slots.shape[2:]
    per = cols // LANES
    comps = lax.axis_size("comp")
    devices = comps * bands
    total = float(levels * rows * cols * devices)
    f32 = jnp.float32
    flat = state.reshape(levels * rows, cols)
    vectors = basis[:, 0]
    kap, vm = kappa[0], vmix[0]

    field = jax.ShapeDtypeStruct((per, levels * rows, LANES), f32)
    import_field = jax.ShapeDtypeStruct((per, FLUX * rows, LANES), f32)
    pay = jax.ShapeDtypeStruct((payload_rows(levels, per), LANES), f32)
    pairs1 = [(i, i ^ 1) for i in range(bands)]
    pairs2 = [p for i in range(1, bands - 1, 2) for p in ((i, i + 1), (i + 1, i))]
    swap = [(i, i ^ 1) for i in range(comps)]

    def crossed(pairs):
        return [((c * bands) + i, (c ^ 1) * bands + k) for c in range(comps) for i, k in pairs]

    sides = (kap, land_mask, recv_slots[0, 0].T, recv_weights[0, 0].T, vm)
    lead = bands * 7 // 16
    group = [lead] + [n for n in reversed(range(bands)) if n != lead]
    bucket, columns, kap, land_mask, slots, weights, vm = call(
        functools.partial(gather_kernel, rows, group),
        (jax.ShapeDtypeStruct((bands * FLUX * cap, LANES), f32), field)
        + tuple(jax.ShapeDtypeStruct(a.shape, a.dtype) for a in sides),
        [HBM] * (2 + len(sides)),
        (HBM,) + (VMEM,) * (1 + len(sides)),
        scratch=(
            pltpu.SMEM((cap, bands), jnp.int32),
            pltpu.VMEM((bands * FLUX * cap, LANES), f32),
            pltpu.SemaphoreType.DMA((2 * per + 1 + len(sides) + OUTPARTS,)),
        ),
    )(*[in_hbm(a) for a in (send_rows[0, 0].T, flat) + sides])
    moved = lax.all_to_all(
        bucket.reshape(bands, FLUX * cap, LANES), "tile", 0, 0, axis_index_groups=[group]
    )
    pack, table = call(
        functools.partial(early_kernel, rows, group),
        (
            jax.ShapeDtypeStruct((bands * cap // LANES * blocks + 2 * pay.shape[0], LANES), f32),
            jax.ShapeDtypeStruct((levels * levels, LANES), f32),
        ),
        [VMEM] * 6,
        (VMEM,) * 2,
    )(slots, weights, columns, kap, land_mask, vm)
    pack = lax.ppermute(pack, "comp", swap)
    gram = call(
        gram_kernel,
        jax.ShapeDtypeStruct((2, LANES), f32),
        [HBM],
        VMEM,
        scratch=(
            pltpu.VMEM(vectors.shape, vectors.dtype),
            pltpu.SemaphoreType.DMA((levels,)),
        ),
    )(in_hbm(vectors))
    still = call(
        functools.partial(still_kernel, rows),
        field,
        [VMEM] * 4,
        VMEM,
        scratch=(pltpu.VMEM((per, levels * rows, LANES), f32),),
    )(columns, kap, land_mask, table)

    foreign, edge1, edge2 = call(
        functools.partial(regrid_kernel, rows, levels),
        (import_field, pay, pay),
        [VMEM] * 3,
        (VMEM,) * 3,
    )(moved, pack, land_mask)
    vectors = call(
        fetch_kernel,
        jax.ShapeDtypeStruct(vectors.shape, vectors.dtype),
        [pl.BlockSpec(memory_space=pl.ANY), HBM],
        VMEM,
        scratch=(pltpu.SemaphoreType.DMA((vecs,)),),
    )(edge1, in_hbm(vectors))
    imported = lax.ppermute(foreign, "comp", swap)
    edge1 = lax.ppermute(edge1, ("comp", "tile"), crossed(pairs1))
    edge2 = lax.ppermute(edge2, ("comp", "tile"), crossed(pairs2))
    most = call(
        functools.partial(forced_kernel, rows),
        field,
        [VMEM] * 5,
        VMEM,
        scratch=(pltpu.VMEM((per, FLUX * rows, LANES), f32),),
    )(still, imported, kap, land_mask, table)
    x, sums = call(
        functools.partial(step_kernel, rows),
        (field, jax.ShapeDtypeStruct((devices, 2, LANES), f32)),
        [VMEM] * 9,
        (VMEM, VMEM),
        aliases={0: 0},
    )(most, columns, edge1, edge2, kap, land_mask, vm, vectors, gram)
    sums = lax.all_to_all(sums, ("comp", "tile"), 0, 0)
    direction, coefs = call(
        functools.partial(finish_kernel, rows, total),
        (
            jax.ShapeDtypeStruct((levels * rows, cols), f32),
            jax.ShapeDtypeStruct((1, vecs), f32),
        ),
        [VMEM] * 3,
        (HBM, HBM),
        scratch=(
            pltpu.VMEM((levels * rows, cols), f32),
            pltpu.VMEM((1, vecs), f32),
            pltpu.SemaphoreType.DMA((PUTS + 1,)),
        ),
    )(x, vectors, sums)
    return direction.reshape(1, levels, rows, cols), coefs.reshape(vecs)


def solution(mesh):
    return jax.shard_map(
        body,
        mesh=mesh,
        in_specs=(
            P("comp", None, "tile", None),
            P(None, "comp", None, "tile", None),
            P("comp", "tile", None),
            P("comp", None, None),
            P("tile", None),
            P("comp", "tile", None, None),
            P("comp", "tile", None, None),
            P("comp", "tile", None, None),
        ),
        out_specs=(P("comp", None, "tile", None), P()),
        check_vma=False,
    )
```
